32 devices in a mesh: groups: 2 (over x), seq: 16 (over z, y, core).
Axes of the slice: x: 2, y: 2, z: 4, core: 2. Of those that a mesh axis runs over, the one named last changes fastest.
Arguments:
- x_true: float32 [3, 4096], P(None, ('groups', 'seq')), parts along dimension 1, may hold values from -96 to 96
- noise: float32 [8, 3, 2048], P('groups', None, 'seq'), parts along dimension 0, may hold values from -6 to 6
- noise_level: int32 [8], P('groups'), parts along dimension 0, may hold values from 0 to 199
- atom_single: bfloat16 [4096, 128], P(('groups', 'seq')), parts along dimension 0, may hold values from -6 to 6
- atom_token: int32 [4096], P(('groups', 'seq')), parts along dimension 0, may hold values from 0 to 255, as said below
- window_edges: int32 [128, 2], P(('groups', 'seq')), parts along dimension 0, may hold values from 0 to 2048, as said below
- atom_pair_bias: float32 [128, 4, 32, 128], P(('groups', 'seq')), parts along dimension 0, may hold values from -6 to 300
- token_single: float32 [512, 768], P(('groups', 'seq')), parts along dimension 0, may hold values from -6 to 6
- pair_bias: float32 [32, 256, 256], P('groups', 'seq'), parts along dimension 0, may hold values from -6 to 300
- w_coord: float32 [3, 128], replicated, may hold values from -3.5 to 3.5
- w_atom_qkv: bfloat16 [4, 128, 384], replicated, may hold values from -0.5 to 0.5
- w_atom_out: bfloat16 [4, 128, 128], replicated, may hold values from -0.5 to 0.5
- w_atom_up: bfloat16 [4, 128, 512], replicated, may hold values from -0.5 to 0.5
- w_atom_down: bfloat16 [4, 256, 128], replicated, may hold values from -0.375 to 0.375
- w_pool: bfloat16 [128, 768], replicated, may hold values from -0.5 to 0.5
- w_token_qkv: bfloat16 [768, 2304], replicated, may hold values from -0.21875 to 0.21875
- w_token_out: bfloat16 [768, 768], replicated, may hold values from -0.21875 to 0.21875
- w_back: bfloat16 [768, 128], replicated, may hold values from -0.21875 to 0.21875
- w_final: bfloat16 [3, 128], replicated, may hold values from -0.5 to 0.5
Outputs:
- denoised: float32 [8, 3, 2048], P('groups', None, 'seq'), parts along dimension 0
- token_state: float32 [8, 256, 768], P('groups', 'seq'), parts along dimension 0
The draws below stay inside these ranges and needn't reach their ends.
There are 2 independent parts, one for each index of `groups`. The reference program is written for one: setup_inputs(seed, part) draws one part's arguments, and reference() takes and returns one part's arrays. A program takes and returns all parts, laid end to end along the dimension named above; an argument that names none is the same for every part. Nothing has to cross between parts.
Inputs may be any that keep to these rules, and one draw needn't show every extreme that they name: `atom_token`: never falls along the atoms; every token has one or more atoms; the atoms of token t lie at or after atom 128 * (t // 16) - 48 and before atom 128 * (t // 16) + 128 + 128 * 3 // 8, so the atoms of shard d of the atoms name tokens of token shards d - 1, d and d + 1 only. For block b: max(0, 32 * b - 48) <= window_edges[b, 0] <= max(0, 32 * b - 48 + 48 // 3) and min(2048, 32 * b + 80 - 48 // 3) <= window_edges[b, 1] <= min(2048, 32 * b + 80).
All inputs are finite; a program needn't handle non-finite values.
Results may differ from the reference program's by a relative error of at most 0.008.
Values may be sent and summed in bfloat16 or wider, within the bound.
No kernel may reach another device: no remote copies, remote signals or barrier semaphores. Data moves between devices by JAX's collectives and lax.ppermute only.
A program may use at most 128 MiB of HBM per device.

```python
import jax
import jax.numpy as jnp
from jax import lax

ATOM_WIDTH = 128
ATOM_HEADS = 4
TOKEN_WIDTH = 768
HEADS = 16
QUERY_BLOCK = 32
KEY_WINDOW = 128
ENC_LAYERS = 2
LEVELS = 200
SAMPLES = 4
ATOM_DEV = 128
TOK_DEV = 16
ATOMS = 2048
TOKENS = 256
ATOM_BLOCKS = 64
RIM = 48
LAYERS = 4


def draw_atom_token(key, part):
    shard_count = ATOMS // ATOM_DEV
    reach_limit = ATOM_DEV * 3 // 8
    shift_key, weight_key = jax.random.split(jax.random.fold_in(key, 11))
    shifts = jax.random.randint(shift_key, (shard_count,), -reach_limit, reach_limit + 1)
    shifts = jnp.where(jnp.arange(shard_count) == shard_count - 1, 0, shifts)
    earlier = jnp.concatenate([jnp.zeros((1,), jnp.int32), shifts[:-1]])
    totals = ATOM_DEV + shifts - earlier
    weights = jax.random.randint(weight_key, (shard_count, TOK_DEV), 1, 9)
    spare_atoms = totals - TOK_DEV
    counts = 1 + weights * spare_atoms[:, None] // jnp.sum(weights, 1, keepdims=True)
    missing = totals - jnp.sum(counts, 1)
    counts = counts + jnp.where(jnp.arange(TOK_DEV) == TOK_DEV - 1, 1, 0)[None, :] * missing[:, None]
    flat_counts = counts.reshape(-1)
    starts = jnp.cumsum(flat_counts) - flat_counts
    return (jnp.searchsorted(starts, jnp.arange(ATOMS), side='right') - 1).astype(jnp.int32)


def draw_window_edges(key, part):
    lower_key, upper_key = jax.random.split(jax.random.fold_in(key, 23))
    block_start = QUERY_BLOCK * jnp.arange(ATOM_BLOCKS)
    lower = jnp.maximum(block_start - RIM + jax.random.randint(lower_key, (ATOM_BLOCKS,), 0, RIM // 3 + 1), 0)
    upper = jnp.minimum(block_start + QUERY_BLOCK + RIM - jax.random.randint(upper_key, (ATOM_BLOCKS,), 0, RIM // 3 + 1), ATOMS)
    return jnp.stack([lower, upper], 1).astype(jnp.int32)


def biased_rows(key, array_shape):
    base_key = jax.random.fold_in(key, 0)
    return jnp.clip(jax.random.normal(base_key, array_shape, jnp.float32), -6.0, 6.0)


def draw_atom_pair_bias(key, part):
    return biased_rows(jax.random.fold_in(key, 31), (ATOM_BLOCKS, ATOM_HEADS, QUERY_BLOCK, KEY_WINDOW))


def draw_pair_bias(key, part):
    return biased_rows(jax.random.fold_in(key, 37), (HEADS, TOKENS, TOKENS))


def plant(entries, rng, least, top_value):
    longest = entries.shape.index(max(entries.shape))
    spots = []
    for shift in (0, 1):
        where = [jax.random.randint(jax.random.fold_in(rng, axis), (), 0, length) for axis, length in enumerate(entries.shape)]
        where[longest] = (where[longest] + shift) % entries.shape[longest]
        spots.append(tuple(where))
    return entries.at[spots[0]].set(least).at[spots[1]].set(top_value)


def block_scale(rng, extent, pieces, least, top_value):
    gain, own = 1.0, jax.random.fold_in(rng, 6)
    for dim, shards_of in pieces:
        steps = jnp.exp(jax.random.uniform(jax.random.fold_in(own, dim), (shards_of,), jnp.float32, least / len(pieces), top_value / len(pieces)))
        gain = gain * jnp.repeat(steps, extent[dim] // shards_of).reshape([-1 if axis == dim else 1 for axis in range(len(extent))])
    return gain


def scatter_about(rng, extent, scale, most, cuts=(), dtype=jnp.bfloat16):
    array = scale * jax.random.normal(rng, extent, jnp.float32)
    if cuts:
        array = array * block_scale(rng, extent, cuts, -0.22, 0.18)
    return jnp.clip(array, -most, most).astype(dtype)


def setup_inputs(seed: int = 0, part: int = 0) -> dict:
    streams_of = jax.random.split(jax.random.key(seed), 20)
    part_splits = jax.random.split(jax.random.fold_in(streams_of[19], part), 20)
    return {
        "x_true": scatter_about(part_splits[0], (3, ATOMS), 16.0, 96.0, ((1, 16),), jnp.float32),
        "noise": scatter_about(part_splits[1], (SAMPLES, 3, ATOMS), 1.0, 6.0, ((2, 16),), jnp.float32),
        "noise_level": plant(jax.random.randint(part_splits[2], (SAMPLES,), 0, LEVELS), jax.random.fold_in(part_splits[2], 1), 0, LEVELS - 1).astype(jnp.int32),
        "atom_single": scatter_about(part_splits[3], (ATOMS, ATOM_WIDTH), 1.0, 6.0, ((0, 16),)),
        "atom_token": draw_atom_token(jax.random.fold_in(jax.random.fold_in(streams_of[19], part), 71), part),
        "window_edges": draw_window_edges(jax.random.fold_in(jax.random.fold_in(streams_of[19], part), 71), part),
        "atom_pair_bias": draw_atom_pair_bias(jax.random.fold_in(jax.random.fold_in(streams_of[19], part), 71), part),
        "token_single": scatter_about(part_splits[7], (TOKENS, TOKEN_WIDTH), 1.0, 6.0, ((0, 16),), jnp.float32),
        "pair_bias": draw_pair_bias(jax.random.fold_in(jax.random.fold_in(streams_of[19], part), 71), part),
        "w_coord": scatter_about(streams_of[9], (3, ATOM_WIDTH), 3 ** -0.5, 3.5, (), jnp.float32),
        "w_atom_qkv": scatter_about(streams_of[10], (LAYERS, ATOM_WIDTH, 3 * ATOM_WIDTH), ATOM_WIDTH ** -0.5, 0.5),
        "w_atom_out": scatter_about(streams_of[11], (LAYERS, ATOM_WIDTH, ATOM_WIDTH), ATOM_WIDTH ** -0.5, 0.5),
        "w_atom_up": scatter_about(streams_of[12], (LAYERS, ATOM_WIDTH, 4 * ATOM_WIDTH), ATOM_WIDTH ** -0.5, 0.5),
        "w_atom_down": scatter_about(streams_of[13], (LAYERS, 2 * ATOM_WIDTH, ATOM_WIDTH), (2 * ATOM_WIDTH) ** -0.5, 0.375),
        "w_pool": scatter_about(streams_of[14], (ATOM_WIDTH, TOKEN_WIDTH), ATOM_WIDTH ** -0.5, 0.5),
        "w_token_qkv": scatter_about(streams_of[15], (TOKEN_WIDTH, 3 * TOKEN_WIDTH), TOKEN_WIDTH ** -0.5, 0.21875),
        "w_token_out": scatter_about(streams_of[16], (TOKEN_WIDTH, TOKEN_WIDTH), TOKEN_WIDTH ** -0.5, 0.21875),
        "w_back": scatter_about(streams_of[17], (TOKEN_WIDTH, ATOM_WIDTH), TOKEN_WIDTH ** -0.5, 0.21875),
        "w_final": scatter_about(streams_of[18], (3, ATOM_WIDTH), ATOM_WIDTH ** -0.5, 0.5),
    }


EPS = 1e-05
SIGMA_DATA = 16.0
HIGH = lax.Precision.HIGHEST

def normed(values):
    centre = lax.optimization_barrier(jnp.mean(values, -1, keepdims=True))
    centred = values - centre
    spread = lax.optimization_barrier(jnp.mean(centred * centred, -1, keepdims=True))
    return centred * lax.rsqrt(spread + EPS)

def noise_scale(noise_level):
    upper_root = 160.0 ** (1.0 / 7.0)
    lower_root = 0.0004 ** (1.0 / 7.0)
    fraction = noise_level.astype(jnp.float32) / (LEVELS - 1)
    return SIGMA_DATA * (upper_root + fraction * (lower_root - upper_root)) ** 7

def atom_layer(stream, layer_index, w_atom_qkv, w_atom_out, w_atom_up, w_atom_down, atom_pair_bias, window_edges):
    channels = stream.shape[-1]
    head_count = atom_pair_bias.shape[1]
    head_size = channels // head_count
    block_count = stream.shape[0] // QUERY_BLOCK
    normal_in = normed(stream).astype(jnp.bfloat16)
    projected = jnp.dot(normal_in, w_atom_qkv[layer_index], preferred_element_type=jnp.float32)
    queries = projected[:, :channels].astype(jnp.bfloat16)
    key_rows = jnp.pad(projected[:, channels:2 * channels].astype(jnp.bfloat16), ((RIM, RIM), (0, 0)))
    value_rows = jnp.pad(projected[:, 2 * channels:].astype(jnp.bfloat16), ((RIM, RIM), (0, 0)))
    window = QUERY_BLOCK * jnp.arange(block_count)[:, None] + jnp.arange(KEY_WINDOW)[None, :]
    key_win = key_rows[window].reshape(block_count, KEY_WINDOW, head_count, head_size).astype(jnp.float32)
    value_win = value_rows[window].reshape(block_count, KEY_WINDOW, head_count, head_size).astype(jnp.float32)
    query_blocks = queries.reshape(block_count, QUERY_BLOCK, head_count, head_size).astype(jnp.float32)
    scores = jnp.einsum('bqhd,bkhd->bhqk', query_blocks, key_win) * head_size ** (-0.5) + atom_pair_bias
    position = window - RIM
    allowed = (position >= window_edges[:, 0:1]) & (position < window_edges[:, 1:2])
    allowed_mask = allowed[:, None, None, :]
    row_max = lax.optimization_barrier(jnp.max(jnp.where(allowed_mask, scores, -jnp.inf), -1, keepdims=True))
    expo = jnp.where(allowed_mask, jnp.exp(scores - row_max), 0.0)
    attend = (expo / lax.optimization_barrier(jnp.sum(expo, -1, keepdims=True))).astype(jnp.bfloat16)
    mixed = jnp.einsum('bhqk,bkhd->bqhd', attend.astype(jnp.float32), value_win)
    mixed = mixed.reshape(stream.shape[0], channels).astype(jnp.bfloat16)
    stream = stream + jnp.dot(mixed, w_atom_out[layer_index], preferred_element_type=jnp.float32)
    normal_mid = normed(stream).astype(jnp.bfloat16)
    gated = jnp.dot(normal_mid, w_atom_up[layer_index], preferred_element_type=jnp.float32)
    hidden = (jax.nn.silu(gated[:, :2 * channels]) * gated[:, 2 * channels:]).astype(jnp.bfloat16)
    return stream + jnp.dot(hidden, w_atom_down[layer_index], preferred_element_type=jnp.float32)

def reference(x_true, noise, noise_level, atom_single, atom_token, window_edges, atom_pair_bias, token_single, pair_bias, w_coord, w_atom_qkv, w_atom_out, w_atom_up, w_atom_down, w_pool, w_token_qkv, w_token_out, w_back, w_final):
    sigma_all = noise_scale(noise_level)
    channels = token_single.shape[1]
    head_count = pair_bias.shape[0]
    head_size = channels // head_count
    token_count = token_single.shape[0]

    def one_sample(inputs):
        noise_one, sigma = inputs
        total = sigma * sigma + SIGMA_DATA * SIGMA_DATA
        noisy = x_true + sigma * noise_one
        scaled = noisy * lax.rsqrt(total)
        stream = atom_single.astype(jnp.float32) + scaled[0][:, None] * w_coord[0] + scaled[1][:, None] * w_coord[1] + scaled[2][:, None] * w_coord[2]
        for layer_index in range(ENC_LAYERS):
            stream = atom_layer(stream, layer_index, w_atom_qkv, w_atom_out, w_atom_up, w_atom_down, atom_pair_bias, window_edges)
        encoded = stream
        pooled_atoms = jax.nn.relu(jnp.dot(normed(encoded).astype(jnp.bfloat16), w_pool, preferred_element_type=jnp.float32))
        token_sums = jax.ops.segment_sum(pooled_atoms, atom_token, num_segments=token_count)
        token_counts = jax.ops.segment_sum(jnp.ones(atom_token.shape, jnp.float32), atom_token, num_segments=token_count)
        token_in = token_sums / token_counts[:, None] + token_single
        normal_tok = normed(token_in).astype(jnp.bfloat16)
        projected = jnp.dot(normal_tok, w_token_qkv, preferred_element_type=jnp.float32).astype(jnp.bfloat16)
        queries = projected[:, :channels].reshape(token_count, head_count, head_size).astype(jnp.float32)
        key_rows = projected[:, channels:2 * channels].reshape(token_count, head_count, head_size).astype(jnp.float32)
        value_rows = projected[:, 2 * channels:].reshape(token_count, head_count, head_size).astype(jnp.float32)
        scores = jnp.einsum('qhd,khd->hqk', queries, key_rows) * head_size ** (-0.5) + pair_bias
        row_max = lax.optimization_barrier(jnp.max(scores, -1, keepdims=True))
        expo = jnp.exp(scores - row_max)
        attend = expo / lax.optimization_barrier(jnp.sum(expo, -1, keepdims=True))
        mixed = jnp.einsum('hqk,khd->qhd', attend, value_rows, precision=HIGH)
        mixed = mixed.reshape(token_count, channels).astype(jnp.bfloat16)
        token_state = token_in + jnp.dot(mixed, w_token_out, preferred_element_type=jnp.float32)
        back_proj = jnp.dot(normed(token_state).astype(jnp.bfloat16), w_back, preferred_element_type=jnp.float32)
        stream = encoded + back_proj[atom_token]
        for layer_index in range(ENC_LAYERS, LAYERS):
            stream = atom_layer(stream, layer_index, w_atom_qkv, w_atom_out, w_atom_up, w_atom_down, atom_pair_bias, window_edges)
        update = jnp.dot(normed(stream).astype(jnp.bfloat16), w_final.T, preferred_element_type=jnp.float32).T
        denoised = (SIGMA_DATA * SIGMA_DATA / total * noisy + sigma * SIGMA_DATA * lax.rsqrt(total) * update) / SIGMA_DATA
        return (denoised, token_state)
    denoised, token_state = lax.map(one_sample, (noise, sigma_all))
    return (denoised, token_state)
```

```python
import functools

import jax
import jax.numpy as jnp
from jax import lax
from jax.experimental import pallas as pl
from jax.experimental.pallas import tpu as pltpu
from jax.sharding import Mesh
from jax.sharding import PartitionSpec as P

QUERY_BLOCK = 32
KEY_WINDOW = 128
ENC_LAYERS = 2
LEVELS = 200
RIM = 48
LAYERS = 4

EPS = 1e-05
SIGMA_DATA = 16.0
BF = jnp.bfloat16
F32 = jnp.float32
SEQ = ("z", "p")
VM = pl.BlockSpec(memory_space=pltpu.VMEM)
SM = pl.BlockSpec(memory_space=pltpu.SMEM)
COUNT_LANES = 128


def normed(values):
    centre = jnp.mean(values, -1, keepdims=True)
    centred = values - centre
    spread = jnp.mean(centred * centred, -1, keepdims=True)
    return centred * lax.rsqrt(spread + EPS)


def dot(a, b):
    return jnp.dot(a, b, preferred_element_type=F32)


def dot_nt(a, b):
    return lax.dot_general(a, b, (((1,), (1,)), ((), ())), preferred_element_type=F32)


def noise_scale(noise_level):
    upper_root = 160.0 ** (1.0 / 7.0)
    lower_root = 0.0004 ** (1.0 / 7.0)
    fraction = noise_level.astype(F32) / (LEVELS - 1)
    root = upper_root + fraction * (lower_root - upper_root)
    square = root * root
    return SIGMA_DATA * (square * square * square * root)


def struct(shape, dtype):
    return jax.ShapeDtypeStruct(shape, dtype)


def call(kernel, name, out_shape, specs, args, scratch=()):
    return pl.pallas_call(
        kernel,
        name=name,
        out_shape=out_shape,
        in_specs=specs,
        out_specs=jax.tree.map(lambda _: VM, out_shape),
        scratch_shapes=scratch,
        compiler_params=pltpu.CompilerParams(vmem_limit_bytes=48 * 1024 * 1024),
    )(*args)


def emit_qkv(stream, weight, odd, samples, rows, q_ref, kv_ref, first_ref, second_ref):
    channels = stream.shape[-1]
    projected = dot(normed(stream).astype(BF), weight)
    q_ref[...] = projected[:, :channels].astype(BF)
    kv_ref[...] = projected[:, channels:].astype(BF)
    upper = rows - RIM
    for s in range(samples):
        first = pl.multiple_of(s * rows + jnp.where(odd == 0, upper, 0), 16)
        second = pl.multiple_of(s * rows + jnp.where(odd == 0, 0, upper), 16)
        first_ref[s * RIM : (s + 1) * RIM] = kv_ref[pl.ds(first, RIM)]
        second_ref[s * RIM : (s + 1) * RIM] = kv_ref[pl.ds(second, RIM)]


def block_body(
    meta, edges, q_ref, kv_ref, first_ref, second_ref, stream, bias_ref, weights, layer,
    samples, rows, padded, mixed_ref,
):
    w_out, w_up, w_down = weights
    channels = q_ref.shape[-1]
    heads = bias_ref.shape[1]
    head_size = channels // heads
    blocks = rows // QUERY_BLOCK
    odd = meta[0]
    first_atom = meta[1]
    first = pl.multiple_of(jnp.where(odd == 0, RIM + rows, 0), 16)
    second = pl.multiple_of(jnp.where(odd == 0, 0, RIM + rows), 16)
    for s in range(samples):
        padded[s, RIM : RIM + rows] = kv_ref[s * rows : (s + 1) * rows]
        padded[s, pl.ds(first, RIM)] = first_ref[s * RIM : (s + 1) * RIM]
        padded[s, pl.ds(second, RIM)] = second_ref[s * RIM : (s + 1) * RIM]
    lane = lax.broadcasted_iota(jnp.int32, (QUERY_BLOCK, channels), 1)
    head_masks = [(lane // head_size == h).astype(F32) for h in range(heads)]
    head_bits = [m.astype(BF) for m in head_masks]
    scale = head_size ** (-0.5)
    stacked = heads * QUERY_BLOCK
    for b in range(blocks):
        position = (
            first_atom
            - RIM
            + QUERY_BLOCK * b
            + lax.broadcasted_iota(jnp.int32, (stacked, KEY_WINDOW), 1)
        )
        allowed = (position >= edges[b, 0]) & (position < edges[b, 1])
        bias = jnp.where(
            allowed, bias_ref[b].reshape(stacked, KEY_WINDOW), -jnp.inf
        )
        for s in range(samples):
            at = s * rows + b * QUERY_BLOCK
            query = q_ref[at : at + QUERY_BLOCK]
            spread = jnp.concatenate([query * bit for bit in head_bits], 0)
            window = slice(QUERY_BLOCK * b, QUERY_BLOCK * b + KEY_WINDOW)
            keys = padded[s, window, :channels]
            values = padded[s, window, channels:]
            scores = dot_nt(spread, keys) * scale + bias
            expo = jnp.exp(scores - jnp.max(scores, -1, keepdims=True))
            total = jnp.sum(expo, -1, keepdims=True)
            attend = (expo * (1.0 / total)).astype(BF)
            out = dot(attend, values)
            mixed = out[:QUERY_BLOCK] * head_masks[0]
            for h in range(1, heads):
                mixed += out[h * QUERY_BLOCK : (h + 1) * QUERY_BLOCK] * head_masks[h]
            mixed_ref[at : at + QUERY_BLOCK] = mixed.astype(BF)
    stream = stream + dot(mixed_ref[...], w_out[layer])
    gated = dot(normed(stream).astype(BF), w_up[layer])
    half = gated.shape[-1] // 2
    gate = gated[:, :half]
    hidden = (gate * (1.0 / (1.0 + jnp.exp(-gate))) * gated[:, half:]).astype(BF)
    return stream + dot(hidden, w_down[layer])


def embed_kernel(
    meta, level, x_true, noise, single, w_coord, w_qkv,
    stream_ref, q_ref, kv_ref, first_ref, second_ref, *, samples, rows,
):
    sigma = noise_scale(level[...])
    inverse = lax.rsqrt(sigma * sigma + SIGMA_DATA * SIGMA_DATA)
    base = single[...].astype(F32)
    for s in range(samples):
        scaled = (x_true[...] + sigma[s : s + 1] * noise[s]) * inverse[s : s + 1]
        stream_ref[s * rows : (s + 1) * rows] = base + lax.dot_general(
            scaled, w_coord[...], (((0,), (0,)), ((), ())),
            precision=lax.Precision.HIGHEST, preferred_element_type=F32,
        )
    emit_qkv(stream_ref[...], w_qkv[0], meta[0], samples, rows, q_ref, kv_ref, first_ref, second_ref)


def block_kernel(
    meta, edges, q, kv, first, second, stream, bias, w_out, w_up, w_down, w_qkv,
    stream_ref, q_ref, kv_ref, first_ref, second_ref, padded, mixed, *, layer, samples, rows,
):
    after = block_body(
        meta, edges, q, kv, first, second, stream[...], bias, (w_out, w_up, w_down), layer,
        samples, rows, padded, mixed,
    )
    stream_ref[...] = after
    emit_qkv(after, w_qkv[layer + 1], meta[0], samples, rows, q_ref, kv_ref, first_ref, second_ref)


def selector_of(meta, atom_token, tokens):
    rows = atom_token.shape[-1]
    relative = atom_token[...] - (meta[2] - 1) * tokens
    row = lax.broadcasted_iota(jnp.int32, (3 * tokens, rows), 0)
    return (row == relative).astype(F32)


def pool_kernel(
    meta, edges, q, kv, first, second, stream, bias, w_out, w_up, w_down, w_pool, atom_token,
    stream_ref, own_ref, *rest, layer, samples, rows, tokens,
):
    send_refs, (padded, mixed, sums) = rest[: samples - 1], rest[samples - 1 :]
    after = block_body(
        meta, edges, q, kv, first, second, stream[...], bias, (w_out, w_up, w_down), layer,
        samples, rows, padded, mixed,
    )
    stream_ref[...] = after
    selector = selector_of(meta, atom_token, tokens)
    counts = jnp.sum(selector, -1, keepdims=True)
    selector = selector.astype(BF)
    normal = normed(after).astype(BF)
    width = w_pool.shape[-1]
    for s in range(samples):
        pooled = jnp.maximum(dot(normal[s * rows : (s + 1) * rows], w_pool[...]), 0.0)
        upper = pooled.astype(BF)
        lower = (pooled - upper.astype(F32)).astype(BF)
        sums[s, :, :width] = dot(selector, upper) + dot(selector, lower)
        sums[s, :, width:] = jnp.broadcast_to(counts, (3 * tokens, COUNT_LANES))
    mine = meta[3]
    own_ref[...] = sums[mine]
    for k in range(1, samples):
        send_refs[k - 1][...] = sums[lax.bitwise_xor(mine, k)].astype(BF)


def plane_kernel(meta, own, *rest, samples, tokens):
    got = rest[: samples - 1]
    mid_ref, low_ref, high_ref, total = rest[samples - 1 :]
    mine = meta[3]
    total[...] = jnp.zeros_like(total)
    at = pl.multiple_of(mine * tokens, tokens)
    total[pl.ds(at, 3 * tokens)] += own[...]
    for k in range(1, samples):
        at = pl.multiple_of(lax.bitwise_xor(mine, k) * tokens, tokens)
        total[pl.ds(at, 3 * tokens)] += got[k - 1][...].astype(F32)
    low_ref[...] = total[:tokens].astype(BF)
    high_ref[...] = total[(samples + 1) * tokens :].astype(BF)
    mid_ref[...] = total[tokens : (samples + 1) * tokens]


def token_in_kernel(
    meta, mid, from_low, from_high, single, *rest, samples, tokens
):
    got = rest[: samples - 1]
    state_ref, normal_ref, total = rest[samples - 1 :]
    width = single.shape[-1]
    total[...] = mid[...]
    total[:tokens] += from_low[...].astype(F32)
    total[(samples - 1) * tokens :] += from_high[...].astype(F32)
    state_ref[...] = total[:, :width] / total[:, width : width + 1]
    mine = meta[3]
    at = pl.multiple_of(mine * tokens, tokens)
    state_ref[pl.ds(at, tokens)] += single[...]
    for k in range(1, samples):
        at = pl.multiple_of(lax.bitwise_xor(mine, k) * tokens, tokens)
        state_ref[pl.ds(at, tokens)] += got[k - 1][...]
    normal_ref[...] = normed(state_ref[...]).astype(BF)


def token_kernel(
    meta, state, normal, *rest, samples, tokens, planes, heads
):
    gathered, rest = rest[: planes - 1], rest[planes - 1 :]
    biases, rest = rest[:samples], rest[samples:]
    w_qkv, w_out, w_back = rest[:3]
    out_ref, back_ref, low_ref, high_ref = rest[3:7]
    everyone, bias_all, q_all, k_all, v_all, mixed_all = rest[7:]
    rows = samples * tokens
    width = state.shape[-1]
    head_size = width // heads
    mine = meta[3]
    plane = meta[4]
    everyone[pl.ds(pl.multiple_of(plane * rows, rows), rows)] = normal[...]
    for k in range(1, planes):
        origin = plane - k + jnp.where(plane < k, planes, 0)
        everyone[pl.ds(pl.multiple_of(origin * rows, rows), rows)] = gathered[k - 1][...]
    for k in range(samples):
        at = pl.multiple_of(lax.bitwise_xor(mine, k) * tokens, tokens)
        bias_all[:, pl.ds(at, tokens)] = biases[k][...]
    q_all[...] = dot(normal[...], w_qkv[:, :width]).astype(BF)
    k_all[...] = dot(everyone[...], w_qkv[:, width : 2 * width]).astype(BF)
    v_all[...] = dot(everyone[...], w_qkv[:, 2 * width :]).astype(BF)
    scale = head_size ** (-0.5)
    mixed_all[...] = jnp.zeros_like(mixed_all)
    for h in range(heads):
        start = h * head_size // 128 * 128
        stop = -(-(h + 1) * head_size // 128) * 128
        lane = lax.broadcasted_iota(jnp.int32, (rows, stop - start), 1) + start
        mask = ((lane >= h * head_size) & (lane < (h + 1) * head_size)).astype(F32)
        query = q_all[:, start:stop] * mask.astype(BF)
        scores = dot_nt(query, k_all[:, start:stop]) * scale + bias_all[h]
        expo = jnp.exp(scores - jnp.max(scores, -1, keepdims=True))
        total = jnp.sum(expo, -1, keepdims=True)
        attend = expo * (1.0 / total)
        upper = attend.astype(BF)
        lower = (attend - upper.astype(F32)).astype(BF)
        values = v_all[:, start:stop]
        out = dot(upper, values) + dot(lower, values)
        mixed_all[:, start:stop] += out * mask
    after = state[...] + dot(mixed_all[...].astype(BF), w_out[...])
    out_ref[...] = after
    back = dot(normed(after).astype(BF), w_back[...]).astype(BF)
    back_ref[...] = back
    low_ref[...] = back[:tokens]
    high_ref[...] = back[rows - tokens :]


def back_kernel(meta, back, from_low, from_high, *rest, samples, tokens):
    own_ref, send_refs, padded = rest[0], rest[1:samples], rest[samples]
    padded[:tokens] = from_low[...]
    padded[tokens : (samples + 1) * tokens] = back[...]
    padded[(samples + 1) * tokens :] = from_high[...]
    mine = meta[3]
    own_ref[...] = padded[pl.ds(pl.multiple_of(mine * tokens, tokens), 3 * tokens)]
    for k in range(1, samples):
        at = pl.multiple_of(lax.bitwise_xor(mine, k) * tokens, tokens)
        send_refs[k - 1][...] = padded[pl.ds(at, 3 * tokens)]


def unpool_kernel(meta, stream, atom_token, w_qkv, *rest, samples, rows, tokens):
    backs, rest = rest[:samples], rest[samples:]
    stream_ref, q_ref, kv_ref, first_ref, second_ref, picked = rest
    selector = selector_of(meta, atom_token, tokens).astype(BF)
    mine = meta[3]
    for k in range(samples):
        picked[lax.bitwise_xor(mine, k)] = lax.dot_general(
            selector, backs[k][...], (((0,), (0,)), ((), ())), preferred_element_type=F32
        )
    after = stream[...] + picked[...].reshape(stream.shape)
    stream_ref[...] = after
    emit_qkv(after, w_qkv[ENC_LAYERS], meta[0], samples, rows, q_ref, kv_ref, first_ref, second_ref)


def final_kernel(
    meta, edges, q, kv, first, second, stream, bias, w_out, w_up, w_down, w_final,
    level, x_true, noise, *rest, layer, samples, rows,
):
    states, rest = rest[:samples], rest[samples:]
    denoised_ref, state_ref, padded, mixed = rest
    after = block_body(
        meta, edges, q, kv, first, second, stream[...], bias, (w_out, w_up, w_down), layer,
        samples, rows, padded, mixed,
    )
    mine = meta[3]
    for k in range(samples):
        state_ref[lax.bitwise_xor(mine, k)] = states[k][...]
    normal = normed(after).astype(BF)
    sigma = noise_scale(level[...])
    total = sigma * sigma + SIGMA_DATA * SIGMA_DATA
    keep = SIGMA_DATA * SIGMA_DATA / total
    move = sigma * SIGMA_DATA * lax.rsqrt(total)
    for s in range(samples):
        update = dot_nt(w_final[...], normal[s * rows : (s + 1) * rows])
        noisy = x_true[...] + sigma[s : s + 1] * noise[s]
        denoised_ref[s] = (keep[s : s + 1] * noisy + move[s : s + 1] * update) / SIGMA_DATA


def swap_rims(pair, count):
    first, second = pair
    lower = [(i, i ^ 1) for i in range(count) if (i ^ 1) < count]
    upper = [(i, i + 1) for i in range(1, count - 1, 2)]
    upper += [(j, i) for i, j in upper]
    return lax.ppermute(first, SEQ, lower), lax.ppermute(second, SEQ, upper)


def across(arrays, count):
    return [
        lax.ppermute(a, "p", [(i, i ^ k) for i in range(count)])
        for k, a in enumerate(arrays, 1)
    ]


def shards(
    x_true, noise, noise_level, atom_single, atom_token, window_edges, atom_pair_bias,
    token_single, pair_bias, w_coord, w_atom_qkv, w_atom_out, w_atom_up, w_atom_down,
    w_pool, w_token_qkv, w_token_out, w_back, w_final,
):
    samples = noise.shape[0]
    rows, channels = atom_single.shape
    tokens, width = token_single.shape
    heads = pair_bias.shape[0]
    planes = lax.axis_size("z")
    count = planes * samples
    mine = lax.axis_index("p")
    plane = lax.axis_index("z")
    device = plane * samples + mine
    meta = jnp.stack([device % 2, device * rows, device, mine, plane]).astype(jnp.int32)
    level = noise_level[:, None]
    atom_token = atom_token[None, :]
    whole = samples * rows
    rim = struct((samples * RIM, 2 * channels), BF)
    atom_outs = (
        struct((whole, channels), F32),
        struct((whole, channels), BF),
        struct((whole, 2 * channels), BF),
        rim,
        rim,
    )
    scratch = [
        pltpu.VMEM((samples, rows + 2 * RIM, 2 * channels), BF),
        pltpu.VMEM((whole, channels), BF),
    ]
    sizes = dict(samples=samples, rows=rows)
    biases = across([pair_bias] * (samples - 1), samples)
    singles = across([token_single] * (samples - 1), samples)

    stream, q, kv, first, second = call(
        functools.partial(embed_kernel, **sizes), "embed", atom_outs, [SM] + [VM] * 6,
        (meta, level, x_true, noise, atom_single, w_coord, w_atom_qkv),
    )
    stacks = (w_atom_out, w_atom_up, w_atom_down)
    for layer in range(ENC_LAYERS - 1):
        first, second = swap_rims((first, second), count)
        stream, q, kv, first, second = call(
            functools.partial(block_kernel, layer=layer, **sizes), f"block{layer}", atom_outs,
            [SM, SM] + [VM] * 10,
            (meta, window_edges, q, kv, first, second, stream, atom_pair_bias, *stacks, w_atom_qkv),
            scratch,
        )
    first, second = swap_rims((first, second), count)
    lanes = width + COUNT_LANES
    encoded, own, *sends = call(
        functools.partial(pool_kernel, layer=ENC_LAYERS - 1, tokens=tokens, **sizes), "pool",
        (atom_outs[0], struct((3 * tokens, lanes), F32))
        + (struct((3 * tokens, lanes), BF),) * (samples - 1),
        [SM, SM] + [VM] * 11,
        (meta, window_edges, q, kv, first, second, stream, atom_pair_bias, *stacks, w_pool, atom_token),
        scratch + [pltpu.VMEM((samples, 3 * tokens, lanes), F32)],
    )
    got = across(sends, samples)
    mid, low, high = call(
        functools.partial(plane_kernel, samples=samples, tokens=tokens), "plane",
        (
            struct((samples * tokens, lanes), F32),
            struct((tokens, lanes), BF),
            struct((tokens, lanes), BF),
        ),
        [SM] + [VM] * samples, (meta, own, *got),
        [pltpu.VMEM(((samples + 2) * tokens, lanes), F32)],
    )
    forward = [(i, i + 1) for i in range(planes - 1)]
    backward = [(j, i) for i, j in forward]
    from_low = lax.ppermute(high, "z", forward)
    from_high = lax.ppermute(low, "z", backward)
    state, normal = call(
        functools.partial(token_in_kernel, samples=samples, tokens=tokens), "token_in",
        (struct((samples * tokens, width), F32), struct((samples * tokens, width), BF)),
        [SM] + [VM] * (4 + samples - 1),
        (meta, mid, from_low, from_high, token_single, *singles),
        [pltpu.VMEM((samples * tokens, lanes), F32)],
    )
    gathered = [
        lax.ppermute(normal, "z", [(i, (i + k) % planes) for i in range(planes)])
        for k in range(1, planes)
    ]
    every = planes * samples * tokens
    held = samples * tokens
    state, back, low, high = call(
        functools.partial(
            token_kernel, samples=samples, tokens=tokens, planes=planes, heads=heads
        ),
        "token",
        (
            struct((held, width), F32),
            struct((held, channels), BF),
            struct((tokens, channels), BF),
            struct((tokens, channels), BF),
        ),
        [SM] + [VM] * (2 + planes - 1 + samples + 3),
        (meta, state, normal, *gathered, pair_bias, *biases, w_token_qkv, w_token_out, w_back),
        [
            pltpu.VMEM((every, width), BF),
            pltpu.VMEM((heads, held, every), F32),
            pltpu.VMEM((held, width), BF),
            pltpu.VMEM((every, width), BF),
            pltpu.VMEM((every, width), BF),
            pltpu.VMEM((held, width), F32),
        ],
    )
    from_low = lax.ppermute(high, "z", forward)
    from_high = lax.ppermute(low, "z", backward)
    own, *sends = call(
        functools.partial(back_kernel, samples=samples, tokens=tokens), "back",
        (struct((3 * tokens, channels), BF),) * samples,
        [SM] + [VM] * 3, (meta, back, from_low, from_high),
        [pltpu.VMEM(((samples + 2) * tokens, channels), BF)],
    )
    got = across(sends, samples)
    state = state.reshape(samples, tokens, width)
    pieces = [
        lax.dynamic_index_in_dim(state, lax.bitwise_xor(mine, k), 0, keepdims=False)
        for k in range(samples)
    ]
    states = [pieces[0]] + across(pieces[1:], samples)
    stream, q, kv, first, second = call(
        functools.partial(unpool_kernel, tokens=tokens, **sizes), "unpool", atom_outs,
        [SM] + [VM] * (3 + samples), (meta, encoded, atom_token, w_atom_qkv, own, *got),
        [pltpu.VMEM((samples, rows, channels), F32)],
    )
    for layer in range(ENC_LAYERS, LAYERS - 1):
        first, second = swap_rims((first, second), count)
        stream, q, kv, first, second = call(
            functools.partial(block_kernel, layer=layer, **sizes), f"block{layer}", atom_outs,
            [SM, SM] + [VM] * 10,
            (meta, window_edges, q, kv, first, second, stream, atom_pair_bias, *stacks, w_atom_qkv),
            scratch,
        )
    first, second = swap_rims((first, second), count)
    return call(
        functools.partial(final_kernel, layer=LAYERS - 1, **sizes), "final",
        (struct(noise.shape, F32), struct((samples, tokens, width), F32)),
        [SM, SM] + [VM] * (13 + samples),
        (
            meta, window_edges, q, kv, first, second, stream, atom_pair_bias, *stacks, w_final,
            level, x_true, noise, *states,
        ),
        scratch,
    )


def solution(mesh):
    def step(*args):
        groups, seq = mesh.devices.shape
        samples = args[1].shape[0] // groups
        split = Mesh(
            mesh.devices.reshape(groups, seq // samples, samples), ("groups",) + SEQ
        )
        both = ("groups",) + SEQ
        in_specs = (
            P(None, both),
            P("groups", None, SEQ),
            P("groups"),
            P(both, None),
            P(both),
            P(both, None),
            P(both, None, None, None),
            P(both, None),
            P("groups", SEQ, None),
        ) + (P(),) * 10
        out_specs = (P("groups", None, SEQ), P("groups", SEQ, None))
        return jax.shard_map(
            shards, mesh=split, in_specs=in_specs, out_specs=out_specs, check_vma=False
        )(*args)

    return step
```

```python
import functools

import jax
import jax.numpy as jnp
from jax import lax
from jax.experimental import pallas as pl
from jax.experimental.pallas import tpu as pltpu
from jax.sharding import Mesh
from jax.sharding import PartitionSpec as P

QUERY_BLOCK = 32
KEY_WINDOW = 128
ENC_LAYERS = 2
LEVELS = 200
RIM = 48
LAYERS = 4

EPS = 1e-05
SIGMA_DATA = 16.0
BF = jnp.bfloat16
F32 = jnp.float32
SEQ = ("z", "p")
VM = pl.BlockSpec(memory_space=pltpu.VMEM)
SM = pl.BlockSpec(memory_space=pltpu.SMEM)
HB = pl.BlockSpec(memory_space=pltpu.HBM)
COUNT_LANES = 128
PLACES = 5
LOG2E = 1.4426950408889634


def normed(values):
    centre = jnp.mean(values, -1, keepdims=True)
    centred = values - centre
    spread = jnp.mean(centred * centred, -1, keepdims=True)
    return centred * lax.rsqrt(spread + EPS)


def dot(a, b):
    return jnp.dot(a, b, preferred_element_type=F32)


def dot_nt(a, b):
    return lax.dot_general(a, b, (((1,), (1,)), ((), ())), preferred_element_type=F32)


def noise_scale(noise_level):
    upper_root = 160.0 ** (1.0 / 7.0)
    lower_root = 0.0004 ** (1.0 / 7.0)
    fraction = noise_level.astype(F32) / (LEVELS - 1)
    root = upper_root + fraction * (lower_root - upper_root)
    square = root * root
    return SIGMA_DATA * (square * square * square * root)


def struct(shape, dtype):
    return jax.ShapeDtypeStruct(shape, dtype)


def call(kernel, out_shape, specs, args, scratch=()):
    return pl.pallas_call(
        kernel,
        out_shape=out_shape,
        in_specs=specs,
        out_specs=jax.tree.map(lambda _: VM, out_shape),
        scratch_shapes=scratch,
        compiler_params=pltpu.CompilerParams(vmem_limit_bytes=48 * 1024 * 1024),
    )(
        *[
            pltpu.with_memory_space_constraint(arg, pltpu.HBM) if spec is HB else arg
            for spec, arg in zip(specs, args)
        ]
    )


def halves(odd, lower, upper):
    first = jnp.where(odd == 0, upper, lower)
    second = jnp.where(odd == 0, lower, upper)
    return pl.multiple_of(first, 16), pl.multiple_of(second, 16)


def emit_rims(kv_ref, odd, samples, rows, first_ref, second_ref):
    for s in range(samples):
        first, second = halves(odd, s * rows, (s + 1) * rows - RIM)
        first_ref[s * RIM : (s + 1) * RIM] = kv_ref[pl.ds(first, RIM)]
        second_ref[s * RIM : (s + 1) * RIM] = kv_ref[pl.ds(second, RIM)]


def block_rows(b, samples, rows):
    return [slice(s * rows + b * QUERY_BLOCK, s * rows + (b + 1) * QUERY_BLOCK) for s in range(samples)]


def load_rows(ref, b, samples, rows):
    return jnp.concatenate([ref[at] for at in block_rows(b, samples, rows)], 0)


def store_rows(ref, b, samples, rows, values):
    for s, at in enumerate(block_rows(b, samples, rows)):
        ref[at] = values[s * QUERY_BLOCK : (s + 1) * QUERY_BLOCK]


def run_stages(stages, count):
    held = {}
    for step in range(count + len(stages) - 1):
        for place in reversed(range(len(stages))):
            unit = step - place
            if 0 <= unit < count:
                held[unit] = stages[place](unit, held.get(unit))


def fetch(pairs, sems):
    copies = [
        pltpu.make_async_copy(source, target, sems.at[i])
        for i, (source, target) in enumerate(pairs)
    ]
    for copy in copies:
        copy.start()
    return copies


def run_block(
    meta, q_ref, kv_ref, first_ref, second_ref, stream_ref, bias_ref, weights, copies,
    samples, rows, padded, out_ref, finish,
):
    w_out, w_up, w_down = weights
    channels = q_ref.shape[-1]
    heads = bias_ref.shape[1] // QUERY_BLOCK
    head_size = channels // heads
    blocks = rows // QUERY_BLOCK
    first, second = halves(meta[0], 0, RIM + rows)
    for s in range(samples):
        padded[s, RIM : RIM + rows] = kv_ref[s * rows : (s + 1) * rows]
        padded[s, pl.ds(first, RIM)] = first_ref[s * RIM : (s + 1) * RIM]
        padded[s, pl.ds(second, RIM)] = second_ref[s * RIM : (s + 1) * RIM]
    lane = lax.broadcasted_iota(jnp.int32, (QUERY_BLOCK, channels), 1)
    head_masks = [(lane // head_size == h).astype(F32) for h in range(heads)]
    head_bits = [m.astype(BF) for m in head_masks]
    head_masks = [jnp.concatenate([m, m], 1) for m in head_masks]
    scale = head_size ** (-0.5) * LOG2E
    ones = jnp.ones((KEY_WINDOW, channels), BF)

    def score(b, _):
        bias = bias_ref[b]
        scores = []
        for s, at in enumerate(block_rows(b, samples, rows)):
            query = q_ref[at]
            spread = jnp.concatenate([query * bit for bit in head_bits], 0)
            keys = padded[s, QUERY_BLOCK * b : QUERY_BLOCK * b + KEY_WINDOW, :channels]
            scores.append(dot_nt(spread, keys) * scale + bias)
        return scores

    def soften(b, scores):
        tops = [jnp.max(score, -1, keepdims=True) for score in scores]
        return [jnp.exp2(score - top).astype(BF) for score, top in zip(scores, tops)]

    def mix(b, expos):
        parts = []
        for s, expo in enumerate(expos):
            values = padded[s, QUERY_BLOCK * b : QUERY_BLOCK * b + KEY_WINDOW, channels:]
            out = dot(expo, jnp.concatenate([values, ones], 1))
            merged = out[:QUERY_BLOCK] * head_masks[0]
            for h in range(1, heads):
                merged += out[h * QUERY_BLOCK : (h + 1) * QUERY_BLOCK] * head_masks[h]
            parts.append(merged[:, :channels] * (1.0 / merged[:, channels:]))
        return jnp.concatenate(parts, 0).astype(BF)

    def project(b, mixed):
        if b == 0:
            for copy in copies:
                copy.wait()
        stream = load_rows(stream_ref, b, samples, rows) + dot(mixed, w_out[...])
        return stream, normed(stream).astype(BF)

    def widen(b, held):
        stream, normal = held
        gated = dot(normal, w_up[...])
        half = gated.shape[-1] // 2
        gate = gated[:, :half]
        hidden = gate * (1.0 / (1.0 + jnp.exp(-gate))) * gated[:, half:]
        return stream, hidden.astype(BF)

    def narrow(b, held):
        stream, hidden = held
        stream = stream + dot(hidden, w_down[...])
        if out_ref is not None:
            store_rows(out_ref, b, samples, rows, stream)
        return normed(stream).astype(BF)

    run_stages([score, soften, mix, project, widen, narrow, finish], blocks)


def block_scratch(samples, rows, channels, weights):
    return (
        [pltpu.VMEM((samples, rows + 2 * RIM, 2 * channels), BF)]
        + [pltpu.VMEM(w.shape[1:], w.dtype) for w in weights]
        + [pltpu.SemaphoreType.DMA((len(weights),))]
    )


def embed_kernel(
    meta, x_true_hbm, noise_hbm, single_hbm, w_coord_hbm, w_qkv_hbm,
    stream_ref, q_ref, kv_ref, first_ref, second_ref,
    x_true, noise, single, w_coord, w_qkv, sems, *, samples, rows,
):
    copies = fetch(
        [
            (x_true_hbm, x_true),
            (noise_hbm, noise),
            (single_hbm, single),
            (w_coord_hbm, w_coord),
            (w_qkv_hbm.at[0], w_qkv),
        ],
        sems,
    )
    channels = single.shape[-1]
    sigma, total = sigma_of(meta, samples)
    inverse = lax.rsqrt(total)
    for copy in copies:
        copy.wait()
    base = single[...].astype(F32)
    scaled = [
        (x_true[c : c + 1] + sigma * noise[c]) * inverse for c in range(x_true.shape[0])
    ]

    def place(s, _):
        coords = jnp.concatenate([one[s : s + 1] for one in scaled], 0)
        return base + lax.dot_general(
            coords, w_coord[...], (((0,), (0,)), ((), ())),
            precision=lax.Precision.HIGHEST, preferred_element_type=F32,
        )

    def normalise(s, stream):
        stream_ref[s * rows : (s + 1) * rows] = stream
        return normed(stream).astype(BF)

    def project(s, normal):
        projected = dot(normal, w_qkv[...])
        q_ref[s * rows : (s + 1) * rows] = projected[:, :channels].astype(BF)
        kv_ref[s * rows : (s + 1) * rows] = projected[:, channels:].astype(BF)

    run_stages([place, normalise, project], samples)
    emit_rims(kv_ref, meta[0], samples, rows, first_ref, second_ref)


def mask_kernel(meta, edges, bias_hbm, _, out_ref, bias, sems):
    blocks, heads, queries, window = bias.shape
    copies = fetch([(bias_hbm.at[b], bias.at[b]) for b in range(blocks)], sems)
    lane = lax.broadcasted_iota(jnp.int32, (heads * queries, window), 1)
    for b in range(blocks):
        position = meta[1] - RIM + QUERY_BLOCK * b + lane
        allowed = (position >= edges[0, b]) & (position < edges[1, b])
        copies[b].wait()
        values = bias[b].reshape(heads * queries, window) * LOG2E
        out_ref[b] = jnp.where(allowed, values, -jnp.inf)


def sigma_of(meta, samples):
    row = lax.broadcasted_iota(jnp.int32, (samples, 1), 0)
    levels = jnp.zeros((samples, 1), jnp.int32)
    for s in range(samples):
        levels = jnp.where(row == s, meta[PLACES + s], levels)
    sigma = noise_scale(levels)
    return sigma, sigma * sigma + SIGMA_DATA * SIGMA_DATA


def block_kernel(
    meta, q, kv, first, second, stream, bias, w_out, w_up, w_down, w_qkv,
    stream_ref, q_ref, kv_ref, first_ref, second_ref, padded, out, up, down, qkv, sems,
    *, layer, samples, rows,
):
    copies = fetch(
        [
            (w_out.at[layer], out),
            (w_up.at[layer], up),
            (w_down.at[layer], down),
            (w_qkv.at[layer + 1], qkv),
        ],
        sems,
    )
    channels = q.shape[-1]

    def finish(b, normal):
        projected = dot(normal, qkv[...]).astype(BF)
        store_rows(q_ref, b, samples, rows, projected[:, :channels])
        store_rows(kv_ref, b, samples, rows, projected[:, channels:])

    run_block(
        meta, q, kv, first, second, stream, bias, (out, up, down), copies,
        samples, rows, padded, stream_ref, finish,
    )
    emit_rims(kv_ref, meta[0], samples, rows, first_ref, second_ref)


def selector_of(meta, atom_token, tokens):
    rows = atom_token.shape[-1]
    relative = atom_token[...] - (meta[2] - 1) * tokens
    row = lax.broadcasted_iota(jnp.int32, (3 * tokens, rows), 0)
    return (row == relative).astype(F32)


def pool_kernel(
    meta, q, kv, first, second, stream, bias, w_out, w_up, w_down, w_pool, atom_token,
    *rest, layer, samples, rows, tokens,
):
    single_hbm = rest[0]
    (stream_ref, mid_ref, first_ref, second_ref, single_ref,
     padded, out, up, down, sems, normal_all, sums, pooling, owners, late_sems) = rest[-15:]
    copies = fetch(
        [(w_out.at[layer], out), (w_up.at[layer], up), (w_down.at[layer], down)], sems
    )
    late = fetch([(w_pool, pooling), (atom_token, owners), (single_hbm, single_ref)], late_sems)

    def finish(b, normal):
        store_rows(normal_all, b, samples, rows, normal)

    run_block(
        meta, q, kv, first, second, stream, bias, (out, up, down), copies,
        samples, rows, padded, stream_ref, finish,
    )
    for copy in late:
        copy.wait()
    selector = selector_of(meta, owners, tokens)
    counts = jnp.sum(selector, -1, keepdims=True)
    selector = selector.astype(BF)
    width = w_pool.shape[-1]

    def pool(s, _):
        return jnp.maximum(dot(normal_all[s * rows : (s + 1) * rows], pooling[...]), 0.0)

    def gather(s, pooled):
        upper = pooled.astype(BF)
        lower = (pooled - upper.astype(F32)).astype(BF)
        sums[s, :, :width] = dot(selector, upper) + dot(selector, lower)
        sums[s, :, width:] = jnp.broadcast_to(counts, (3 * tokens, COUNT_LANES))

    run_stages([pool, gather], samples)
    for s in range(samples):
        at = slice(s * tokens, (s + 1) * tokens)
        mid_ref[at] = sums[s, tokens : 2 * tokens]
        first_at, second_at = halves(meta[0], 0, 2 * tokens)
        first_ref[at] = sums[s, pl.ds(first_at, tokens)].astype(BF)
        second_ref[at] = sums[s, pl.ds(second_at, tokens)].astype(BF)


def token_in_kernel(
    meta, mid, first, second, single, _, state_ref, *rest, samples, tokens
):
    send_refs, normal_all = rest[:samples], rest[samples]
    width = single.shape[-1]
    total = mid[...] + first[...].astype(F32) + second[...].astype(F32)
    share = total[:, :width] / total[:, width : width + 1]
    for s in range(samples):
        at = slice(s * tokens, (s + 1) * tokens)
        state = share[at] + single[...]
        state_ref[at] = state
        normal_all[s] = normed(state).astype(BF)
    mine = meta[3]
    for k in range(samples):
        send_refs[k][...] = normal_all[lax.bitwise_xor(mine, k)]


def plane_kernel(meta, *rest, samples, tokens):
    parts, out_ref = rest[:samples], rest[samples]
    mine = meta[3]
    for k in range(samples):
        at = pl.multiple_of(lax.bitwise_xor(mine, k) * tokens, tokens)
        out_ref[pl.ds(at, tokens)] = parts[k][...]


def token_kernel(
    meta, normal, *rest, samples, tokens, planes, heads
):
    gathered, rest = rest[: planes - 1], rest[planes - 1 :]
    biases, rest = rest[:samples], rest[samples:]
    w_qkv, rest = rest[0], rest[1:]
    send_refs = rest[:samples]
    everyone, bias_all, q_all, k_all, v_all, mixed_all, sems = rest[samples:]
    rows = samples * tokens
    width = normal.shape[-1]
    head_size = width // heads
    mine = meta[3]
    plane = meta[4]
    copies = fetch(
        [
            (
                biases[k],
                bias_all.at[:, pl.ds(pl.multiple_of(lax.bitwise_xor(mine, k) * tokens, tokens), tokens)],
            )
            for k in range(samples)
        ],
        sems,
    )
    everyone[pl.ds(pl.multiple_of(plane * rows, rows), rows)] = normal[...]
    for k in range(1, planes):
        origin = plane - k + jnp.where(plane < k, planes, 0)
        everyone[pl.ds(pl.multiple_of(origin * rows, rows), rows)] = gathered[k - 1][...]
    q_all[...] = dot(normal[...], w_qkv[:, :width]).astype(BF)
    k_all[...] = dot(everyone[...], w_qkv[:, width : 2 * width]).astype(BF)
    v_all[...] = dot(everyone[...], w_qkv[:, 2 * width :]).astype(BF)
    for copy in copies:
        copy.wait()
    scale = head_size ** (-0.5) * LOG2E
    mixed_all[...] = jnp.zeros_like(mixed_all)

    def lanes_of(h):
        start = h * head_size // 128 * 128
        stop = -(-(h + 1) * head_size // 128) * 128
        lane = lax.broadcasted_iota(jnp.int32, (rows, stop - start), 1) + start
        mask = ((lane >= h * head_size) & (lane < (h + 1) * head_size)).astype(F32)
        return slice(start, stop), mask

    def score(h, _):
        at, mask = lanes_of(h)
        query = q_all[:, at] * mask.astype(BF)
        return dot_nt(query, k_all[:, at]) * scale + bias_all[h] * LOG2E

    def soften(h, scores):
        expo = jnp.exp2(scores - jnp.max(scores, -1, keepdims=True))
        attend = expo * (1.0 / jnp.sum(expo, -1, keepdims=True))
        upper = attend.astype(BF)
        return upper, (attend - upper.astype(F32)).astype(BF)

    def mix(h, attends):
        at, mask = lanes_of(h)
        values = v_all[:, at]
        mixed_all[:, at] += (dot(attends[0], values) + dot(attends[1], values)) * mask

    run_stages([score, soften, mix], heads)
    for k in range(samples):
        at = pl.multiple_of(lax.bitwise_xor(mine, k) * tokens, tokens)
        send_refs[k][...] = mixed_all[pl.ds(at, tokens)].astype(BF)


def token_out_kernel(meta, state, *rest, samples, tokens):
    parts, (w_out, w_back, out_ref, back_ref, mixed) = rest[:samples], rest[samples:]
    mine = meta[3]
    for k in range(samples):
        at = pl.multiple_of(lax.bitwise_xor(mine, k) * tokens, tokens)
        mixed[pl.ds(at, tokens)] = parts[k][...]
    after = state[...] + dot(mixed[...], w_out[...])
    for s in range(samples):
        out_ref[s] = after[s * tokens : (s + 1) * tokens]
    back_ref[...] = dot(normed(after).astype(BF), w_back[...]).astype(BF)


def unpool_kernel(
    meta, stream, atom_token, back, first, second, w_qkv,
    stream_ref, q_ref, kv_ref, first_ref, second_ref, padded, *, samples, rows, tokens,
):
    channels = stream.shape[-1]
    selector = selector_of(meta, atom_token, tokens).astype(BF)
    first_at, second_at = halves(meta[0], 0, 2 * tokens)

    def place(s, _):
        at = slice(s * tokens, (s + 1) * tokens)
        padded[s, tokens : 2 * tokens] = back[at]
        padded[s, pl.ds(first_at, tokens)] = first[at]
        padded[s, pl.ds(second_at, tokens)] = second[at]
        picked = lax.dot_general(
            selector, padded[s], (((0,), (0,)), ((), ())), preferred_element_type=F32
        )
        return stream[s * rows : (s + 1) * rows] + picked

    def normalise(s, after):
        stream_ref[s * rows : (s + 1) * rows] = after
        return normed(after).astype(BF)

    def project(s, normal):
        projected = dot(normal, w_qkv[ENC_LAYERS])
        q_ref[s * rows : (s + 1) * rows] = projected[:, :channels].astype(BF)
        kv_ref[s * rows : (s + 1) * rows] = projected[:, channels:].astype(BF)

    run_stages([place, normalise, project], samples)
    emit_rims(kv_ref, meta[0], samples, rows, first_ref, second_ref)


def final_kernel(
    meta, q, kv, first, second, stream, bias, w_out, w_up, w_down, w_final,
    x_true, noise, denoised_ref, padded, out, up, down, sems, normal_all,
    *, layer, samples, rows,
):
    copies = fetch(
        [(w_out.at[layer], out), (w_up.at[layer], up), (w_down.at[layer], down)], sems
    )

    def finish(b, normal):
        store_rows(normal_all, b, samples, rows, normal)

    run_block(
        meta, q, kv, first, second, stream, bias, (out, up, down), copies,
        samples, rows, padded, None, finish,
    )
    sigma, total = sigma_of(meta, samples)
    keep = SIGMA_DATA * SIGMA_DATA / total
    move = sigma * SIGMA_DATA * lax.rsqrt(total)
    updates = [
        dot_nt(w_final[...], normal_all[s * rows : (s + 1) * rows]) for s in range(samples)
    ]
    for c in range(x_true.shape[0]):
        noisy = x_true[c : c + 1] + sigma * noise[c]
        update = jnp.concatenate([one[c : c + 1] for one in updates], 0)
        denoised_ref[c] = (keep * noisy + move * update) / SIGMA_DATA


def swap(pair, count):
    first, second = pair
    lower = [(i, i ^ 1) for i in range(count)]
    upper = [(i, i + 1) for i in range(1, count - 1, 2)]
    upper += [(j, i) for i, j in upper]
    upper += [(0, count - 1), (count - 1, 0)]
    second = lax.ppermute(second, SEQ, upper)
    first = lax.ppermute(first, SEQ, lower)
    return first, second


def toward(array, k, count):
    return lax.ppermute(array, "p", [(i, i ^ k) for i in range(count)])


def across(arrays, count):
    return [toward(array, k, count) for k, array in enumerate(arrays, 1)]


def shards(
    x_true, noise, noise_level, atom_single, atom_token, window_edges, atom_pair_bias,
    token_single, pair_bias, w_coord, w_atom_qkv, w_atom_out, w_atom_up, w_atom_down,
    w_pool, w_token_qkv, w_token_out, w_back, w_final,
):
    samples = noise.shape[0]
    rows, channels = atom_single.shape
    tokens, width = token_single.shape
    heads = pair_bias.shape[0]
    planes = lax.axis_size("z")
    count = planes * samples
    mine = lax.axis_index("p")
    plane = lax.axis_index("z")
    device = plane * samples + mine
    places = [device % 2, device * rows, device, mine, plane]
    meta = jnp.stack(places + [noise_level[s] for s in range(samples)])
    atom_token = atom_token[None, :]
    edges = window_edges.T
    noise = noise.transpose(1, 0, 2)
    whole = samples * rows
    held = samples * tokens
    rim = struct((samples * RIM, 2 * channels), BF)
    atom_outs = (
        struct((whole, channels), F32),
        struct((whole, channels), BF),
        struct((whole, 2 * channels), BF),
        rim,
        rim,
    )
    stacks = (w_atom_out, w_atom_up, w_atom_down)
    scratch = block_scratch(samples, rows, channels, stacks)
    wide = block_scratch(samples, rows, channels, stacks + (w_atom_qkv,))
    normals = pltpu.VMEM((whole, channels), BF)
    sizes = dict(samples=samples, rows=rows)

    def block(layer, q, kv, rims, stream):
        return call(
            functools.partial(block_kernel, layer=layer, **sizes), atom_outs,
            [SM] + [VM] * 6 + [HB] * 4,
            (meta, q, kv, *rims, stream, bias, *stacks, w_atom_qkv),
            wide,
        )

    stream, q, kv, *rims = call(
        functools.partial(embed_kernel, **sizes), atom_outs, [SM] + [HB] * 5,
        (meta, x_true, noise, atom_single, w_coord, w_atom_qkv),
        [
            pltpu.VMEM(x_true.shape, F32),
            pltpu.VMEM(noise.shape, F32),
            pltpu.VMEM(atom_single.shape, BF),
            pltpu.VMEM(w_coord.shape, F32),
            pltpu.VMEM(w_atom_qkv.shape[1:], BF),
            pltpu.SemaphoreType.DMA((5,)),
        ],
    )
    blocks, atom_heads, queries, window = atom_pair_bias.shape
    bias = call(
        mask_kernel, struct((blocks, atom_heads * queries, window), F32),
        [SM, SM, HB, VM], (meta, edges, atom_pair_bias, stream),
        [pltpu.VMEM(atom_pair_bias.shape, F32), pltpu.SemaphoreType.DMA((blocks,))],
    )
    for layer in range(ENC_LAYERS - 1):
        rims = swap(rims, count)
        if layer == 0:
            held_bias, _ = lax.optimization_barrier((pair_bias, stream))
            biases = [pair_bias]
            for k in (1, 2):
                biases.append(toward(held_bias, k, samples))
        stream, q, kv, *rims = block(layer, q, kv, rims, stream)
        if layer == 0:
            passed, *rims = lax.optimization_barrier((biases[2], *rims))
            biases.append(toward(passed, 1, samples))
    rims = swap(rims, count)
    lanes = width + COUNT_LANES
    edge = struct((held, lanes), BF)
    encoded, mid, first, second, single = call(
        functools.partial(pool_kernel, layer=ENC_LAYERS - 1, tokens=tokens, **sizes),
        (atom_outs[0], struct((held, lanes), F32), edge, edge, struct((tokens, width), F32)),
        [SM] + [VM] * 6 + [HB] * 7,
        (meta, q, kv, *rims, stream, bias, *stacks, w_pool, atom_token, token_single, biases[1]),
        scratch
        + [
            normals,
            pltpu.VMEM((samples, 3 * tokens, lanes), F32),
            pltpu.VMEM(w_pool.shape, BF),
            pltpu.VMEM(atom_token.shape, jnp.int32),
            pltpu.SemaphoreType.DMA((3,)),
        ],
    )
    rims = swap((first, second), count)
    piece = struct((tokens, width), BF)
    state, *sends = call(
        functools.partial(token_in_kernel, samples=samples, tokens=tokens),
        (struct((held, width), F32),) + (piece,) * samples,
        [SM] + [VM] * 4 + [HB], (meta, mid, *rims, single, biases[3]),
        [pltpu.VMEM((samples, tokens, width), BF)],
    )
    got = across(sends[1:], samples)
    normal = call(
        functools.partial(plane_kernel, samples=samples, tokens=tokens),
        struct((held, width), BF), [SM] + [VM] * samples, (meta, sends[0], *got),
    )
    gathered = []
    for k in range(1, planes):
        shift = [(i, (i + k) % planes) for i in range(planes)]
        gathered.append(lax.ppermute(normal, "z", shift))
    every = planes * held
    sends = call(
        functools.partial(
            token_kernel, samples=samples, tokens=tokens, planes=planes, heads=heads
        ),
        (piece,) * samples,
        [SM] + [VM] * planes + [HB] * samples + [VM],
        (meta, normal, *gathered, *biases, w_token_qkv),
        [
            pltpu.VMEM((every, width), BF),
            pltpu.VMEM((heads, held, every), F32),
            pltpu.VMEM((held, width), BF),
            pltpu.VMEM((every, width), BF),
            pltpu.VMEM((every, width), BF),
            pltpu.VMEM((held, width), F32),
            pltpu.SemaphoreType.DMA((samples,)),
        ],
    )
    got = across(sends[1:], samples)
    token_state, back = call(
        functools.partial(token_out_kernel, samples=samples, tokens=tokens),
        (struct((samples, tokens, width), F32), struct((held, channels), BF)),
        [SM] + [VM] * (1 + samples + 2), (meta, state, sends[0], *got, w_token_out, w_back),
        [pltpu.VMEM((held, width), BF)],
    )
    backs = swap((back, back), count)
    stream, q, kv, *rims = call(
        functools.partial(unpool_kernel, tokens=tokens, **sizes), atom_outs,
        [SM] + [VM] * 6, (meta, encoded, atom_token, back, *backs, w_atom_qkv),
        [pltpu.VMEM((samples, 3 * tokens, channels), BF)],
    )
    for layer in range(ENC_LAYERS, LAYERS - 1):
        rims = swap(rims, count)
        stream, q, kv, *rims = block(layer, q, kv, rims, stream)
    rims = swap(rims, count)
    denoised = call(
        functools.partial(final_kernel, layer=LAYERS - 1, **sizes),
        struct(noise.shape, F32), [SM] + [VM] * 6 + [HB] * 3 + [VM] * 3,
        (
            meta, q, kv, *rims, stream, bias, *stacks, w_final, x_true, noise,
        ),
        scratch + [normals],
    )
    return denoised.transpose(1, 0, 2), token_state


def solution(mesh):
    def step(*args):
        groups, seq = mesh.devices.shape
        samples = args[1].shape[0] // groups
        split = Mesh(
            mesh.devices.reshape(groups, seq // samples, samples), ("groups",) + SEQ
        )
        both = ("groups",) + SEQ
        in_specs = (
            P(None, both),
            P("groups", None, SEQ),
            P("groups"),
            P(both, None),
            P(both),
            P(both, None),
            P(both, None, None, None),
            P(both, None),
            P("groups", SEQ, None),
        ) + (P(),) * 10
        out_specs = (P("groups", None, SEQ), P("groups", SEQ, None))
        return jax.shard_map(
            shards, mesh=split, in_specs=in_specs, out_specs=out_specs, check_vma=False
        )(*args)

    return step
```

```python
import functools

import jax
import jax.numpy as jnp
from jax import lax
from jax.experimental import pallas as pl
from jax.experimental.pallas import tpu as pltpu
from jax.sharding import Mesh
from jax.sharding import PartitionSpec as P

QUERY_BLOCK = 32
KEY_WINDOW = 128
ENC_LAYERS = 2
LEVELS = 200
RIM = 48
LAYERS = 4

EPS = 1e-05
SIGMA_DATA = 16.0
BF = jnp.bfloat16
F32 = jnp.float32
SEQ = ("z", "p")
VM = pl.BlockSpec(memory_space=pltpu.VMEM)
SM = pl.BlockSpec(memory_space=pltpu.SMEM)
HB = pl.BlockSpec(memory_space=pltpu.HBM)
COUNT_LANES = 128
PLACES = 5
LOG2E = 1.4426950408889634


def normed(values):
    centre = jnp.mean(values, -1, keepdims=True)
    centred = values - centre
    spread = jnp.mean(centred * centred, -1, keepdims=True)
    return centred * lax.rsqrt(spread + EPS)


def dot(a, b):
    return jnp.dot(a, b, preferred_element_type=F32)


def dot_nt(a, b):
    return lax.dot_general(a, b, (((1,), (1,)), ((), ())), preferred_element_type=F32)


def noise_scale(noise_level):
    upper_root = 160.0 ** (1.0 / 7.0)
    lower_root = 0.0004 ** (1.0 / 7.0)
    fraction = noise_level.astype(F32) / (LEVELS - 1)
    root = upper_root + fraction * (lower_root - upper_root)
    square = root * root
    return SIGMA_DATA * (square * square * square * root)


def struct(shape, dtype):
    return jax.ShapeDtypeStruct(shape, dtype)


def call(kernel, out_shape, specs, args, scratch=()):
    return pl.pallas_call(
        kernel,
        out_shape=out_shape,
        in_specs=specs,
        out_specs=jax.tree.map(lambda _: VM, out_shape),
        scratch_shapes=scratch,
        compiler_params=pltpu.CompilerParams(vmem_limit_bytes=48 * 1024 * 1024),
    )(
        *[
            pltpu.with_memory_space_constraint(arg, pltpu.HBM) if spec is HB else arg
            for spec, arg in zip(specs, args)
        ]
    )


def halves(odd, lower, upper):
    first = jnp.where(odd == 0, upper, lower)
    second = jnp.where(odd == 0, lower, upper)
    return pl.multiple_of(first, 16), pl.multiple_of(second, 16)


def emit_rims(kv_ref, odd, samples, rows, first_ref, second_ref):
    for s in range(samples):
        first, second = halves(odd, s * rows, (s + 1) * rows - RIM)
        first_ref[s * RIM : (s + 1) * RIM] = kv_ref[pl.ds(first, RIM)]
        second_ref[s * RIM : (s + 1) * RIM] = kv_ref[pl.ds(second, RIM)]


def block_rows(b, samples, rows):
    return [slice(s * rows + b * QUERY_BLOCK, s * rows + (b + 1) * QUERY_BLOCK) for s in range(samples)]


def load_rows(ref, b, samples, rows):
    return jnp.concatenate([ref[at] for at in block_rows(b, samples, rows)], 0)


def store_rows(ref, b, samples, rows, values):
    for s, at in enumerate(block_rows(b, samples, rows)):
        ref[at] = values[s * QUERY_BLOCK : (s + 1) * QUERY_BLOCK]


def run_stages(stages, count):
    held = {}
    for step in range(count + len(stages) - 1):
        for place in reversed(range(len(stages))):
            unit = step - place
            if 0 <= unit < count:
                held[unit] = stages[place](unit, held.get(unit))


def fetch(pairs, sems):
    copies = [
        pltpu.make_async_copy(source, target, sems.at[i])
        for i, (source, target) in enumerate(pairs)
    ]
    for copy in copies:
        copy.start()
    return copies


def run_block(
    meta, q_ref, kv_ref, first_ref, second_ref, stream_ref, bias_ref, weights, copies,
    samples, rows, padded, out_ref, finish,
):
    w_out, w_up, w_down = weights
    channels = q_ref.shape[-1]
    heads = bias_ref.shape[1] // QUERY_BLOCK
    head_size = channels // heads
    blocks = rows // QUERY_BLOCK
    first, second = halves(meta[0], 0, RIM + rows)
    for s in range(samples):
        padded[s, RIM : RIM + rows] = kv_ref[s * rows : (s + 1) * rows]
        padded[s, pl.ds(first, RIM)] = first_ref[s * RIM : (s + 1) * RIM]
        padded[s, pl.ds(second, RIM)] = second_ref[s * RIM : (s + 1) * RIM]
    lane = lax.broadcasted_iota(jnp.int32, (QUERY_BLOCK, channels), 1)
    head_masks = [(lane // head_size == h).astype(F32) for h in range(heads)]
    head_bits = [m.astype(BF) for m in head_masks]
    head_masks = [jnp.concatenate([m, m], 1) for m in head_masks]
    scale = head_size ** (-0.5) * LOG2E
    ones = jnp.ones((KEY_WINDOW, channels), BF)

    def score(b, _):
        bias = bias_ref[b]
        scores = []
        for s, at in enumerate(block_rows(b, samples, rows)):
            query = q_ref[at]
            spread = jnp.concatenate([query * bit for bit in head_bits], 0)
            keys = padded[s, QUERY_BLOCK * b : QUERY_BLOCK * b + KEY_WINDOW, :channels]
            scores.append(dot_nt(spread, keys) * scale + bias)
        return scores

    def soften(b, scores):
        tops = [jnp.max(score, -1, keepdims=True) for score in scores]
        return [jnp.exp2(score - top).astype(BF) for score, top in zip(scores, tops)]

    def mix(b, expos):
        parts = []
        for s, expo in enumerate(expos):
            values = padded[s, QUERY_BLOCK * b : QUERY_BLOCK * b + KEY_WINDOW, channels:]
            out = dot(expo, jnp.concatenate([values, ones], 1))
            merged = out[:QUERY_BLOCK] * head_masks[0]
            for h in range(1, heads):
                merged += out[h * QUERY_BLOCK : (h + 1) * QUERY_BLOCK] * head_masks[h]
            parts.append(merged[:, :channels] * (1.0 / merged[:, channels:]))
        return jnp.concatenate(parts, 0).astype(BF)

    def project(b, mixed):
        if b == 0:
            for copy in copies:
                copy.wait()
        stream = load_rows(stream_ref, b, samples, rows) + dot(mixed, w_out[...])
        return stream, normed(stream).astype(BF)

    def widen(b, held):
        stream, normal = held
        gated = dot(normal, w_up[...])
        half = gated.shape[-1] // 2
        gate = gated[:, :half]
        hidden = gate * (1.0 / (1.0 + jnp.exp(-gate))) * gated[:, half:]
        return stream, hidden.astype(BF)

    def narrow(b, held):
        stream, hidden = held
        stream = stream + dot(hidden, w_down[...])
        if out_ref is not None:
            store_rows(out_ref, b, samples, rows, stream)
        return normed(stream).astype(BF)

    run_stages([score, soften, mix, project, widen, narrow, finish], blocks)


def block_scratch(samples, rows, channels, weights):
    return (
        [pltpu.VMEM((samples, rows + 2 * RIM, 2 * channels), BF)]
        + [pltpu.VMEM(w.shape[1:], w.dtype) for w in weights]
        + [pltpu.SemaphoreType.DMA((len(weights),))]
    )


def embed_kernel(
    meta, x_true_hbm, noise_hbm, single_hbm, w_coord_hbm, w_qkv_hbm,
    stream_ref, q_ref, kv_ref, first_ref, second_ref,
    x_true, noise, single, w_coord, w_qkv, sems, *, samples, rows,
):
    copies = fetch(
        [
            (x_true_hbm, x_true),
            (noise_hbm, noise),
            (single_hbm, single),
            (w_coord_hbm, w_coord),
            (w_qkv_hbm.at[0], w_qkv),
        ],
        sems,
    )
    channels = single.shape[-1]
    sigma, total = sigma_of(meta, samples)
    inverse = lax.rsqrt(total)
    for copy in copies:
        copy.wait()
    base = single[...].astype(F32)
    scaled = [
        (x_true[c : c + 1] + sigma * noise[c]) * inverse for c in range(x_true.shape[0])
    ]

    def place(s, _):
        coords = jnp.concatenate([one[s : s + 1] for one in scaled], 0)
        return base + lax.dot_general(
            coords, w_coord[...], (((0,), (0,)), ((), ())),
            precision=lax.Precision.HIGHEST, preferred_element_type=F32,
        )

    def normalise(s, stream):
        stream_ref[s * rows : (s + 1) * rows] = stream
        return normed(stream).astype(BF)

    def project(s, normal):
        projected = dot(normal, w_qkv[...])
        q_ref[s * rows : (s + 1) * rows] = projected[:, :channels].astype(BF)
        kv_ref[s * rows : (s + 1) * rows] = projected[:, channels:].astype(BF)

    run_stages([place, normalise, project], samples)
    emit_rims(kv_ref, meta[0], samples, rows, first_ref, second_ref)


def mask_kernel(meta, edges, bias_hbm, _, out_ref, bias, sems):
    blocks, heads, queries, window = bias.shape
    copies = fetch([(bias_hbm.at[b], bias.at[b]) for b in range(blocks)], sems)
    lane = lax.broadcasted_iota(jnp.int32, (heads * queries, window), 1)
    for b in range(blocks):
        position = meta[1] - RIM + QUERY_BLOCK * b + lane
        allowed = (position >= edges[0, b]) & (position < edges[1, b])
        copies[b].wait()
        values = bias[b].reshape(heads * queries, window) * LOG2E
        out_ref[b] = jnp.where(allowed, values, -jnp.inf)


def sigma_of(meta, samples):
    row = lax.broadcasted_iota(jnp.int32, (samples, 1), 0)
    levels = jnp.zeros((samples, 1), jnp.int32)
    for s in range(samples):
        levels = jnp.where(row == s, meta[PLACES + s], levels)
    sigma = noise_scale(levels)
    return sigma, sigma * sigma + SIGMA_DATA * SIGMA_DATA


def block_kernel(
    meta, q, kv, first, second, stream, bias, w_out, w_up, w_down, w_qkv,
    stream_ref, q_ref, kv_ref, first_ref, second_ref, padded, out, up, down, qkv, sems,
    *, layer, samples, rows,
):
    copies = fetch(
        [
            (w_out.at[layer], out),
            (w_up.at[layer], up),
            (w_down.at[layer], down),
            (w_qkv.at[layer + 1], qkv),
        ],
        sems,
    )
    channels = q.shape[-1]

    def finish(b, normal):
        projected = dot(normal, qkv[...]).astype(BF)
        store_rows(q_ref, b, samples, rows, projected[:, :channels])
        store_rows(kv_ref, b, samples, rows, projected[:, channels:])

    run_block(
        meta, q, kv, first, second, stream, bias, (out, up, down), copies,
        samples, rows, padded, stream_ref, finish,
    )
    emit_rims(kv_ref, meta[0], samples, rows, first_ref, second_ref)


def selector_of(meta, atom_token, tokens):
    rows = atom_token.shape[-1]
    relative = atom_token[...] - (meta[2] - 1) * tokens
    row = lax.broadcasted_iota(jnp.int32, (3 * tokens, rows), 0)
    return (row == relative).astype(F32)


def pool_kernel(
    meta, q, kv, first, second, stream, bias, w_out, w_up, w_down, w_pool, atom_token,
    *rest, layer, samples, rows, tokens,
):
    single_hbm = rest[0]
    (stream_ref, mid_ref, first_ref, second_ref,
     padded, out, up, down, sems, normal_all, sums, pooling, owners, single, late_sems) = rest[-15:]
    copies = fetch(
        [(w_out.at[layer], out), (w_up.at[layer], up), (w_down.at[layer], down)], sems
    )
    late = fetch([(w_pool, pooling), (atom_token, owners), (single_hbm, single)], late_sems)

    def finish(b, normal):
        store_rows(normal_all, b, samples, rows, normal)

    run_block(
        meta, q, kv, first, second, stream, bias, (out, up, down), copies,
        samples, rows, padded, stream_ref, finish,
    )
    for copy in late:
        copy.wait()
    selector = selector_of(meta, owners, tokens)
    counts = jnp.sum(selector, -1, keepdims=True)
    selector = selector.astype(BF)
    width = w_pool.shape[-1]

    def pool(s, _):
        return jnp.maximum(dot(normal_all[s * rows : (s + 1) * rows], pooling[...]), 0.0)

    def gather(s, pooled):
        upper = pooled.astype(BF)
        lower = (pooled - upper.astype(F32)).astype(BF)
        sums[s, :, :width] = dot(selector, upper) + dot(selector, lower)
        sums[s, :, width:] = jnp.broadcast_to(counts, (3 * tokens, COUNT_LANES))

    run_stages([pool, gather], samples)
    mid_ref[samples * tokens :, :width] = single[...]
    mid_ref[samples * tokens :, width:] = jnp.zeros((tokens, COUNT_LANES), F32)
    for s in range(samples):
        at = slice(s * tokens, (s + 1) * tokens)
        mid_ref[at] = sums[s, tokens : 2 * tokens]
        first_at, second_at = halves(meta[0], 0, 2 * tokens)
        first_ref[at] = sums[s, pl.ds(first_at, tokens)].astype(BF)
        second_ref[at] = sums[s, pl.ds(second_at, tokens)].astype(BF)


def token_in_kernel(
    meta, mid, first, second, _, state_ref, *rest, samples, tokens
):
    send_refs, normal_all = rest[:samples], rest[samples]
    width = state_ref.shape[-1]
    held = samples * tokens
    single = mid[held:, :width]
    total = mid[:held] + first[...].astype(F32) + second[...].astype(F32)
    share = total[:, :width] / total[:, width : width + 1]
    for s in range(samples):
        at = slice(s * tokens, (s + 1) * tokens)
        state = share[at] + single
        state_ref[at] = state
        normal_all[s] = normed(state).astype(BF)
    mine = meta[3]
    for k in range(samples):
        send_refs[k][...] = normal_all[lax.bitwise_xor(mine, k)]


def plane_kernel(meta, *rest, samples, tokens):
    parts, out_ref = rest[:samples], rest[samples]
    mine = meta[3]
    for k in range(samples):
        at = pl.multiple_of(lax.bitwise_xor(mine, k) * tokens, tokens)
        out_ref[pl.ds(at, tokens)] = parts[k][...]


def token_own_kernel(meta, normal, *rest, samples, tokens):
    biases, (w_qkv, q_ref, kv_ref, bias_ref, sems) = rest[:samples], rest[samples:]
    mine = meta[3]
    starts = [
        pl.multiple_of(lax.bitwise_xor(mine, k) * tokens, tokens) for k in range(samples)
    ]
    copies = fetch(
        [(biases[k], bias_ref.at[:, pl.ds(starts[k], tokens)]) for k in range(samples)], sems
    )
    width = normal.shape[-1]
    projected = dot(normal[...], w_qkv[...]).astype(BF)
    q_ref[...] = projected[:, :width]
    kv_ref[...] = projected[:, width:]
    for copy in copies:
        copy.wait()


def token_kernel(meta, q_own, kv_own, bias_all, *rest, samples, tokens, planes, heads):
    gathered, w_qkv, rest = rest[: planes - 1], rest[planes - 1], rest[planes:]
    send_refs, (kv_all, mixed_all) = rest[:samples], rest[samples:]
    rows = samples * tokens
    width = q_own.shape[-1]
    head_size = width // heads
    mine = meta[3]
    plane = meta[4]
    kv_all[pl.ds(pl.multiple_of(plane * rows, rows), rows)] = kv_own[...]
    others = jnp.concatenate([one[...] for one in gathered], 0)
    others = dot(others, w_qkv[:, width:]).astype(BF)
    for k in range(1, planes):
        origin = plane - k + jnp.where(plane < k, planes, 0)
        at = pl.multiple_of(origin * rows, rows)
        kv_all[pl.ds(at, rows)] = others[(k - 1) * rows : k * rows]
    scale = head_size ** (-0.5) * LOG2E
    mixed_all[...] = jnp.zeros_like(mixed_all)

    def lanes_of(h):
        start = h * head_size // 128 * 128
        stop = -(-(h + 1) * head_size // 128) * 128
        lane = lax.broadcasted_iota(jnp.int32, (rows, stop - start), 1) + start
        mask = ((lane >= h * head_size) & (lane < (h + 1) * head_size)).astype(F32)
        return slice(start, stop), mask

    def score(h, _):
        at, mask = lanes_of(h)
        query = q_own[:, at] * mask.astype(BF)
        return dot_nt(query, kv_all[:, at]) * scale + bias_all[h] * LOG2E

    def soften(h, scores):
        expo = jnp.exp2(scores - jnp.max(scores, -1, keepdims=True))
        attend = expo * (1.0 / jnp.sum(expo, -1, keepdims=True))
        upper = attend.astype(BF)
        return upper, (attend - upper.astype(F32)).astype(BF)

    def mix(h, attends):
        at, mask = lanes_of(h)
        values = kv_all[:, width + at.start : width + at.stop]
        mixed_all[:, at] += (dot(attends[0], values) + dot(attends[1], values)) * mask

    run_stages([score, soften, mix], heads)
    for k in range(samples):
        at = pl.multiple_of(lax.bitwise_xor(mine, k) * tokens, tokens)
        send_refs[k][...] = mixed_all[pl.ds(at, tokens)].astype(BF)


def token_out_kernel(meta, state, *rest, samples, tokens):
    parts, (w_out, w_back, out_ref, back_ref, mixed) = rest[:samples], rest[samples:]
    mine = meta[3]
    for k in range(samples):
        at = pl.multiple_of(lax.bitwise_xor(mine, k) * tokens, tokens)
        mixed[pl.ds(at, tokens)] = parts[k][...]
    after = state[...] + dot(mixed[...], w_out[...])
    for s in range(samples):
        out_ref[s] = after[s * tokens : (s + 1) * tokens]
    back_ref[...] = dot(normed(after).astype(BF), w_back[...]).astype(BF)


def unpool_kernel(
    meta, stream, atom_token, back, first, second, w_qkv,
    stream_ref, q_ref, kv_ref, first_ref, second_ref, padded, *, samples, rows, tokens,
):
    channels = stream.shape[-1]
    selector = selector_of(meta, atom_token, tokens).astype(BF)
    first_at, second_at = halves(meta[0], 0, 2 * tokens)

    def place(s, _):
        at = slice(s * tokens, (s + 1) * tokens)
        padded[s, tokens : 2 * tokens] = back[at]
        padded[s, pl.ds(first_at, tokens)] = first[at]
        padded[s, pl.ds(second_at, tokens)] = second[at]
        picked = lax.dot_general(
            selector, padded[s], (((0,), (0,)), ((), ())), preferred_element_type=F32
        )
        return stream[s * rows : (s + 1) * rows] + picked

    def normalise(s, after):
        stream_ref[s * rows : (s + 1) * rows] = after
        return normed(after).astype(BF)

    def project(s, normal):
        projected = dot(normal, w_qkv[ENC_LAYERS])
        q_ref[s * rows : (s + 1) * rows] = projected[:, :channels].astype(BF)
        kv_ref[s * rows : (s + 1) * rows] = projected[:, channels:].astype(BF)

    run_stages([place, normalise, project], samples)
    emit_rims(kv_ref, meta[0], samples, rows, first_ref, second_ref)


def final_kernel(
    meta, q, kv, first, second, stream, bias, w_out, w_up, w_down, w_final,
    x_true, noise, denoised_ref, padded, out, up, down, sems, normal_all,
    *, layer, samples, rows,
):
    copies = fetch(
        [(w_out.at[layer], out), (w_up.at[layer], up), (w_down.at[layer], down)], sems
    )

    def finish(b, normal):
        store_rows(normal_all, b, samples, rows, normal)

    run_block(
        meta, q, kv, first, second, stream, bias, (out, up, down), copies,
        samples, rows, padded, None, finish,
    )
    sigma, total = sigma_of(meta, samples)
    keep = SIGMA_DATA * SIGMA_DATA / total
    move = sigma * SIGMA_DATA * lax.rsqrt(total)
    updates = [
        dot_nt(w_final[...], normal_all[s * rows : (s + 1) * rows]) for s in range(samples)
    ]
    for c in range(x_true.shape[0]):
        noisy = x_true[c : c + 1] + sigma * noise[c]
        update = jnp.concatenate([one[c : c + 1] for one in updates], 0)
        denoised_ref[c] = (keep * noisy + move * update) / SIGMA_DATA


def swap(pair, count):
    first, second = pair
    groups = lax.axis_size("groups")
    lower = [(i, i ^ 1) for i in range(count)]
    upper = []
    for g in range(groups):
        inner = [(g * count + i, g * count + i + 1) for i in range(1, count - 1, 2)]
        upper += inner + [(j, i) for i, j in inner]
        for end in (0, count - 1):
            other = (g ^ 1) * count + end if groups % 2 == 0 else (g + 1) * count - 1 - end
            upper.append((g * count + end, other))
    second = lax.ppermute(second, ("groups",) + SEQ, upper)
    first = lax.ppermute(first, SEQ, lower)
    return first, second


def toward(array, k, count):
    return lax.ppermute(array, "p", [(i, i ^ k) for i in range(count)])


def across(arrays, count):
    return [toward(array, k, count) for k, array in enumerate(arrays, 1)]


def shards(
    x_true, noise, noise_level, atom_single, atom_token, window_edges, atom_pair_bias,
    token_single, pair_bias, w_coord, w_atom_qkv, w_atom_out, w_atom_up, w_atom_down,
    w_pool, w_token_qkv, w_token_out, w_back, w_final,
):
    samples = noise.shape[0]
    rows, channels = atom_single.shape
    tokens, width = token_single.shape
    heads = pair_bias.shape[0]
    planes = lax.axis_size("z")
    count = planes * samples
    mine = lax.axis_index("p")
    plane = lax.axis_index("z")
    device = plane * samples + mine
    places = [device % 2, device * rows, device, mine, plane]
    meta = jnp.stack(places + [noise_level[s] for s in range(samples)])
    atom_token = atom_token[None, :]
    edges = window_edges.T
    noise = noise.transpose(1, 0, 2)
    whole = samples * rows
    held = samples * tokens
    rim = struct((samples * RIM, 2 * channels), BF)
    atom_outs = (
        struct((whole, channels), F32),
        struct((whole, channels), BF),
        struct((whole, 2 * channels), BF),
        rim,
        rim,
    )
    stacks = (w_atom_out, w_atom_up, w_atom_down)
    scratch = block_scratch(samples, rows, channels, stacks)
    wide = block_scratch(samples, rows, channels, stacks + (w_atom_qkv,))
    normals = pltpu.VMEM((whole, channels), BF)
    sizes = dict(samples=samples, rows=rows)

    def block(layer, q, kv, rims, stream):
        return call(
            functools.partial(block_kernel, layer=layer, **sizes), atom_outs,
            [SM] + [VM] * 6 + [HB] * 4,
            (meta, q, kv, *rims, stream, bias, *stacks, w_atom_qkv),
            wide,
        )

    stream, q, kv, *rims = call(
        functools.partial(embed_kernel, **sizes), atom_outs, [SM] + [HB] * 5,
        (meta, x_true, noise, atom_single, w_coord, w_atom_qkv),
        [
            pltpu.VMEM(x_true.shape, F32),
            pltpu.VMEM(noise.shape, F32),
            pltpu.VMEM(atom_single.shape, BF),
            pltpu.VMEM(w_coord.shape, F32),
            pltpu.VMEM(w_atom_qkv.shape[1:], BF),
            pltpu.SemaphoreType.DMA((5,)),
        ],
    )
    blocks, atom_heads, queries, window = atom_pair_bias.shape
    bias = call(
        mask_kernel, struct((blocks, atom_heads * queries, window), F32),
        [SM, SM, HB, VM], (meta, edges, atom_pair_bias, stream),
        [pltpu.VMEM(atom_pair_bias.shape, F32), pltpu.SemaphoreType.DMA((blocks,))],
    )
    for layer in range(ENC_LAYERS - 1):
        rims = swap(rims, count)
        if layer == 0:
            held_bias, _ = lax.optimization_barrier((pair_bias, stream))
            biases = [pair_bias]
            for k in (1, 2):
                biases.append(toward(held_bias, k, samples))
        stream, q, kv, *rims = block(layer, q, kv, rims, stream)
        if layer == 0:
            passed, *rims = lax.optimization_barrier((biases[2], *rims))
            biases.append(toward(passed, 1, samples))
    rims = swap(rims, count)
    lanes = width + COUNT_LANES
    edge = struct((held, lanes), BF)
    encoded, mid, *rims = call(
        functools.partial(pool_kernel, layer=ENC_LAYERS - 1, tokens=tokens, **sizes),
        (atom_outs[0], struct((held + tokens, lanes), F32), edge, edge),
        [SM] + [VM] * 6 + [HB] * 7,
        (meta, q, kv, *rims, stream, bias, *stacks, w_pool, atom_token, token_single, biases[1]),
        scratch
        + [
            normals,
            pltpu.VMEM((samples, 3 * tokens, lanes), F32),
            pltpu.VMEM(w_pool.shape, BF),
            pltpu.VMEM(atom_token.shape, jnp.int32),
            pltpu.VMEM(token_single.shape, F32),
            pltpu.SemaphoreType.DMA((3,)),
        ],
    )
    rims = swap(rims, count)
    piece = struct((tokens, width), BF)
    state, *sends = call(
        functools.partial(token_in_kernel, samples=samples, tokens=tokens),
        (struct((held, width), F32),) + (piece,) * samples,
        [SM] + [VM] * 3 + [HB], (meta, mid, *rims, biases[3]),
        [pltpu.VMEM((samples, tokens, width), BF)],
    )
    got = across(sends[1:], samples)
    normal = call(
        functools.partial(plane_kernel, samples=samples, tokens=tokens),
        struct((held, width), BF), [SM] + [VM] * samples, (meta, sends[0], *got),
    )
    gathered = []
    for k in range(1, planes):
        shift = [(i, (i + k) % planes) for i in range(planes)]
        gathered.append(lax.ppermute(normal, "z", shift))
    every = planes * held
    q_own, kv_own, bias_all = call(
        functools.partial(token_own_kernel, samples=samples, tokens=tokens),
        (
            struct((held, width), BF),
            struct((held, 2 * width), BF),
            struct((heads, held, every), F32),
        ),
        [SM, VM] + [HB] * samples + [VM], (meta, normal, *biases, w_token_qkv),
        [pltpu.SemaphoreType.DMA((samples,))],
    )
    sends = call(
        functools.partial(
            token_kernel, samples=samples, tokens=tokens, planes=planes, heads=heads
        ),
        (piece,) * samples, [SM] + [VM] * (3 + planes),
        (meta, q_own, kv_own, bias_all, *gathered, w_token_qkv),
        [pltpu.VMEM((every, 2 * width), BF), pltpu.VMEM((held, width), F32)],
    )
    got = across(sends[1:], samples)
    token_state, back = call(
        functools.partial(token_out_kernel, samples=samples, tokens=tokens),
        (struct((samples, tokens, width), F32), struct((held, channels), BF)),
        [SM] + [VM] * (1 + samples + 2), (meta, state, sends[0], *got, w_token_out, w_back),
        [pltpu.VMEM((held, width), BF)],
    )
    backs = swap((back, back), count)
    stream, q, kv, *rims = call(
        functools.partial(unpool_kernel, tokens=tokens, **sizes), atom_outs,
        [SM] + [VM] * 6, (meta, encoded, atom_token, back, *backs, w_atom_qkv),
        [pltpu.VMEM((samples, 3 * tokens, channels), BF)],
    )
    for layer in range(ENC_LAYERS, LAYERS - 1):
        rims = swap(rims, count)
        stream, q, kv, *rims = block(layer, q, kv, rims, stream)
    rims = swap(rims, count)
    denoised = call(
        functools.partial(final_kernel, layer=LAYERS - 1, **sizes),
        struct(noise.shape, F32), [SM] + [VM] * 6 + [HB] * 3 + [VM] * 3,
        (
            meta, q, kv, *rims, stream, bias, *stacks, w_final, x_true, noise,
        ),
        scratch + [normals],
    )
    return denoised.transpose(1, 0, 2), token_state


def solution(mesh):
    def step(*args):
        groups, seq = mesh.devices.shape
        samples = args[1].shape[0] // groups
        split = Mesh(
            mesh.devices.reshape(groups, seq // samples, samples), ("groups",) + SEQ
        )
        both = ("groups",) + SEQ
        in_specs = (
            P(None, both),
            P("groups", None, SEQ),
            P("groups"),
            P(both, None),
            P(both),
            P(both, None),
            P(both, None, None, None),
            P(both, None),
            P("groups", SEQ, None),
        ) + (P(),) * 10
        out_specs = (P("groups", None, SEQ), P("groups", SEQ, None))
        return jax.shard_map(
            shards, mesh=split, in_specs=in_specs, out_specs=out_specs, check_vma=False
        )(*args)

    return step
```

```python
import functools

import jax
import jax.numpy as jnp
from jax import lax
from jax.experimental import pallas as pl
from jax.experimental.pallas import tpu as pltpu
from jax.sharding import Mesh
from jax.sharding import PartitionSpec as P

QUERY_BLOCK = 32
KEY_WINDOW = 128
ENC_LAYERS = 2
LEVELS = 200
RIM = 48
LAYERS = 4

EPS = 1e-05
SIGMA_DATA = 16.0
BF = jnp.bfloat16
F32 = jnp.float32
SEQ = ("z", "p")
VM = pl.BlockSpec(memory_space=pltpu.VMEM)
SM = pl.BlockSpec(memory_space=pltpu.SMEM)
HB = pl.BlockSpec(memory_space=pltpu.HBM)
COUNT_LANES = 128
LOG2E = 1.4426950408889634


def normed(values):
    centre = jnp.mean(values, -1, keepdims=True)
    centred = values - centre
    spread = jnp.mean(centred * centred, -1, keepdims=True)
    return centred * lax.rsqrt(spread + EPS)


def dot(a, b):
    return jnp.dot(a, b, preferred_element_type=F32)


def dot_nt(a, b):
    return lax.dot_general(a, b, (((1,), (1,)), ((), ())), preferred_element_type=F32)


def noise_scale(noise_level):
    upper_root = 160.0 ** (1.0 / 7.0)
    lower_root = 0.0004 ** (1.0 / 7.0)
    fraction = noise_level.astype(F32) / (LEVELS - 1)
    root = upper_root + fraction * (lower_root - upper_root)
    square = root * root
    return SIGMA_DATA * (square * square * square * root)


def struct(shape, dtype):
    return jax.ShapeDtypeStruct(shape, dtype)


def call(kernel, out_shape, specs, args, scratch=()):
    return pl.pallas_call(
        kernel,
        out_shape=out_shape,
        in_specs=specs,
        out_specs=jax.tree.map(lambda _: VM, out_shape),
        scratch_shapes=scratch,
        compiler_params=pltpu.CompilerParams(vmem_limit_bytes=48 * 1024 * 1024),
    )(
        *[
            pltpu.with_memory_space_constraint(arg, pltpu.HBM) if spec is HB else arg
            for spec, arg in zip(specs, args)
        ]
    )


def halves(odd, lower, upper):
    first = jnp.where(odd == 0, upper, lower)
    second = jnp.where(odd == 0, lower, upper)
    return pl.multiple_of(first, 16), pl.multiple_of(second, 16)


def emit_rims(kv_ref, odd, samples, rows, first_ref, second_ref):
    for s in range(samples):
        first, second = halves(odd, s * rows, (s + 1) * rows - RIM)
        first_ref[s * RIM : (s + 1) * RIM] = kv_ref[pl.ds(first, RIM)]
        second_ref[s * RIM : (s + 1) * RIM] = kv_ref[pl.ds(second, RIM)]


def block_rows(b, samples, rows):
    return [slice(s * rows + b * QUERY_BLOCK, s * rows + (b + 1) * QUERY_BLOCK) for s in range(samples)]


def load_rows(ref, b, samples, rows):
    return jnp.concatenate([ref[at] for at in block_rows(b, samples, rows)], 0)


def store_rows(ref, b, samples, rows, values):
    for s, at in enumerate(block_rows(b, samples, rows)):
        ref[at] = values[s * QUERY_BLOCK : (s + 1) * QUERY_BLOCK]


def run_stages(stages, count):
    held = {}
    for step in range(count + len(stages) - 1):
        for place in reversed(range(len(stages))):
            unit = step - place
            if 0 <= unit < count:
                held[unit] = stages[place](unit, held.get(unit))


def fetch(pairs, sems):
    copies = [
        pltpu.make_async_copy(source, target, sems.at[i])
        for i, (source, target) in enumerate(pairs)
    ]
    for copy in copies:
        copy.start()
    return copies


def run_block(
    meta, q_ref, kv_ref, first_ref, second_ref, stream_ref, bias_ref, weights, copies,
    samples, rows, padded, out_ref, finish,
):
    w_out, w_up, w_down = weights
    channels = q_ref.shape[-1]
    heads = bias_ref.shape[1] // QUERY_BLOCK
    head_size = channels // heads
    blocks = rows // QUERY_BLOCK
    first, second = halves(meta[0], 0, RIM + rows)
    for s in range(samples):
        padded[s, RIM : RIM + rows] = kv_ref[s * rows : (s + 1) * rows]
        padded[s, pl.ds(first, RIM)] = first_ref[s * RIM : (s + 1) * RIM]
        padded[s, pl.ds(second, RIM)] = second_ref[s * RIM : (s + 1) * RIM]
    lane = lax.broadcasted_iota(jnp.int32, (QUERY_BLOCK, channels), 1)
    head_masks = [(lane // head_size == h).astype(F32) for h in range(heads)]
    head_bits = [m.astype(BF) for m in head_masks]
    head_masks = [jnp.concatenate([m, m], 1) for m in head_masks]
    scale = head_size ** (-0.5) * LOG2E
    ones = jnp.ones((KEY_WINDOW, channels), BF)

    def score(b, _):
        bias = bias_ref[b]
        scores = []
        for s, at in enumerate(block_rows(b, samples, rows)):
            query = q_ref[at]
            spread = jnp.concatenate([query * bit for bit in head_bits], 0)
            keys = padded[s, QUERY_BLOCK * b : QUERY_BLOCK * b + KEY_WINDOW, :channels]
            scores.append(dot_nt(spread, keys) * scale + bias)
        return scores

    def soften(b, scores):
        tops = [jnp.max(score, -1, keepdims=True) for score in scores]
        return [jnp.exp2(score - top).astype(BF) for score, top in zip(scores, tops)]

    def mix(b, expos):
        parts = []
        for s, expo in enumerate(expos):
            values = padded[s, QUERY_BLOCK * b : QUERY_BLOCK * b + KEY_WINDOW, channels:]
            out = dot(expo, jnp.concatenate([values, ones], 1))
            merged = out[:QUERY_BLOCK] * head_masks[0]
            for h in range(1, heads):
                merged += out[h * QUERY_BLOCK : (h + 1) * QUERY_BLOCK] * head_masks[h]
            parts.append(merged[:, :channels] * (1.0 / merged[:, channels:]))
        return jnp.concatenate(parts, 0).astype(BF)

    def project(b, mixed):
        if b == 0:
            for copy in copies:
                copy.wait()
        stream = load_rows(stream_ref, b, samples, rows) + dot(mixed, w_out[...])
        return stream, normed(stream).astype(BF)

    def widen(b, held):
        stream, normal = held
        gated = dot(normal, w_up[...])
        half = gated.shape[-1] // 2
        gate = gated[:, :half]
        hidden = gate * (1.0 / (1.0 + jnp.exp(-gate))) * gated[:, half:]
        return stream, hidden.astype(BF)

    def narrow(b, held):
        stream, hidden = held
        stream = stream + dot(hidden, w_down[...])
        if out_ref is not None:
            store_rows(out_ref, b, samples, rows, stream)
        return normed(stream).astype(BF)

    run_stages([score, soften, mix, project, widen, narrow, finish], blocks)


def block_scratch(samples, rows, channels, weights):
    return (
        [pltpu.VMEM((samples, rows + 2 * RIM, 2 * channels), BF)]
        + [pltpu.VMEM(w.shape[1:], w.dtype) for w in weights]
        + [pltpu.SemaphoreType.DMA((len(weights),))]
    )


def embed_kernel(
    meta, level_hbm, x_true_hbm, noise_hbm, single_hbm, w_coord_hbm, w_qkv_hbm,
    stream_ref, q_ref, kv_ref, first_ref, second_ref,
    level, x_true, noise, single, w_coord, w_qkv, sems, *, samples, rows,
):
    copies = fetch(
        [
            (level_hbm, level),
            (x_true_hbm, x_true),
            (noise_hbm, noise),
            (single_hbm, single),
            (w_coord_hbm, w_coord),
            (w_qkv_hbm.at[0], w_qkv),
        ],
        sems,
    )
    channels = single.shape[-1]
    for copy in copies:
        copy.wait()
    sigma, total = sigma_of(level, samples)
    inverse = lax.rsqrt(total)
    base = single[...].astype(F32)
    scaled = [
        (x_true[c : c + 1] + sigma * noise[c]) * inverse for c in range(x_true.shape[0])
    ]

    def place(s, _):
        coords = jnp.concatenate([one[s : s + 1] for one in scaled], 0)
        return base + lax.dot_general(
            coords, w_coord[...], (((0,), (0,)), ((), ())),
            precision=lax.Precision.HIGHEST, preferred_element_type=F32,
        )

    def normalise(s, stream):
        stream_ref[s * rows : (s + 1) * rows] = stream
        return normed(stream).astype(BF)

    def project(s, normal):
        projected = dot(normal, w_qkv[...])
        q_ref[s * rows : (s + 1) * rows] = projected[:, :channels].astype(BF)
        kv_ref[s * rows : (s + 1) * rows] = projected[:, channels:].astype(BF)

    run_stages([place, normalise, project], samples)
    emit_rims(kv_ref, meta[0], samples, rows, first_ref, second_ref)


def mask_kernel(meta, edges, bias_hbm, _, out_ref, bias, sems):
    blocks, heads, queries, window = bias.shape
    copies = fetch([(bias_hbm.at[b], bias.at[b]) for b in range(blocks)], sems)
    lane = lax.broadcasted_iota(jnp.int32, (heads * queries, window), 1)
    for b in range(blocks):
        position = meta[1] - RIM + QUERY_BLOCK * b + lane
        allowed = (position >= edges[0, b]) & (position < edges[1, b])
        copies[b].wait()
        values = bias[b].reshape(heads * queries, window) * LOG2E
        out_ref[b] = jnp.where(allowed, values, -jnp.inf)


def sigma_of(level, samples):
    row = lax.broadcasted_iota(jnp.int32, (samples, 1), 0)
    levels = jnp.zeros((samples, 1), jnp.int32)
    for s in range(samples):
        levels = jnp.where(row == s, level[s], levels)
    sigma = noise_scale(levels)
    return sigma, sigma * sigma + SIGMA_DATA * SIGMA_DATA


def block_kernel(
    meta, q, kv, first, second, stream, bias, w_out, w_up, w_down, w_qkv,
    stream_ref, q_ref, kv_ref, first_ref, second_ref, padded, out, up, down, qkv, sems,
    *, layer, samples, rows,
):
    copies = fetch(
        [
            (w_out.at[layer], out),
            (w_up.at[layer], up),
            (w_down.at[layer], down),
            (w_qkv.at[layer + 1], qkv),
        ],
        sems,
    )
    channels = q.shape[-1]

    def finish(b, normal):
        projected = dot(normal, qkv[...]).astype(BF)
        store_rows(q_ref, b, samples, rows, projected[:, :channels])
        store_rows(kv_ref, b, samples, rows, projected[:, channels:])

    run_block(
        meta, q, kv, first, second, stream, bias, (out, up, down), copies,
        samples, rows, padded, stream_ref, finish,
    )
    emit_rims(kv_ref, meta[0], samples, rows, first_ref, second_ref)


def selector_of(meta, atom_token, tokens):
    rows = atom_token.shape[-1]
    relative = atom_token[...] - (meta[2] - 1) * tokens
    row = lax.broadcasted_iota(jnp.int32, (3 * tokens, rows), 0)
    return (row == relative).astype(F32)


def pool_kernel(
    meta, q, kv, first, second, stream, bias, w_out, w_up, w_down, w_pool, atom_token,
    *rest, layer, samples, rows, tokens,
):
    single_hbm = rest[0]
    (stream_ref, mid_ref, first_ref, second_ref, first_rim, second_rim,
     padded, out, up, down, sems, normal_all, sums, pooling, owners, single, late_sems) = rest[-17:]
    copies = fetch(
        [(w_out.at[layer], out), (w_up.at[layer], up), (w_down.at[layer], down)], sems
    )
    late = fetch([(w_pool, pooling), (atom_token, owners), (single_hbm, single)], late_sems)

    def finish(b, normal):
        store_rows(normal_all, b, samples, rows, normal)

    run_block(
        meta, q, kv, first, second, stream, bias, (out, up, down), copies,
        samples, rows, padded, stream_ref, finish,
    )
    for copy in late:
        copy.wait()
    selector = selector_of(meta, owners, tokens)
    counts = jnp.sum(selector, -1, keepdims=True)
    selector = selector.astype(BF)
    width = w_pool.shape[-1]

    def pool(s, _):
        return jnp.maximum(dot(normal_all[s * rows : (s + 1) * rows], pooling[...]), 0.0)

    def gather(s, pooled):
        upper = pooled.astype(BF)
        lower = (pooled - upper.astype(F32)).astype(BF)
        sums[s, :, :width] = dot(selector, upper) + dot(selector, lower)
        sums[s, :, width:] = jnp.broadcast_to(counts, (3 * tokens, COUNT_LANES))

    run_stages([pool, gather], samples)
    ends = [owners[:, :RIM], owners[:, rows - RIM :]]
    for at, side in ((first_rim, 0), (second_rim, 1)):
        for s in range(samples):
            start = halves(meta[0], s * rows, (s + 1) * rows - RIM)[side]
            at[s * RIM : (s + 1) * RIM] = stream_ref[pl.ds(start, RIM)]
        named = jnp.where(meta[0] == side, ends[1], ends[0]).astype(F32)
        at[samples * RIM :] = jnp.zeros((8, at.shape[-1]), F32)
        at[samples * RIM : samples * RIM + 1, :RIM] = named
    mid_ref[samples * tokens :, :width] = single[...]
    mid_ref[samples * tokens :, width:] = jnp.zeros((tokens, COUNT_LANES), F32)
    for s in range(samples):
        at = slice(s * tokens, (s + 1) * tokens)
        mid_ref[at] = sums[s, tokens : 2 * tokens]
        first_at, second_at = halves(meta[0], 0, 2 * tokens)
        first_ref[at] = sums[s, pl.ds(first_at, tokens)].astype(BF)
        second_ref[at] = sums[s, pl.ds(second_at, tokens)].astype(BF)


def token_in_kernel(
    meta, mid, first, second, state_ref, *rest, samples, tokens
):
    send_refs, normal_all = rest[:samples], rest[samples]
    width = state_ref.shape[-1]
    held = samples * tokens
    single = mid[held:, :width]
    total = mid[:held] + first[...].astype(F32) + second[...].astype(F32)
    share = total[:, :width] / total[:, width : width + 1]
    for s in range(samples):
        at = slice(s * tokens, (s + 1) * tokens)
        state = share[at] + single
        state_ref[at] = state
        normal_all[s] = normed(state).astype(BF)
    mine = meta[3]
    for k in range(samples):
        send_refs[k][...] = normal_all[lax.bitwise_xor(mine, k)]


def plane_kernel(meta, *rest, samples, tokens):
    parts, out_ref = rest[:samples], rest[samples]
    mine = meta[3]
    for k in range(samples):
        at = pl.multiple_of(lax.bitwise_xor(mine, k) * tokens, tokens)
        out_ref[pl.ds(at, tokens)] = parts[k][...]


def token_own_kernel(meta, normal, *rest, samples, tokens):
    biases, (w_qkv, q_ref, kv_ref, bias_ref, sems) = rest[:samples], rest[samples:]
    mine = meta[3]
    starts = [
        pl.multiple_of(lax.bitwise_xor(mine, k) * tokens, tokens) for k in range(samples)
    ]
    copies = fetch(
        [(biases[k], bias_ref.at[:, pl.ds(starts[k], tokens)]) for k in range(samples)], sems
    )
    width = normal.shape[-1]
    projected = dot(normal[...], w_qkv[...]).astype(BF)
    q_ref[...] = projected[:, :width]
    kv_ref[...] = projected[:, width:]
    for copy in copies:
        copy.wait()


def token_kernel(meta, q_own, kv_own, bias_all, *rest, samples, tokens, planes, heads):
    gathered, w_qkv, rest = rest[: planes - 1], rest[planes - 1], rest[planes:]
    send_refs, (kv_all, mixed_all) = rest[:samples], rest[samples:]
    rows = samples * tokens
    width = q_own.shape[-1]
    head_size = width // heads
    mine = meta[3]
    plane = meta[4]
    kv_all[pl.ds(pl.multiple_of(plane * rows, rows), rows)] = kv_own[...]
    others = jnp.concatenate([one[...] for one in gathered], 0)
    others = dot(others, w_qkv[:, width:]).astype(BF)
    for k in range(1, planes):
        origin = plane - k + jnp.where(plane < k, planes, 0)
        at = pl.multiple_of(origin * rows, rows)
        kv_all[pl.ds(at, rows)] = others[(k - 1) * rows : k * rows]
    scale = head_size ** (-0.5) * LOG2E
    mixed_all[...] = jnp.zeros_like(mixed_all)

    def lanes_of(h):
        start = h * head_size // 128 * 128
        stop = -(-(h + 1) * head_size // 128) * 128
        lane = lax.broadcasted_iota(jnp.int32, (rows, stop - start), 1) + start
        mask = ((lane >= h * head_size) & (lane < (h + 1) * head_size)).astype(F32)
        return slice(start, stop), mask

    def score(h, _):
        at, mask = lanes_of(h)
        query = q_own[:, at] * mask.astype(BF)
        return dot_nt(query, kv_all[:, at]) * scale + bias_all[h] * LOG2E

    def soften(h, scores):
        expo = jnp.exp2(scores - jnp.max(scores, -1, keepdims=True))
        attend = expo * (1.0 / jnp.sum(expo, -1, keepdims=True))
        upper = attend.astype(BF)
        return upper, (attend - upper.astype(F32)).astype(BF)

    def mix(h, attends):
        at, mask = lanes_of(h)
        values = kv_all[:, width + at.start : width + at.stop]
        mixed_all[:, at] += (dot(attends[0], values) + dot(attends[1], values)) * mask

    run_stages([score, soften, mix], heads)
    for k in range(samples):
        at = pl.multiple_of(lax.bitwise_xor(mine, k) * tokens, tokens)
        send_refs[k][...] = mixed_all[pl.ds(at, tokens)].astype(BF)


def token_out_kernel(meta, state, *rest, samples, tokens):
    parts, (w_out, w_back, out_ref, back_ref, mixed) = rest[:samples], rest[samples:]
    mine = meta[3]
    for k in range(samples):
        at = pl.multiple_of(lax.bitwise_xor(mine, k) * tokens, tokens)
        mixed[pl.ds(at, tokens)] = parts[k][...]
    after = state[...] + dot(mixed[...], w_out[...])
    for s in range(samples):
        out_ref[s] = after[s * tokens : (s + 1) * tokens]
    back_ref[...] = dot(normed(after).astype(BF), w_back[...]).astype(BF)


def unpool_kernel(
    meta, stream, atom_token, back, first, second, first_rim, second_rim, w_qkv,
    stream_ref, q_ref, kv_ref, first_ref, second_ref, padded, *, samples, rows, tokens,
):
    channels = stream.shape[-1]
    weight = w_qkv.at[ENC_LAYERS]
    selector = selector_of(meta, atom_token, tokens).astype(BF)
    first_at, second_at = halves(meta[0], 0, 2 * tokens)
    row = lax.broadcasted_iota(jnp.int32, (3 * tokens, RIM), 0).astype(F32)
    base = ((meta[2] - 1) * tokens).astype(F32)
    rims = [
        (rim, (row == rim[samples * RIM : samples * RIM + 1, :RIM] - base).astype(BF), out)
        for rim, out in ((first_rim, first_ref), (second_rim, second_ref))
    ]

    def pick(chosen, s):
        return lax.dot_general(
            chosen, padded[s], (((0,), (0,)), ((), ())), preferred_element_type=F32
        )

    def place(s, _):
        at = slice(s * tokens, (s + 1) * tokens)
        padded[s, tokens : 2 * tokens] = back[at]
        padded[s, pl.ds(first_at, tokens)] = first[at]
        padded[s, pl.ds(second_at, tokens)] = second[at]
        own = stream[s * rows : (s + 1) * rows] + pick(selector, s)
        stream_ref[s * rows : (s + 1) * rows] = own
        parts = [own]
        for rim, chosen, _ in rims:
            parts.append(rim[s * RIM : (s + 1) * RIM] + pick(chosen, s))
        return jnp.concatenate(parts, 0)

    def normalise(s, after):
        return normed(after).astype(BF)

    def project(s, normal):
        projected = dot(normal, weight[...])
        q_ref[s * rows : (s + 1) * rows] = projected[:rows, :channels].astype(BF)
        key_values = projected[:, channels:].astype(BF)
        kv_ref[s * rows : (s + 1) * rows] = key_values[:rows]
        for side, (_, _, out) in enumerate(rims):
            start = rows + side * RIM
            out[s * RIM : (s + 1) * RIM] = key_values[start : start + RIM]

    run_stages([place, normalise, project], samples)


def final_kernel(
    meta, q, kv, first, second, stream, bias, w_out, w_up, w_down, w_final,
    level_hbm, x_true, noise, denoised_ref, padded, out, up, down, sems, normal_all,
    level, late_sems, *, layer, samples, rows,
):
    copies = fetch(
        [(w_out.at[layer], out), (w_up.at[layer], up), (w_down.at[layer], down)], sems
    )
    late = fetch([(level_hbm, level)], late_sems)

    def finish(b, normal):
        store_rows(normal_all, b, samples, rows, normal)

    run_block(
        meta, q, kv, first, second, stream, bias, (out, up, down), copies,
        samples, rows, padded, None, finish,
    )
    late[0].wait()
    sigma, total = sigma_of(level, samples)
    keep = SIGMA_DATA * SIGMA_DATA / total
    move = sigma * SIGMA_DATA * lax.rsqrt(total)
    updates = [
        dot_nt(w_final[...], normal_all[s * rows : (s + 1) * rows]) for s in range(samples)
    ]
    for c in range(x_true.shape[0]):
        noisy = x_true[c : c + 1] + sigma * noise[c]
        update = jnp.concatenate([one[c : c + 1] for one in updates], 0)
        denoised_ref[c] = (keep * noisy + move * update) / SIGMA_DATA


def swap(pair, count):
    first, second = pair
    groups = lax.axis_size("groups")
    lower = [(i, i ^ 1) for i in range(count)]
    upper = []
    for g in range(groups):
        inner = [(g * count + i, g * count + i + 1) for i in range(1, count - 1, 2)]
        upper += inner + [(j, i) for i, j in inner]
        for end in (0, count - 1):
            other = (g ^ 1) * count + end if groups % 2 == 0 else (g + 1) * count - 1 - end
            upper.append((g * count + end, other))
    second = lax.ppermute(second, ("groups",) + SEQ, upper)
    first = lax.ppermute(first, SEQ, lower)
    return first, second


def toward(array, k, count):
    return lax.ppermute(array, "p", [(i, i ^ k) for i in range(count)])


def across(arrays, count):
    return [toward(array, k, count) for k, array in enumerate(arrays, 1)]


def shards(
    x_true, noise, noise_level, atom_single, atom_token, window_edges, atom_pair_bias,
    token_single, pair_bias, w_coord, w_atom_qkv, w_atom_out, w_atom_up, w_atom_down,
    w_pool, w_token_qkv, w_token_out, w_back, w_final,
):
    samples = noise.shape[0]
    rows, channels = atom_single.shape
    tokens, width = token_single.shape
    heads = pair_bias.shape[0]
    planes = lax.axis_size("z")
    count = planes * samples
    mine = lax.axis_index("p")
    plane = lax.axis_index("z")
    device = plane * samples + mine
    meta = jnp.stack([device % 2, device * rows, device, mine, plane]).astype(jnp.int32)
    atom_token = atom_token[None, :]
    edges = window_edges.T
    noise = noise.transpose(1, 0, 2)
    whole = samples * rows
    held = samples * tokens
    rim = struct((samples * RIM, 2 * channels), BF)
    atom_outs = (
        struct((whole, channels), F32),
        struct((whole, channels), BF),
        struct((whole, 2 * channels), BF),
        rim,
        rim,
    )
    stacks = (w_atom_out, w_atom_up, w_atom_down)
    scratch = block_scratch(samples, rows, channels, stacks)
    wide = block_scratch(samples, rows, channels, stacks + (w_atom_qkv,))
    normals = pltpu.VMEM((whole, channels), BF)
    sizes = dict(samples=samples, rows=rows)

    def block(layer, q, kv, rims, stream):
        return call(
            functools.partial(block_kernel, layer=layer, **sizes), atom_outs,
            [SM] + [VM] * 6 + [HB] * 4,
            (meta, q, kv, *rims, stream, bias, *stacks, w_atom_qkv),
            wide,
        )

    stream, q, kv, *rims = call(
        functools.partial(embed_kernel, **sizes), atom_outs, [SM] + [HB] * 6,
        (meta, noise_level, x_true, noise, atom_single, w_coord, w_atom_qkv),
        [
            pltpu.SMEM(noise_level.shape, jnp.int32),
            pltpu.VMEM(x_true.shape, F32),
            pltpu.VMEM(noise.shape, F32),
            pltpu.VMEM(atom_single.shape, BF),
            pltpu.VMEM(w_coord.shape, F32),
            pltpu.VMEM(w_atom_qkv.shape[1:], BF),
            pltpu.SemaphoreType.DMA((6,)),
        ],
    )
    blocks, atom_heads, queries, window = atom_pair_bias.shape
    bias = call(
        mask_kernel, struct((blocks, atom_heads * queries, window), F32),
        [SM, SM, HB, VM], (meta, edges, atom_pair_bias, stream),
        [pltpu.VMEM(atom_pair_bias.shape, F32), pltpu.SemaphoreType.DMA((blocks,))],
    )
    for layer in range(ENC_LAYERS - 1):
        rims = swap(rims, count)
        if layer == 0:
            held_bias, _ = lax.optimization_barrier((pair_bias, stream))
            biases = [pair_bias]
            for k in (1, 2):
                biases.append(toward(held_bias, k, samples))
        stream, q, kv, *rims = block(layer, q, kv, rims, stream)
    rims = swap(rims, count)
    lanes = width + COUNT_LANES
    edge = struct((held, lanes), BF)
    stream_rim = struct((samples * RIM + 8, channels), F32)
    encoded, mid, first, second, *stream_rims = call(
        functools.partial(pool_kernel, layer=ENC_LAYERS - 1, tokens=tokens, **sizes),
        (atom_outs[0], struct((held + tokens, lanes), F32), edge, edge, stream_rim, stream_rim),
        [SM] + [VM] * 6 + [HB] * 6 + [VM] * 2,
        (
            meta, q, kv, *rims, stream, bias, *stacks, w_pool, atom_token, token_single,
            *biases[1:3],
        ),
        scratch
        + [
            normals,
            pltpu.VMEM((samples, 3 * tokens, lanes), F32),
            pltpu.VMEM(w_pool.shape, BF),
            pltpu.VMEM(atom_token.shape, jnp.int32),
            pltpu.VMEM(token_single.shape, F32),
            pltpu.SemaphoreType.DMA((3,)),
        ],
    )
    passed, _ = lax.optimization_barrier((biases[2], mid))
    biases.append(toward(passed, 1, samples))
    rims = swap((first, second), count)
    piece = struct((tokens, width), BF)
    state, *sends = call(
        functools.partial(token_in_kernel, samples=samples, tokens=tokens),
        (struct((held, width), F32),) + (piece,) * samples,
        [SM] + [VM] * 3, (meta, mid, *rims),
        [pltpu.VMEM((samples, tokens, width), BF)],
    )
    got = across(sends[1:], samples)
    normal = call(
        functools.partial(plane_kernel, samples=samples, tokens=tokens),
        struct((held, width), BF), [SM] + [VM] * samples, (meta, sends[0], *got),
    )
    gathered = []
    for k in range(1, planes):
        shift = [(i, (i + k) % planes) for i in range(planes)]
        gathered.append(lax.ppermute(normal, "z", shift))
    stream_rims = swap(stream_rims, count)
    every = planes * held
    q_own, kv_own, bias_all = call(
        functools.partial(token_own_kernel, samples=samples, tokens=tokens),
        (
            struct((held, width), BF),
            struct((held, 2 * width), BF),
            struct((heads, held, every), F32),
        ),
        [SM, VM, HB] + [VM] * samples, (meta, normal, *biases, w_token_qkv),
        [pltpu.SemaphoreType.DMA((samples,))],
    )
    sends = call(
        functools.partial(
            token_kernel, samples=samples, tokens=tokens, planes=planes, heads=heads
        ),
        (piece,) * samples, [SM] + [VM] * (3 + planes),
        (meta, q_own, kv_own, bias_all, *gathered, w_token_qkv),
        [pltpu.VMEM((every, 2 * width), BF), pltpu.VMEM((held, width), F32)],
    )
    got = across(sends[1:], samples)
    token_state, back = call(
        functools.partial(token_out_kernel, samples=samples, tokens=tokens),
        (struct((samples, tokens, width), F32), struct((held, channels), BF)),
        [SM] + [VM] * (1 + samples + 2), (meta, state, sends[0], *got, w_token_out, w_back),
        [pltpu.VMEM((held, width), BF)],
    )
    backs = swap((back, back), count)
    stream, q, kv, *rims = call(
        functools.partial(unpool_kernel, tokens=tokens, **sizes), atom_outs,
        [SM] + [VM] * 8,
        (meta, encoded, atom_token, back, *backs, *stream_rims, w_atom_qkv),
        [pltpu.VMEM((samples, 3 * tokens, channels), BF)],
    )
    for layer in range(ENC_LAYERS, LAYERS - 1):
        if layer > ENC_LAYERS:
            rims = swap(rims, count)
        stream, q, kv, *rims = block(layer, q, kv, rims, stream)
    rims = swap(rims, count)
    denoised = call(
        functools.partial(final_kernel, layer=LAYERS - 1, **sizes),
        struct(noise.shape, F32), [SM] + [VM] * 6 + [HB] * 3 + [VM, HB, VM, VM],
        (
            meta, q, kv, *rims, stream, bias, *stacks, w_final, noise_level, x_true, noise,
        ),
        scratch
        + [
            normals,
            pltpu.SMEM(noise_level.shape, jnp.int32),
            pltpu.SemaphoreType.DMA((1,)),
        ],
    )
    return denoised.transpose(1, 0, 2), token_state


def solution(mesh):
    def step(*args):
        groups, seq = mesh.devices.shape
        samples = args[1].shape[0] // groups
        split = Mesh(
            mesh.devices.reshape(groups, seq // samples, samples), ("groups",) + SEQ
        )
        both = ("groups",) + SEQ
        in_specs = (
            P(None, both),
            P("groups", None, SEQ),
            P("groups"),
            P(both, None),
            P(both),
            P(both, None),
            P(both, None, None, None),
            P(both, None),
            P("groups", SEQ, None),
        ) + (P(),) * 10
        out_specs = (P("groups", None, SEQ), P("groups", SEQ, None))
        return jax.shard_map(
            shards, mesh=split, in_specs=in_specs, out_specs=out_specs, check_vma=False
        )(*args)

    return step
```

```python
import functools

import jax
import jax.numpy as jnp
from jax import lax
from jax.experimental import pallas as pl
from jax.experimental.pallas import tpu as pltpu
from jax.sharding import Mesh
from jax.sharding import PartitionSpec as P

QUERY_BLOCK = 32
KEY_WINDOW = 128
ENC_LAYERS = 2
LEVELS = 200
RIM = 48
LAYERS = 4

EPS = 1e-05
SIGMA_DATA = 16.0
BF = jnp.bfloat16
F32 = jnp.float32
SEQ = ("z", "p")
VM = pl.BlockSpec(memory_space=pltpu.VMEM)
SM = pl.BlockSpec(memory_space=pltpu.SMEM)
HB = pl.BlockSpec(memory_space=pltpu.HBM)
COUNT_LANES = 128
LOG2E = 1.4426950408889634


def normed(values):
    centre = jnp.mean(values, -1, keepdims=True)
    centred = values - centre
    spread = jnp.mean(centred * centred, -1, keepdims=True)
    return centred * lax.rsqrt(spread + EPS)


def dot(a, b):
    return jnp.dot(a, b, preferred_element_type=F32)


def dot_nt(a, b):
    return lax.dot_general(a, b, (((1,), (1,)), ((), ())), preferred_element_type=F32)


def noise_scale(noise_level):
    upper_root = 160.0 ** (1.0 / 7.0)
    lower_root = 0.0004 ** (1.0 / 7.0)
    fraction = noise_level.astype(F32) / (LEVELS - 1)
    root = upper_root + fraction * (lower_root - upper_root)
    square = root * root
    return SIGMA_DATA * (square * square * square * root)


def struct(shape, dtype):
    return jax.ShapeDtypeStruct(shape, dtype)


def call(kernel, out_shape, specs, args, scratch=(), out_specs=None):
    return pl.pallas_call(
        kernel,
        out_shape=out_shape,
        in_specs=specs,
        out_specs=out_specs or jax.tree.map(lambda _: VM, out_shape),
        scratch_shapes=scratch,
        compiler_params=pltpu.CompilerParams(vmem_limit_bytes=48 * 1024 * 1024),
    )(
        *[
            pltpu.with_memory_space_constraint(arg, pltpu.HBM) if spec is HB else arg
            for spec, arg in zip(specs, args)
        ]
    )


def halves(odd, lower, upper):
    first = jnp.where(odd == 0, upper, lower)
    second = jnp.where(odd == 0, lower, upper)
    return pl.multiple_of(first, 16), pl.multiple_of(second, 16)


def emit_rims(kv_ref, odd, samples, rows, first_ref, second_ref):
    for s in range(samples):
        first, second = halves(odd, s * rows, (s + 1) * rows - RIM)
        first_ref[s * RIM : (s + 1) * RIM] = kv_ref[pl.ds(first, RIM)]
        second_ref[s * RIM : (s + 1) * RIM] = kv_ref[pl.ds(second, RIM)]


def unit_rows(samples, rows):
    starts = [(b, s, s * rows + b * QUERY_BLOCK) for b in range(rows // QUERY_BLOCK) for s in range(samples)]
    return [(b, s, slice(at, at + QUERY_BLOCK)) for b, s, at in starts]


def in_stages(stages, units):
    held = [None] * len(units)
    for stage in stages:
        held = [stage(unit, before) for unit, before in zip(units, held)]


def fetch(pairs, sems):
    copies = [
        pltpu.make_async_copy(source, target, sems.at[i])
        for i, (source, target) in enumerate(pairs)
    ]
    for copy in copies:
        copy.start()
    return copies


def run_block(
    meta, q_ref, kv_ref, first_ref, second_ref, stream_ref, bias_ref, weights, copies,
    samples, rows, padded, mixed, out_ref,
):
    w_out, w_up, w_down = weights
    channels = q_ref.shape[-1]
    heads = bias_ref.shape[1] // QUERY_BLOCK
    head_size = channels // heads
    first, second = halves(meta[0], 0, RIM + rows)
    for s in range(samples):
        padded[s, RIM : RIM + rows] = kv_ref[s * rows : (s + 1) * rows]
        padded[s, pl.ds(first, RIM)] = first_ref[s * RIM : (s + 1) * RIM]
        padded[s, pl.ds(second, RIM)] = second_ref[s * RIM : (s + 1) * RIM]
    lane = lax.broadcasted_iota(jnp.int32, (QUERY_BLOCK, channels), 1)
    head_masks = [(lane // head_size == h).astype(F32) for h in range(heads)]
    head_bits = [m.astype(BF) for m in head_masks]
    head_masks = [jnp.concatenate([m, m], 1) for m in head_masks]
    scale = head_size ** (-0.5) * LOG2E
    ones = jnp.ones((KEY_WINDOW, channels), BF)

    units = unit_rows(samples, rows)

    def window(b):
        return slice(QUERY_BLOCK * b, QUERY_BLOCK * b + KEY_WINDOW)

    def score(unit, _):
        b, s, at = unit
        query = q_ref[at]
        spread = jnp.concatenate([query * bit for bit in head_bits], 0)
        return dot_nt(spread, padded[s, window(b), :channels]) * scale + bias_ref[b]

    def soften(_, scores):
        return jnp.exp2(scores - jnp.max(scores, -1, keepdims=True)).astype(BF)

    def mix(unit, expo):
        b, s, at = unit
        values = padded[s, window(b), channels:]
        out = dot(expo, jnp.concatenate([values, ones], 1))
        merged = out[:QUERY_BLOCK] * head_masks[0]
        for h in range(1, heads):
            merged += out[h * QUERY_BLOCK : (h + 1) * QUERY_BLOCK] * head_masks[h]
        mixed[at] = (merged[:, :channels] * (1.0 / merged[:, channels:])).astype(BF)

    in_stages([score, soften, mix], units)
    for copy in copies:
        copy.wait()
    stream = stream_ref[...] + dot(mixed[...], w_out[...])
    gated = dot(normed(stream).astype(BF), w_up[...])
    half = gated.shape[-1] // 2
    gate = gated[:, :half]
    hidden = (gate * (1.0 / (1.0 + jnp.exp(-gate))) * gated[:, half:]).astype(BF)
    stream = stream + dot(hidden, w_down[...])
    if out_ref is not None:
        out_ref[...] = stream
    return normed(stream).astype(BF)


def block_scratch(samples, rows, channels, weights):
    return (
        [
            pltpu.VMEM((samples, rows + 2 * RIM, 2 * channels), BF),
            pltpu.VMEM((samples * rows, channels), BF),
        ]
        + [pltpu.VMEM(w.shape[1:], w.dtype) for w in weights]
        + [pltpu.SemaphoreType.DMA((len(weights),))]
    )


def embed_kernel(
    meta, level_hbm, x_true_hbm, noise_hbm, single_hbm, w_coord_hbm, w_qkv_hbm,
    stream_ref, q_ref, kv_ref, first_ref, second_ref,
    level, x_true, noise, single, w_coord, w_qkv, sems, *, samples, rows,
):
    copies = fetch(
        [
            (level_hbm, level),
            (x_true_hbm, x_true),
            (noise_hbm, noise),
            (single_hbm, single),
            (w_coord_hbm, w_coord),
            (w_qkv_hbm.at[0], w_qkv),
        ],
        sems,
    )
    channels = single.shape[-1]
    for copy in copies:
        copy.wait()
    sigma, total = sigma_of(level, samples)
    inverse = lax.rsqrt(total)
    base = single[...].astype(F32)
    scaled = [
        (x_true[c : c + 1] + sigma * noise[c]) * inverse for c in range(x_true.shape[0])
    ]

    def place(s, _):
        coords = jnp.concatenate([one[s : s + 1] for one in scaled], 0)
        return base + lax.dot_general(
            coords, w_coord[...], (((0,), (0,)), ((), ())),
            precision=lax.Precision.HIGHEST, preferred_element_type=F32,
        )

    def normalise(s, stream):
        stream_ref[s * rows : (s + 1) * rows] = stream
        return normed(stream).astype(BF)

    def project(s, normal):
        projected = dot(normal, w_qkv[...])
        q_ref[s * rows : (s + 1) * rows] = projected[:, :channels].astype(BF)
        kv_ref[s * rows : (s + 1) * rows] = projected[:, channels:].astype(BF)

    in_stages([place, normalise, project], range(samples))
    emit_rims(kv_ref, meta[0], samples, rows, first_ref, second_ref)


def mask_kernel(meta, edges, bias_hbm, _, out_ref, bias, sems):
    blocks, heads, queries, window = bias.shape
    copies = fetch([(bias_hbm.at[b], bias.at[b]) for b in range(blocks)], sems)
    lane = lax.broadcasted_iota(jnp.int32, (heads * queries, window), 1)
    for b in range(blocks):
        position = meta[1] - RIM + QUERY_BLOCK * b + lane
        allowed = (position >= edges[0, b]) & (position < edges[1, b])
        copies[b].wait()
        values = bias[b].reshape(heads * queries, window) * LOG2E
        out_ref[b] = jnp.where(allowed, values, -jnp.inf)


def sigma_of(level, samples):
    row = lax.broadcasted_iota(jnp.int32, (samples, 1), 0)
    levels = jnp.zeros((samples, 1), jnp.int32)
    for s in range(samples):
        levels = jnp.where(row == s, level[s], levels)
    sigma = noise_scale(levels)
    return sigma, sigma * sigma + SIGMA_DATA * SIGMA_DATA


def block_kernel(
    meta, q, kv, first, second, stream, bias, w_out, w_up, w_down, w_qkv,
    stream_ref, q_ref, kv_ref, first_ref, second_ref, padded, mixed, out, up, down, qkv, sems,
    *, layer, samples, rows,
):
    copies = fetch(
        [
            (w_out.at[layer], out),
            (w_up.at[layer], up),
            (w_down.at[layer], down),
            (w_qkv.at[layer + 1], qkv),
        ],
        sems,
    )
    channels = q.shape[-1]

    normal = run_block(
        meta, q, kv, first, second, stream, bias, (out, up, down), copies,
        samples, rows, padded, mixed, stream_ref,
    )
    projected = dot(normal, qkv[...]).astype(BF)
    q_ref[...] = projected[:, :channels]
    kv_ref[...] = projected[:, channels:]
    emit_rims(kv_ref, meta[0], samples, rows, first_ref, second_ref)


def selector_of(meta, atom_token, tokens):
    rows = atom_token.shape[-1]
    relative = atom_token[...] - (meta[2] - 1) * tokens
    row = lax.broadcasted_iota(jnp.int32, (3 * tokens, rows), 0)
    return (row == relative).astype(F32)


def pool_kernel(
    meta, q, kv, first, second, stream, bias, w_out, w_up, w_down, w_pool, atom_token,
    *rest, layer, samples, rows, tokens,
):
    single_hbm = rest[0]
    (stream_ref, mid_ref, first_ref, second_ref, first_rim, second_rim,
     padded, mixed, out, up, down, sems, sums, pooling, owners, single, late_sems) = rest[-17:]
    copies = fetch(
        [(w_out.at[layer], out), (w_up.at[layer], up), (w_down.at[layer], down)], sems
    )
    late = fetch([(w_pool, pooling), (atom_token, owners), (single_hbm, single)], late_sems)

    normal = run_block(
        meta, q, kv, first, second, stream, bias, (out, up, down), copies,
        samples, rows, padded, mixed, stream_ref,
    )
    for copy in late:
        copy.wait()
    selector = selector_of(meta, owners, tokens)
    counts = jnp.sum(selector, -1, keepdims=True)
    selector = selector.astype(BF)
    width = w_pool.shape[-1]

    def pool(s, _):
        return jnp.maximum(dot(normal[s * rows : (s + 1) * rows], pooling[...]), 0.0)

    def gather(s, pooled):
        upper = pooled.astype(BF)
        lower = (pooled - upper.astype(F32)).astype(BF)
        sums[s, :, :width] = dot(selector, upper) + dot(selector, lower)
        sums[s, :, width:] = jnp.broadcast_to(counts, (3 * tokens, COUNT_LANES))

    in_stages([pool, gather], range(samples))
    ends = [owners[:, :RIM], owners[:, rows - RIM :]]
    for at, side in ((first_rim, 0), (second_rim, 1)):
        for s in range(samples):
            start = halves(meta[0], s * rows, (s + 1) * rows - RIM)[side]
            at[s * RIM : (s + 1) * RIM] = stream_ref[pl.ds(start, RIM)]
        named = jnp.where(meta[0] == side, ends[1], ends[0]).astype(F32)
        at[samples * RIM :] = jnp.zeros((8, at.shape[-1]), F32)
        at[samples * RIM : samples * RIM + 1, :RIM] = named
    mid_ref[samples * tokens :, :width] = single[...]
    mid_ref[samples * tokens :, width:] = jnp.zeros((tokens, COUNT_LANES), F32)
    for s in range(samples):
        at = slice(s * tokens, (s + 1) * tokens)
        mid_ref[at] = sums[s, tokens : 2 * tokens]
        first_at, second_at = halves(meta[0], 0, 2 * tokens)
        first_ref[at] = sums[s, pl.ds(first_at, tokens)].astype(BF)
        second_ref[at] = sums[s, pl.ds(second_at, tokens)].astype(BF)


def token_in_kernel(
    meta, mid, first, second, state_ref, *rest, samples, tokens
):
    send_refs, normal_all = rest[:samples], rest[samples]
    width = state_ref.shape[-1]
    held = samples * tokens
    single = mid[held:, :width]
    total = mid[:held] + first[...].astype(F32) + second[...].astype(F32)
    share = total[:, :width] / total[:, width : width + 1]
    for s in range(samples):
        at = slice(s * tokens, (s + 1) * tokens)
        state = share[at] + single
        state_ref[at] = state
        normal_all[s] = normed(state).astype(BF)
    mine = meta[3]
    for k in range(samples):
        send_refs[k][...] = normal_all[lax.bitwise_xor(mine, k)]


def plane_kernel(meta, *rest, samples, tokens):
    parts, out_ref = rest[:samples], rest[samples]
    mine = meta[3]
    for k in range(samples):
        at = pl.multiple_of(lax.bitwise_xor(mine, k) * tokens, tokens)
        out_ref[pl.ds(at, tokens)] = parts[k][...]


def token_own_kernel(meta, normal, *rest, samples, tokens):
    biases, (w_qkv, q_ref, kv_ref, bias_ref, sems) = rest[:samples], rest[samples:]
    mine = meta[3]
    starts = [
        pl.multiple_of(lax.bitwise_xor(mine, k) * tokens, tokens) for k in range(samples)
    ]
    copies = fetch(
        [(biases[k], bias_ref.at[:, pl.ds(starts[k], tokens)]) for k in range(samples)], sems
    )
    width = normal.shape[-1]
    projected = dot(normal[...], w_qkv[...]).astype(BF)
    q_ref[...] = projected[:, :width]
    kv_ref[...] = projected[:, width:]
    for copy in copies:
        copy.wait()


def token_kernel(meta, q_own, kv_own, bias_all, *rest, samples, tokens, planes, heads):
    gathered, w_qkv, rest = rest[: planes - 1], rest[planes - 1], rest[planes:]
    send_refs, (kv_all, mixed_all) = rest[:samples], rest[samples:]
    rows = samples * tokens
    width = q_own.shape[-1]
    head_size = width // heads
    mine = meta[3]
    plane = meta[4]
    kv_all[pl.ds(pl.multiple_of(plane * rows, rows), rows)] = kv_own[...]
    others = jnp.concatenate([one[...] for one in gathered], 0)
    others = dot(others, w_qkv[:, width:]).astype(BF)
    for k in range(1, planes):
        origin = plane - k + jnp.where(plane < k, planes, 0)
        at = pl.multiple_of(origin * rows, rows)
        kv_all[pl.ds(at, rows)] = others[(k - 1) * rows : k * rows]
    scale = head_size ** (-0.5) * LOG2E
    mixed_all[...] = jnp.zeros_like(mixed_all)

    def lanes_of(h):
        start = h * head_size // 128 * 128
        stop = -(-(h + 1) * head_size // 128) * 128
        lane = lax.broadcasted_iota(jnp.int32, (rows, stop - start), 1) + start
        mask = ((lane >= h * head_size) & (lane < (h + 1) * head_size)).astype(F32)
        return slice(start, stop), mask

    def score(h, _):
        at, mask = lanes_of(h)
        query = q_own[:, at] * mask.astype(BF)
        return dot_nt(query, kv_all[:, at]) * scale + bias_all[h] * LOG2E

    def soften(h, scores):
        expo = jnp.exp2(scores - jnp.max(scores, -1, keepdims=True))
        attend = expo * (1.0 / jnp.sum(expo, -1, keepdims=True))
        upper = attend.astype(BF)
        return upper, (attend - upper.astype(F32)).astype(BF)

    def mix(h, attends):
        at, mask = lanes_of(h)
        values = kv_all[:, width + at.start : width + at.stop]
        mixed_all[:, at] += (dot(attends[0], values) + dot(attends[1], values)) * mask

    in_stages([score, soften, mix], range(heads))
    for k in range(samples):
        at = pl.multiple_of(lax.bitwise_xor(mine, k) * tokens, tokens)
        send_refs[k][...] = mixed_all[pl.ds(at, tokens)].astype(BF)


def token_out_kernel(meta, state, *rest, samples, tokens):
    parts, (w_out, w_back, out_ref, back_ref, mixed) = rest[:samples], rest[samples:]
    mine = meta[3]
    for k in range(samples):
        at = pl.multiple_of(lax.bitwise_xor(mine, k) * tokens, tokens)
        mixed[pl.ds(at, tokens)] = parts[k][...]
    after = state[...] + dot(mixed[...], w_out[...])
    for s in range(samples):
        out_ref[s] = after[s * tokens : (s + 1) * tokens]
    back_ref[...] = dot(normed(after).astype(BF), w_back[...]).astype(BF)


def unpool_kernel(
    meta, stream, atom_token, back, first, second, first_rim, second_rim, w_qkv,
    stream_ref, q_ref, kv_ref, first_ref, second_ref, padded, *, samples, rows, tokens,
):
    channels = stream.shape[-1]
    weight = w_qkv.at[ENC_LAYERS]
    selector = selector_of(meta, atom_token, tokens).astype(BF)
    first_at, second_at = halves(meta[0], 0, 2 * tokens)
    row = lax.broadcasted_iota(jnp.int32, (3 * tokens, RIM), 0).astype(F32)
    base = ((meta[2] - 1) * tokens).astype(F32)
    rims = [
        (rim, (row == rim[samples * RIM : samples * RIM + 1, :RIM] - base).astype(BF), out)
        for rim, out in ((first_rim, first_ref), (second_rim, second_ref))
    ]

    def pick(chosen, s):
        return lax.dot_general(
            chosen, padded[s], (((0,), (0,)), ((), ())), preferred_element_type=F32
        )

    def place(s, _):
        at = slice(s * tokens, (s + 1) * tokens)
        padded[s, tokens : 2 * tokens] = back[at]
        padded[s, pl.ds(first_at, tokens)] = first[at]
        padded[s, pl.ds(second_at, tokens)] = second[at]
        own = stream[s * rows : (s + 1) * rows] + pick(selector, s)
        stream_ref[s * rows : (s + 1) * rows] = own
        parts = [own]
        for rim, chosen, _ in rims:
            parts.append(rim[s * RIM : (s + 1) * RIM] + pick(chosen, s))
        return jnp.concatenate(parts, 0)

    def normalise(s, after):
        return normed(after).astype(BF)

    def project(s, normal):
        projected = dot(normal, weight[...])
        q_ref[s * rows : (s + 1) * rows] = projected[:rows, :channels].astype(BF)
        key_values = projected[:, channels:].astype(BF)
        kv_ref[s * rows : (s + 1) * rows] = key_values[:rows]
        for side, (_, _, out) in enumerate(rims):
            start = rows + side * RIM
            out[s * RIM : (s + 1) * RIM] = key_values[start : start + RIM]

    in_stages([place, normalise, project], range(samples))


def final_kernel(
    meta, q, kv, first, second, stream, bias, w_out, w_up, w_down, w_final,
    level_hbm, x_true, noise, state, denoised_ref, state_ref, padded, mixed, out, up, down, sems,
    level, late_sems, *, layer, samples, rows,
):
    copies = fetch(
        [(w_out.at[layer], out), (w_up.at[layer], up), (w_down.at[layer], down)], sems
    )
    late = fetch([(level_hbm, level), (state, state_ref)], late_sems)

    normal = run_block(
        meta, q, kv, first, second, stream, bias, (out, up, down), copies,
        samples, rows, padded, mixed, None,
    )
    late[0].wait()
    sigma, total = sigma_of(level, samples)
    keep = SIGMA_DATA * SIGMA_DATA / total
    move = sigma * SIGMA_DATA * lax.rsqrt(total)
    updates = [
        dot_nt(w_final[...], normal[s * rows : (s + 1) * rows]) for s in range(samples)
    ]
    for c in range(x_true.shape[0]):
        noisy = x_true[c : c + 1] + sigma * noise[c]
        update = jnp.concatenate([one[c : c + 1] for one in updates], 0)
        denoised_ref[c] = (keep * noisy + move * update) / SIGMA_DATA
    late[1].wait()


def swap(pair, count):
    first, second = pair
    groups = lax.axis_size("groups")
    lower = [(i, i ^ 1) for i in range(count)]
    upper = []
    for g in range(groups):
        inner = [(g * count + i, g * count + i + 1) for i in range(1, count - 1, 2)]
        upper += inner + [(j, i) for i, j in inner]
        for end in (0, count - 1):
            other = (g ^ 1) * count + end if groups % 2 == 0 else (g + 1) * count - 1 - end
            upper.append((g * count + end, other))
    second = lax.ppermute(second, ("groups",) + SEQ, upper)
    first = lax.ppermute(first, SEQ, lower)
    return first, second


def toward(array, k, count):
    return lax.ppermute(array, "p", [(i, i ^ k) for i in range(count)])


def across(arrays, count):
    return [toward(array, k, count) for k, array in enumerate(arrays, 1)]


def shards(
    x_true, noise, noise_level, atom_single, atom_token, window_edges, atom_pair_bias,
    token_single, pair_bias, w_coord, w_atom_qkv, w_atom_out, w_atom_up, w_atom_down,
    w_pool, w_token_qkv, w_token_out, w_back, w_final,
):
    samples = noise.shape[0]
    rows, channels = atom_single.shape
    tokens, width = token_single.shape
    heads = pair_bias.shape[0]
    planes = lax.axis_size("z")
    count = planes * samples
    mine = lax.axis_index("p")
    plane = lax.axis_index("z")
    device = plane * samples + mine
    meta = jnp.stack([device % 2, device * rows, device, mine, plane]).astype(jnp.int32)
    atom_token = atom_token[None, :]
    edges = window_edges.T
    noise = noise.transpose(1, 0, 2)
    whole = samples * rows
    held = samples * tokens
    rim = struct((samples * RIM, 2 * channels), BF)
    atom_outs = (
        struct((whole, channels), F32),
        struct((whole, channels), BF),
        struct((whole, 2 * channels), BF),
        rim,
        rim,
    )
    stacks = (w_atom_out, w_atom_up, w_atom_down)
    scratch = block_scratch(samples, rows, channels, stacks)
    wide = block_scratch(samples, rows, channels, stacks + (w_atom_qkv,))
    sizes = dict(samples=samples, rows=rows)

    def block(layer, q, kv, rims, stream):
        return call(
            functools.partial(block_kernel, layer=layer, **sizes), atom_outs,
            [SM] + [VM] * 6 + [HB] * 4,
            (meta, q, kv, *rims, stream, bias, *stacks, w_atom_qkv),
            wide,
        )

    stream, q, kv, *rims = call(
        functools.partial(embed_kernel, **sizes), atom_outs, [SM] + [HB] * 6,
        (meta, noise_level, x_true, noise, atom_single, w_coord, w_atom_qkv),
        [
            pltpu.SMEM(noise_level.shape, jnp.int32),
            pltpu.VMEM(x_true.shape, F32),
            pltpu.VMEM(noise.shape, F32),
            pltpu.VMEM(atom_single.shape, BF),
            pltpu.VMEM(w_coord.shape, F32),
            pltpu.VMEM(w_atom_qkv.shape[1:], BF),
            pltpu.SemaphoreType.DMA((6,)),
        ],
    )
    blocks, atom_heads, queries, window = atom_pair_bias.shape
    bias = call(
        mask_kernel, struct((blocks, atom_heads * queries, window), F32),
        [SM, SM, HB, VM], (meta, edges, atom_pair_bias, stream),
        [pltpu.VMEM(atom_pair_bias.shape, F32), pltpu.SemaphoreType.DMA((blocks,))],
    )
    for layer in range(ENC_LAYERS - 1):
        rims = swap(rims, count)
        if layer == 0:
            held_bias, _ = lax.optimization_barrier((pair_bias, stream))
            biases = [pair_bias]
            for k in (1, 2):
                biases.append(toward(held_bias, k, samples))
        stream, q, kv, *rims = block(layer, q, kv, rims, stream)
    rims = swap(rims, count)
    lanes = width + COUNT_LANES
    edge = struct((held, lanes), BF)
    stream_rim = struct((samples * RIM + 8, channels), F32)
    encoded, mid, first, second, *stream_rims = call(
        functools.partial(pool_kernel, layer=ENC_LAYERS - 1, tokens=tokens, **sizes),
        (atom_outs[0], struct((held + tokens, lanes), F32), edge, edge, stream_rim, stream_rim),
        [SM] + [VM] * 6 + [HB] * 6 + [VM] * 2,
        (
            meta, q, kv, *rims, stream, bias, *stacks, w_pool, atom_token, token_single,
            *biases[1:3],
        ),
        scratch
        + [
            pltpu.VMEM((samples, 3 * tokens, lanes), F32),
            pltpu.VMEM(w_pool.shape, BF),
            pltpu.VMEM(atom_token.shape, jnp.int32),
            pltpu.VMEM(token_single.shape, F32),
            pltpu.SemaphoreType.DMA((3,)),
        ],
    )
    passed, _ = lax.optimization_barrier((biases[2], mid))
    biases.append(toward(passed, 1, samples))
    rims = swap((first, second), count)
    piece = struct((tokens, width), BF)
    state, *sends = call(
        functools.partial(token_in_kernel, samples=samples, tokens=tokens),
        (struct((held, width), F32),) + (piece,) * samples,
        [SM] + [VM] * 3, (meta, mid, *rims),
        [pltpu.VMEM((samples, tokens, width), BF)],
    )
    got = across(sends[1:], samples)
    normal = call(
        functools.partial(plane_kernel, samples=samples, tokens=tokens),
        struct((held, width), BF), [SM] + [VM] * samples, (meta, sends[0], *got),
    )
    gathered = []
    for k in range(1, planes):
        shift = [(i, (i + k) % planes) for i in range(planes)]
        gathered.append(lax.ppermute(normal, "z", shift))
    stream_rims = swap(stream_rims, count)
    every = planes * held
    q_own, kv_own, bias_all = call(
        functools.partial(token_own_kernel, samples=samples, tokens=tokens),
        (
            struct((held, width), BF),
            struct((held, 2 * width), BF),
            struct((heads, held, every), F32),
        ),
        [SM, VM, HB] + [VM] * samples, (meta, normal, *biases, w_token_qkv),
        [pltpu.SemaphoreType.DMA((samples,))],
    )
    sends = call(
        functools.partial(
            token_kernel, samples=samples, tokens=tokens, planes=planes, heads=heads
        ),
        (piece,) * samples, [SM] + [VM] * (3 + planes),
        (meta, q_own, kv_own, bias_all, *gathered, w_token_qkv),
        [pltpu.VMEM((every, 2 * width), BF), pltpu.VMEM((held, width), F32)],
    )
    got = across(sends[1:], samples)
    after, back = call(
        functools.partial(token_out_kernel, samples=samples, tokens=tokens),
        (struct((samples, tokens, width), F32), struct((held, channels), BF)),
        [SM] + [VM] * (1 + samples + 2), (meta, state, sends[0], *got, w_token_out, w_back),
        [pltpu.VMEM((held, width), BF)],
    )
    backs = swap((back, back), count)
    stream, q, kv, *rims = call(
        functools.partial(unpool_kernel, tokens=tokens, **sizes), atom_outs,
        [SM] + [VM] * 8,
        (meta, encoded, atom_token, back, *backs, *stream_rims, w_atom_qkv),
        [pltpu.VMEM((samples, 3 * tokens, channels), BF)],
    )
    for layer in range(ENC_LAYERS, LAYERS - 1):
        if layer > ENC_LAYERS:
            rims = swap(rims, count)
        stream, q, kv, *rims = block(layer, q, kv, rims, stream)
    rims = swap(rims, count)
    denoised, token_state = call(
        functools.partial(final_kernel, layer=LAYERS - 1, **sizes),
        (struct(noise.shape, F32), struct((samples, tokens, width), F32)),
        [SM] + [VM] * 6 + [HB] * 3 + [VM, HB, VM, VM, VM],
        (
            meta, q, kv, *rims, stream, bias, *stacks, w_final, noise_level, x_true, noise,
            after,
        ),
        scratch
        + [
            pltpu.SMEM(noise_level.shape, jnp.int32),
            pltpu.SemaphoreType.DMA((2,)),
        ],
        (VM, HB),
    )
    return denoised.transpose(1, 0, 2), token_state


def solution(mesh):
    def step(*args):
        groups, seq = mesh.devices.shape
        samples = args[1].shape[0] // groups
        split = Mesh(
            mesh.devices.reshape(groups, seq // samples, samples), ("groups",) + SEQ
        )
        both = ("groups",) + SEQ
        in_specs = (
            P(None, both),
            P("groups", None, SEQ),
            P("groups"),
            P(both, None),
            P(both),
            P(both, None),
            P(both, None, None, None),
            P(both, None),
            P("groups", SEQ, None),
        ) + (P(),) * 10
        out_specs = (P("groups", None, SEQ), P("groups", SEQ, None))
        return jax.shard_map(
            shards, mesh=split, in_specs=in_specs, out_specs=out_specs, check_vma=False
        )(*args)

    return step
```

```python
import functools

import jax
import jax.numpy as jnp
from jax import lax
from jax.experimental import pallas as pl
from jax.experimental.pallas import tpu as pltpu
from jax.sharding import Mesh
from jax.sharding import PartitionSpec as P

QUERY_BLOCK = 32
KEY_WINDOW = 128
ENC_LAYERS = 2
LEVELS = 200
RIM = 48
LAYERS = 4

EPS = 1e-05
SIGMA_DATA = 16.0
BF = jnp.bfloat16
F32 = jnp.float32
SEQ = ("z", "p")
VM = pl.BlockSpec(memory_space=pltpu.VMEM)
SM = pl.BlockSpec(memory_space=pltpu.SMEM)
HB = pl.BlockSpec(memory_space=pltpu.HBM)
COUNT_LANES = 128
LOG2E = 1.4426950408889634


def normed(values):
    centre = jnp.mean(values, -1, keepdims=True)
    centred = values - centre
    spread = jnp.mean(centred * centred, -1, keepdims=True)
    return centred * lax.rsqrt(spread + EPS)


def dot(a, b):
    return jnp.dot(a, b, preferred_element_type=F32)


def dot_nt(a, b):
    return lax.dot_general(a, b, (((1,), (1,)), ((), ())), preferred_element_type=F32)


def noise_scale(noise_level):
    upper_root = 160.0 ** (1.0 / 7.0)
    lower_root = 0.0004 ** (1.0 / 7.0)
    fraction = noise_level.astype(F32) / (LEVELS - 1)
    root = upper_root + fraction * (lower_root - upper_root)
    square = root * root
    return SIGMA_DATA * (square * square * square * root)


def struct(shape, dtype):
    return jax.ShapeDtypeStruct(shape, dtype)


def call(kernel, out_shape, specs, args, scratch=(), out_specs=None):
    return pl.pallas_call(
        kernel,
        out_shape=out_shape,
        in_specs=specs,
        out_specs=out_specs or jax.tree.map(lambda _: VM, out_shape),
        scratch_shapes=scratch,
        compiler_params=pltpu.CompilerParams(vmem_limit_bytes=48 * 1024 * 1024),
    )(
        *[
            pltpu.with_memory_space_constraint(arg, pltpu.HBM) if spec is HB else arg
            for spec, arg in zip(specs, args)
        ]
    )


def halves(odd, lower, upper):
    first = jnp.where(odd == 0, upper, lower)
    second = jnp.where(odd == 0, lower, upper)
    return pl.multiple_of(first, 16), pl.multiple_of(second, 16)


def emit_rims(kv_ref, odd, samples, rows, first_ref, second_ref):
    for s in range(samples):
        first, second = halves(odd, s * rows, (s + 1) * rows - RIM)
        first_ref[s * RIM : (s + 1) * RIM] = kv_ref[pl.ds(first, RIM)]
        second_ref[s * RIM : (s + 1) * RIM] = kv_ref[pl.ds(second, RIM)]


def unit_rows(samples, rows):
    starts = [(b, s, s * rows + b * QUERY_BLOCK) for b in range(rows // QUERY_BLOCK) for s in range(samples)]
    return [(b, s, slice(at, at + QUERY_BLOCK)) for b, s, at in starts]


def in_stages(stages, units):
    held = [None] * len(units)
    for stage in stages:
        held = [stage(unit, before) for unit, before in zip(units, held)]


def fetch(pairs, sems):
    copies = [
        pltpu.make_async_copy(source, target, sems.at[i])
        for i, (source, target) in enumerate(pairs)
    ]
    for copy in copies:
        copy.start()
    return copies


def run_block(
    meta, q_ref, kv_ref, first_ref, second_ref, stream_ref, bias_ref, weights, layer,
    samples, rows, padded, mixed, out_ref,
):
    w_out, w_up, w_down = weights
    channels = q_ref.shape[-1]
    heads = bias_ref.shape[1] // QUERY_BLOCK
    head_size = channels // heads
    first, second = halves(meta[0], 0, RIM + rows)
    for s in range(samples):
        padded[s, RIM : RIM + rows] = kv_ref[s * rows : (s + 1) * rows]
        padded[s, pl.ds(first, RIM)] = first_ref[s * RIM : (s + 1) * RIM]
        padded[s, pl.ds(second, RIM)] = second_ref[s * RIM : (s + 1) * RIM]
    lane = lax.broadcasted_iota(jnp.int32, (QUERY_BLOCK, channels), 1)
    head_masks = [(lane // head_size == h).astype(F32) for h in range(heads)]
    head_bits = [m.astype(BF) for m in head_masks]
    head_masks = [jnp.concatenate([m, m], 1) for m in head_masks]
    scale = head_size ** (-0.5) * LOG2E
    ones = jnp.ones((KEY_WINDOW, channels), BF)

    units = unit_rows(samples, rows)

    def window(b):
        return slice(QUERY_BLOCK * b, QUERY_BLOCK * b + KEY_WINDOW)

    def score(unit, _):
        b, s, at = unit
        query = q_ref[at]
        spread = jnp.concatenate([query * bit for bit in head_bits], 0)
        return dot_nt(spread, padded[s, window(b), :channels]) * scale + bias_ref[b]

    def soften(_, scores):
        return jnp.exp2(scores - jnp.max(scores, -1, keepdims=True)).astype(BF)

    def mix(unit, expo):
        b, s, at = unit
        values = padded[s, window(b), channels:]
        out = dot(expo, jnp.concatenate([values, ones], 1))
        merged = out[:QUERY_BLOCK] * head_masks[0]
        for h in range(1, heads):
            merged += out[h * QUERY_BLOCK : (h + 1) * QUERY_BLOCK] * head_masks[h]
        mixed[at] = (merged[:, :channels] * (1.0 / merged[:, channels:])).astype(BF)

    in_stages([score, soften, mix], units)
    stream = stream_ref[...] + dot(mixed[...], w_out[layer])
    gated = dot(normed(stream).astype(BF), w_up[layer])
    half = gated.shape[-1] // 2
    gate = gated[:, :half]
    hidden = (gate * (1.0 / (1.0 + jnp.exp(-gate))) * gated[:, half:]).astype(BF)
    stream = stream + dot(hidden, w_down[layer])
    if out_ref is not None:
        out_ref[...] = stream
    return normed(stream).astype(BF)


def block_scratch(samples, rows, channels):
    return [
        pltpu.VMEM((samples, rows + 2 * RIM, 2 * channels), BF),
        pltpu.VMEM((samples * rows, channels), BF),
    ]


def embed_kernel(
    meta, level_hbm, x_true_hbm, noise_hbm, single_hbm, w_coord_hbm, w_qkv_hbm,
    stream_ref, q_ref, kv_ref, first_ref, second_ref,
    level, x_true, noise, single, w_coord, w_qkv, sems, *, samples, rows,
):
    copies = fetch(
        [
            (level_hbm, level),
            (x_true_hbm, x_true),
            (noise_hbm, noise),
            (single_hbm, single),
            (w_coord_hbm, w_coord),
            (w_qkv_hbm.at[0], w_qkv),
        ],
        sems,
    )
    channels = single.shape[-1]
    for copy in copies:
        copy.wait()
    sigma, total = sigma_of(level, samples)
    inverse = lax.rsqrt(total)
    base = single[...].astype(F32)
    scaled = [
        (x_true[c : c + 1] + sigma * noise[c]) * inverse for c in range(x_true.shape[0])
    ]

    def place(s, _):
        coords = jnp.concatenate([one[s : s + 1] for one in scaled], 0)
        return base + lax.dot_general(
            coords, w_coord[...], (((0,), (0,)), ((), ())),
            precision=lax.Precision.HIGHEST, preferred_element_type=F32,
        )

    def normalise(s, stream):
        stream_ref[s * rows : (s + 1) * rows] = stream
        return normed(stream).astype(BF)

    def project(s, normal):
        projected = dot(normal, w_qkv[...])
        q_ref[s * rows : (s + 1) * rows] = projected[:, :channels].astype(BF)
        kv_ref[s * rows : (s + 1) * rows] = projected[:, channels:].astype(BF)

    in_stages([place, normalise, project], range(samples))
    emit_rims(kv_ref, meta[0], samples, rows, first_ref, second_ref)


def prepare_kernel(meta, edges_hbm, bias_hbm, _, *rest):
    moved = (len(rest) - 4) // 2
    sources, out_ref, targets = rest[:moved], rest[moved], rest[moved + 1 : 2 * moved + 1]
    bias, edges, sems = rest[2 * moved + 1 :]
    blocks, heads, queries, window = bias.shape
    pieces = [(bias_hbm.at[b], bias.at[b]) for b in range(blocks)]
    copies = fetch(pieces + list(zip(sources, targets)) + [(edges_hbm, edges)], sems)
    copies.pop().wait()
    lane = lax.broadcasted_iota(jnp.int32, (heads * queries, window), 1)
    for b in range(blocks):
        position = meta[1] - RIM + QUERY_BLOCK * b + lane
        allowed = (position >= edges[0, b]) & (position < edges[1, b])
        copies[b].wait()
        values = bias[b].reshape(heads * queries, window) * LOG2E
        out_ref[b] = jnp.where(allowed, values, -jnp.inf)
    for copy in copies[blocks:]:
        copy.wait()


def sigma_of(level, samples):
    row = lax.broadcasted_iota(jnp.int32, (samples, 1), 0)
    levels = jnp.zeros((samples, 1), jnp.int32)
    for s in range(samples):
        levels = jnp.where(row == s, level[s], levels)
    sigma = noise_scale(levels)
    return sigma, sigma * sigma + SIGMA_DATA * SIGMA_DATA


def block_kernel(
    meta, q, kv, first, second, stream, bias, w_out, w_up, w_down, w_qkv,
    stream_ref, q_ref, kv_ref, first_ref, second_ref, padded, mixed, *, layer, samples, rows,
):
    channels = q.shape[-1]
    normal = run_block(
        meta, q, kv, first, second, stream, bias, (w_out, w_up, w_down), layer,
        samples, rows, padded, mixed, stream_ref,
    )
    projected = dot(normal, w_qkv[layer + 1]).astype(BF)
    q_ref[...] = projected[:, :channels]
    kv_ref[...] = projected[:, channels:]
    emit_rims(kv_ref, meta[0], samples, rows, first_ref, second_ref)


def selector_of(meta, atom_token, tokens):
    rows = atom_token.shape[-1]
    relative = atom_token[...] - (meta[2] - 1) * tokens
    row = lax.broadcasted_iota(jnp.int32, (3 * tokens, rows), 0)
    return (row == relative).astype(F32)


def pool_kernel(
    meta, q, kv, first, second, stream, bias, w_out, w_up, w_down, pooling, owners, single,
    *rest, layer, samples, rows, tokens,
):
    (stream_ref, mid_ref, first_ref, second_ref, first_rim, second_rim,
     padded, mixed, sums) = rest[-9:]
    normal = run_block(
        meta, q, kv, first, second, stream, bias, (w_out, w_up, w_down), layer,
        samples, rows, padded, mixed, stream_ref,
    )
    selector = selector_of(meta, owners, tokens)
    counts = jnp.sum(selector, -1, keepdims=True)
    selector = selector.astype(BF)
    width = pooling.shape[-1]

    def pool(s, _):
        return jnp.maximum(dot(normal[s * rows : (s + 1) * rows], pooling[...]), 0.0)

    def gather(s, pooled):
        upper = pooled.astype(BF)
        lower = (pooled - upper.astype(F32)).astype(BF)
        sums[s, :, :width] = dot(selector, upper) + dot(selector, lower)
        sums[s, :, width:] = jnp.broadcast_to(counts, (3 * tokens, COUNT_LANES))

    in_stages([pool, gather], range(samples))
    ends = [owners[:, :RIM], owners[:, rows - RIM :]]
    for at, side in ((first_rim, 0), (second_rim, 1)):
        for s in range(samples):
            start = halves(meta[0], s * rows, (s + 1) * rows - RIM)[side]
            at[s * RIM : (s + 1) * RIM] = stream_ref[pl.ds(start, RIM)]
        named = jnp.where(meta[0] == side, ends[1], ends[0]).astype(F32)
        at[samples * RIM :] = jnp.zeros((8, at.shape[-1]), F32)
        at[samples * RIM : samples * RIM + 1, :RIM] = named
    mid_ref[samples * tokens :, :width] = single[...]
    mid_ref[samples * tokens :, width:] = jnp.zeros((tokens, COUNT_LANES), F32)
    for s in range(samples):
        at = slice(s * tokens, (s + 1) * tokens)
        mid_ref[at] = sums[s, tokens : 2 * tokens]
        first_at, second_at = halves(meta[0], 0, 2 * tokens)
        first_ref[at] = sums[s, pl.ds(first_at, tokens)].astype(BF)
        second_ref[at] = sums[s, pl.ds(second_at, tokens)].astype(BF)


def token_in_kernel(
    meta, mid, first, second, state_ref, *rest, samples, tokens
):
    send_refs, normal_all = rest[:samples], rest[samples]
    width = state_ref.shape[-1]
    held = samples * tokens
    single = mid[held:, :width]
    total = mid[:held] + first[...].astype(F32) + second[...].astype(F32)
    share = total[:, :width] / total[:, width : width + 1]
    for s in range(samples):
        at = slice(s * tokens, (s + 1) * tokens)
        state = share[at] + single
        state_ref[at] = state
        normal_all[s] = normed(state).astype(BF)
    mine = meta[3]
    for k in range(samples):
        send_refs[k][...] = normal_all[lax.bitwise_xor(mine, k)]


def plane_kernel(meta, *rest, samples, tokens):
    parts, out_ref = rest[:samples], rest[samples]
    mine = meta[3]
    for k in range(samples):
        at = pl.multiple_of(lax.bitwise_xor(mine, k) * tokens, tokens)
        out_ref[pl.ds(at, tokens)] = parts[k][...]


def token_own_kernel(meta, normal, *rest, samples, tokens):
    biases, (w_qkv, q_ref, kv_ref, bias_ref, sems) = rest[:samples], rest[samples:]
    mine = meta[3]
    starts = [
        pl.multiple_of(lax.bitwise_xor(mine, k) * tokens, tokens) for k in range(samples)
    ]
    copies = fetch(
        [(biases[k], bias_ref.at[:, pl.ds(starts[k], tokens)]) for k in range(samples)], sems
    )
    width = normal.shape[-1]
    projected = dot(normal[...], w_qkv[...]).astype(BF)
    q_ref[...] = projected[:, :width]
    kv_ref[...] = projected[:, width:]
    for copy in copies:
        copy.wait()


def token_kernel(meta, q_own, kv_own, bias_all, *rest, samples, tokens, planes, heads):
    gathered, w_qkv, rest = rest[: planes - 1], rest[planes - 1], rest[planes:]
    send_refs, (kv_all, mixed_all) = rest[:samples], rest[samples:]
    rows = samples * tokens
    width = q_own.shape[-1]
    head_size = width // heads
    mine = meta[3]
    plane = meta[4]
    kv_all[pl.ds(pl.multiple_of(plane * rows, rows), rows)] = kv_own[...]
    others = jnp.concatenate([one[...] for one in gathered], 0)
    others = dot(others, w_qkv[:, width:]).astype(BF)
    for k in range(1, planes):
        origin = plane - k + jnp.where(plane < k, planes, 0)
        at = pl.multiple_of(origin * rows, rows)
        kv_all[pl.ds(at, rows)] = others[(k - 1) * rows : k * rows]
    scale = head_size ** (-0.5) * LOG2E
    mixed_all[...] = jnp.zeros_like(mixed_all)

    def lanes_of(h):
        start = h * head_size // 128 * 128
        stop = -(-(h + 1) * head_size // 128) * 128
        lane = lax.broadcasted_iota(jnp.int32, (rows, stop - start), 1) + start
        mask = ((lane >= h * head_size) & (lane < (h + 1) * head_size)).astype(F32)
        return slice(start, stop), mask

    def score(h, _):
        at, mask = lanes_of(h)
        query = q_own[:, at] * mask.astype(BF)
        return dot_nt(query, kv_all[:, at]) * scale + bias_all[h] * LOG2E

    def soften(h, scores):
        expo = jnp.exp2(scores - jnp.max(scores, -1, keepdims=True))
        attend = expo * (1.0 / jnp.sum(expo, -1, keepdims=True))
        upper = attend.astype(BF)
        return upper, (attend - upper.astype(F32)).astype(BF)

    def mix(h, attends):
        at, mask = lanes_of(h)
        values = kv_all[:, width + at.start : width + at.stop]
        mixed_all[:, at] += (dot(attends[0], values) + dot(attends[1], values)) * mask

    in_stages([score, soften, mix], range(heads))
    for k in range(samples):
        at = pl.multiple_of(lax.bitwise_xor(mine, k) * tokens, tokens)
        send_refs[k][...] = mixed_all[pl.ds(at, tokens)].astype(BF)


def token_out_kernel(meta, state, *rest, samples, tokens):
    parts, (w_out, w_back, out_ref, back_ref, mixed) = rest[:samples], rest[samples:]
    mine = meta[3]
    for k in range(samples):
        at = pl.multiple_of(lax.bitwise_xor(mine, k) * tokens, tokens)
        mixed[pl.ds(at, tokens)] = parts[k][...]
    after = state[...] + dot(mixed[...], w_out[...])
    for s in range(samples):
        out_ref[s] = after[s * tokens : (s + 1) * tokens]
    back_ref[...] = dot(normed(after).astype(BF), w_back[...]).astype(BF)


def unpool_kernel(
    meta, stream, atom_token, back, first, second, first_rim, second_rim, w_qkv,
    stream_ref, q_ref, kv_ref, first_ref, second_ref, padded, *, samples, rows, tokens,
):
    channels = stream.shape[-1]
    weight = w_qkv.at[ENC_LAYERS]
    selector = selector_of(meta, atom_token, tokens).astype(BF)
    first_at, second_at = halves(meta[0], 0, 2 * tokens)
    row = lax.broadcasted_iota(jnp.int32, (3 * tokens, RIM), 0).astype(F32)
    base = ((meta[2] - 1) * tokens).astype(F32)
    rims = [
        (rim, (row == rim[samples * RIM : samples * RIM + 1, :RIM] - base).astype(BF), out)
        for rim, out in ((first_rim, first_ref), (second_rim, second_ref))
    ]

    def pick(chosen, s):
        return lax.dot_general(
            chosen, padded[s], (((0,), (0,)), ((), ())), preferred_element_type=F32
        )

    def place(s, _):
        at = slice(s * tokens, (s + 1) * tokens)
        padded[s, tokens : 2 * tokens] = back[at]
        padded[s, pl.ds(first_at, tokens)] = first[at]
        padded[s, pl.ds(second_at, tokens)] = second[at]
        own = stream[s * rows : (s + 1) * rows] + pick(selector, s)
        stream_ref[s * rows : (s + 1) * rows] = own
        parts = [own]
        for rim, chosen, _ in rims:
            parts.append(rim[s * RIM : (s + 1) * RIM] + pick(chosen, s))
        return jnp.concatenate(parts, 0)

    def normalise(s, after):
        return normed(after).astype(BF)

    def project(s, normal):
        projected = dot(normal, weight[...])
        q_ref[s * rows : (s + 1) * rows] = projected[:rows, :channels].astype(BF)
        key_values = projected[:, channels:].astype(BF)
        kv_ref[s * rows : (s + 1) * rows] = key_values[:rows]
        for side, (_, _, out) in enumerate(rims):
            start = rows + side * RIM
            out[s * RIM : (s + 1) * RIM] = key_values[start : start + RIM]

    in_stages([place, normalise, project], range(samples))


def final_kernel(
    meta, q, kv, first, second, stream, bias, w_out, w_up, w_down, w_final,
    level_hbm, x_true, noise, state, denoised_ref, state_ref, padded, mixed,
    level, late_sems, *, layer, samples, rows,
):
    late = fetch([(level_hbm, level), (state, state_ref)], late_sems)

    normal = run_block(
        meta, q, kv, first, second, stream, bias, (w_out, w_up, w_down), layer,
        samples, rows, padded, mixed, None,
    )
    late[0].wait()
    sigma, total = sigma_of(level, samples)
    keep = SIGMA_DATA * SIGMA_DATA / total
    move = sigma * SIGMA_DATA * lax.rsqrt(total)
    updates = [
        dot_nt(w_final[...], normal[s * rows : (s + 1) * rows]) for s in range(samples)
    ]
    for c in range(x_true.shape[0]):
        noisy = x_true[c : c + 1] + sigma * noise[c]
        update = jnp.concatenate([one[c : c + 1] for one in updates], 0)
        denoised_ref[c] = (keep * noisy + move * update) / SIGMA_DATA
    late[1].wait()


def swap(pair, count):
    first, second = pair
    groups = lax.axis_size("groups")
    lower = [(i, i ^ 1) for i in range(count)]
    upper = []
    for g in range(groups):
        inner = [(g * count + i, g * count + i + 1) for i in range(1, count - 1, 2)]
        upper += inner + [(j, i) for i, j in inner]
        for end in (0, count - 1):
            other = (g ^ 1) * count + end if groups % 2 == 0 else (g + 1) * count - 1 - end
            upper.append((g * count + end, other))
    second = lax.ppermute(second, ("groups",) + SEQ, upper)
    first = lax.ppermute(first, SEQ, lower)
    return first, second


def toward(array, k, count):
    return lax.ppermute(array, "p", [(i, i ^ k) for i in range(count)])


def across(arrays, count):
    return [toward(array, k, count) for k, array in enumerate(arrays, 1)]


def shards(
    x_true, noise, noise_level, atom_single, atom_token, window_edges, atom_pair_bias,
    token_single, pair_bias, w_coord, w_atom_qkv, w_atom_out, w_atom_up, w_atom_down,
    w_pool, w_token_qkv, w_token_out, w_back, w_final,
):
    samples = noise.shape[0]
    rows, channels = atom_single.shape
    tokens, width = token_single.shape
    heads = pair_bias.shape[0]
    planes = lax.axis_size("z")
    count = planes * samples
    mine = lax.axis_index("p")
    plane = lax.axis_index("z")
    device = plane * samples + mine
    meta = jnp.stack([device % 2, device * rows, device, mine, plane]).astype(jnp.int32)
    atom_token = atom_token[None, :]
    edges = window_edges.T
    noise = noise.transpose(1, 0, 2)
    whole = samples * rows
    held = samples * tokens
    rim = struct((samples * RIM, 2 * channels), BF)
    atom_outs = (
        struct((whole, channels), F32),
        struct((whole, channels), BF),
        struct((whole, 2 * channels), BF),
        rim,
        rim,
    )
    stacks = (w_atom_out, w_atom_up, w_atom_down)
    scratch = block_scratch(samples, rows, channels)
    sizes = dict(samples=samples, rows=rows)

    stream, q, kv, *rims = call(
        functools.partial(embed_kernel, **sizes), atom_outs, [SM] + [HB] * 6,
        (meta, noise_level, x_true, noise, atom_single, w_coord, w_atom_qkv),
        [
            pltpu.SMEM(noise_level.shape, jnp.int32),
            pltpu.VMEM(x_true.shape, F32),
            pltpu.VMEM(noise.shape, F32),
            pltpu.VMEM(atom_single.shape, BF),
            pltpu.VMEM(w_coord.shape, F32),
            pltpu.VMEM(w_atom_qkv.shape[1:], BF),
            pltpu.SemaphoreType.DMA((6,)),
        ],
    )
    blocks, atom_heads, queries, window = atom_pair_bias.shape
    moved = (*stacks, w_atom_qkv, w_pool, atom_token, token_single)
    bias, *stacks, w_atom_qkv, w_pool, atom_token, token_single = call(
        prepare_kernel,
        (struct((blocks, atom_heads * queries, window), F32),)
        + tuple(struct(array.shape, array.dtype) for array in moved),
        [SM, HB, HB, VM] + [HB] * len(moved), (meta, edges, atom_pair_bias, stream, *moved),
        [
            pltpu.VMEM(atom_pair_bias.shape, F32),
            pltpu.SMEM(edges.shape, jnp.int32),
            pltpu.SemaphoreType.DMA((blocks + len(moved) + 1,)),
        ],
    )

    def block(layer, q, kv, rims, stream):
        return call(
            functools.partial(block_kernel, layer=layer, **sizes), atom_outs,
            [SM] + [VM] * 10,
            (meta, q, kv, *rims, stream, bias, *stacks, w_atom_qkv),
            scratch,
        )

    for layer in range(ENC_LAYERS - 1):
        rims = swap(rims, count)
        if layer == 0:
            held_bias, _ = lax.optimization_barrier((pair_bias, stream))
            biases = [pair_bias]
            for k in (1, 2):
                biases.append(toward(held_bias, k, samples))
        stream, q, kv, *rims = block(layer, q, kv, rims, stream)
    rims = swap(rims, count)
    lanes = width + COUNT_LANES
    edge = struct((held, lanes), BF)
    stream_rim = struct((samples * RIM + 8, channels), F32)
    encoded, mid, first, second, *stream_rims = call(
        functools.partial(pool_kernel, layer=ENC_LAYERS - 1, tokens=tokens, **sizes),
        (atom_outs[0], struct((held + tokens, lanes), F32), edge, edge, stream_rim, stream_rim),
        [SM] + [VM] * 14,
        (
            meta, q, kv, *rims, stream, bias, *stacks, w_pool, atom_token, token_single,
            *biases[1:3],
        ),
        scratch + [pltpu.VMEM((samples, 3 * tokens, lanes), F32)],
    )
    passed, _ = lax.optimization_barrier((biases[2], mid))
    biases.append(toward(passed, 1, samples))
    rims = swap((first, second), count)
    piece = struct((tokens, width), BF)
    state, *sends = call(
        functools.partial(token_in_kernel, samples=samples, tokens=tokens),
        (struct((held, width), F32),) + (piece,) * samples,
        [SM] + [VM] * 3, (meta, mid, *rims),
        [pltpu.VMEM((samples, tokens, width), BF)],
    )
    got = across(sends[1:], samples)
    normal = call(
        functools.partial(plane_kernel, samples=samples, tokens=tokens),
        struct((held, width), BF), [SM] + [VM] * samples, (meta, sends[0], *got),
    )
    gathered = []
    for k in range(1, planes):
        shift = [(i, (i + k) % planes) for i in range(planes)]
        gathered.append(lax.ppermute(normal, "z", shift))
    stream_rims = swap(stream_rims, count)
    every = planes * held
    q_own, kv_own, bias_all = call(
        functools.partial(token_own_kernel, samples=samples, tokens=tokens),
        (
            struct((held, width), BF),
            struct((held, 2 * width), BF),
            struct((heads, held, every), F32),
        ),
        [SM, VM, HB] + [VM] * samples, (meta, normal, *biases, w_token_qkv),
        [pltpu.SemaphoreType.DMA((samples,))],
    )
    sends = call(
        functools.partial(
            token_kernel, samples=samples, tokens=tokens, planes=planes, heads=heads
        ),
        (piece,) * samples, [SM] + [VM] * (3 + planes),
        (meta, q_own, kv_own, bias_all, *gathered, w_token_qkv),
        [pltpu.VMEM((every, 2 * width), BF), pltpu.VMEM((held, width), F32)],
    )
    got = across(sends[1:], samples)
    after, back = call(
        functools.partial(token_out_kernel, samples=samples, tokens=tokens),
        (struct((samples, tokens, width), F32), struct((held, channels), BF)),
        [SM] + [VM] * (1 + samples + 2), (meta, state, sends[0], *got, w_token_out, w_back),
        [pltpu.VMEM((held, width), BF)],
    )
    backs = swap((back, back), count)
    stream, q, kv, *rims = call(
        functools.partial(unpool_kernel, tokens=tokens, **sizes), atom_outs,
        [SM] + [VM] * 8,
        (meta, encoded, atom_token, back, *backs, *stream_rims, w_atom_qkv),
        [pltpu.VMEM((samples, 3 * tokens, channels), BF)],
    )
    for layer in range(ENC_LAYERS, LAYERS - 1):
        if layer > ENC_LAYERS:
            rims = swap(rims, count)
        stream, q, kv, *rims = block(layer, q, kv, rims, stream)
    rims = swap(rims, count)
    denoised, token_state = call(
        functools.partial(final_kernel, layer=LAYERS - 1, **sizes),
        (struct(noise.shape, F32), struct((samples, tokens, width), F32)),
        [SM] + [VM] * 10 + [HB, VM, VM, VM],
        (
            meta, q, kv, *rims, stream, bias, *stacks, w_final, noise_level, x_true, noise,
            after,
        ),
        scratch
        + [
            pltpu.SMEM(noise_level.shape, jnp.int32),
            pltpu.SemaphoreType.DMA((2,)),
        ],
        (VM, HB),
    )
    return denoised.transpose(1, 0, 2), token_state


def solution(mesh):
    def step(*args):
        groups, seq = mesh.devices.shape
        samples = args[1].shape[0] // groups
        split = Mesh(
            mesh.devices.reshape(groups, seq // samples, samples), ("groups",) + SEQ
        )
        both = ("groups",) + SEQ
        in_specs = (
            P(None, both),
            P("groups", None, SEQ),
            P("groups"),
            P(both, None),
            P(both),
            P(both, None),
            P(both, None, None, None),
            P(both, None),
            P("groups", SEQ, None),
        ) + (P(),) * 10
        out_specs = (P("groups", None, SEQ), P("groups", SEQ, None))
        return jax.shard_map(
            shards, mesh=split, in_specs=in_specs, out_specs=out_specs, check_vma=False
        )(*args)

    return step
```

```python
import functools

import jax
import jax.numpy as jnp
from jax import lax
from jax.experimental import pallas as pl
from jax.experimental.pallas import tpu as pltpu
from jax.sharding import Mesh
from jax.sharding import PartitionSpec as P

QUERY_BLOCK = 32
KEY_WINDOW = 128
ENC_LAYERS = 2
LEVELS = 200
RIM = 48
LAYERS = 4

EPS = 1e-05
SIGMA_DATA = 16.0
BF = jnp.bfloat16
F32 = jnp.float32
SEQ = ("z", "p")
VM = pl.BlockSpec(memory_space=pltpu.VMEM)
HB = pl.BlockSpec(memory_space=pltpu.HBM)
COUNT_LANES = 128
LOG2E = 1.4426950408889634


def normed(values):
    centre = jnp.mean(values, -1, keepdims=True)
    centred = values - centre
    spread = jnp.mean(centred * centred, -1, keepdims=True)
    return centred * lax.rsqrt(spread + EPS)


def dot(a, b):
    return jnp.dot(a, b, preferred_element_type=F32)


def dot_nt(a, b):
    return lax.dot_general(a, b, (((1,), (1,)), ((), ())), preferred_element_type=F32)


def noise_scale(noise_level):
    upper_root = 160.0 ** (1.0 / 7.0)
    lower_root = 0.0004 ** (1.0 / 7.0)
    fraction = noise_level.astype(F32) / (LEVELS - 1)
    root = upper_root + fraction * (lower_root - upper_root)
    square = root * root
    return SIGMA_DATA * (square * square * square * root)


def struct(shape, dtype):
    return jax.ShapeDtypeStruct(shape, dtype)


def places():
    mine = lax.axis_index("p")
    plane = lax.axis_index("z")
    device = plane * lax.axis_size("p") + mine
    return lax.rem(device, 2), device, mine, plane


def call(kernel, out_shape, specs, args, scratch=(), out_specs=None):
    def body(*refs):
        kernel(places(), *refs)

    return pl.pallas_call(
        body,
        out_shape=out_shape,
        in_specs=specs,
        out_specs=out_specs or jax.tree.map(lambda _: VM, out_shape),
        scratch_shapes=scratch,
        compiler_params=pltpu.CompilerParams(vmem_limit_bytes=48 * 1024 * 1024),
    )(
        *[
            pltpu.with_memory_space_constraint(arg, pltpu.HBM) if spec is HB else arg
            for spec, arg in zip(specs, args)
        ]
    )


def halves(odd, lower, upper):
    first = jnp.where(odd == 0, upper, lower)
    second = jnp.where(odd == 0, lower, upper)
    return pl.multiple_of(first, 16), pl.multiple_of(second, 16)


def emit_rims(kv_ref, odd, samples, rows, first_ref, second_ref):
    for s in range(samples):
        first, second = halves(odd, s * rows, (s + 1) * rows - RIM)
        first_ref[s * RIM : (s + 1) * RIM] = kv_ref[pl.ds(first, RIM)]
        second_ref[s * RIM : (s + 1) * RIM] = kv_ref[pl.ds(second, RIM)]


def unit_rows(samples, rows):
    starts = [(b, s, s * rows + b * QUERY_BLOCK) for b in range(rows // QUERY_BLOCK) for s in range(samples)]
    return [(b, s, slice(at, at + QUERY_BLOCK)) for b, s, at in starts]


def in_stages(stages, units):
    held = [None] * len(units)
    for stage in stages:
        held = [stage(unit, before) for unit, before in zip(units, held)]


def fetch(pairs, sems):
    copies = [
        pltpu.make_async_copy(source, target, sems.at[i])
        for i, (source, target) in enumerate(pairs)
    ]
    for copy in copies:
        copy.start()
    return copies


def run_block(
    meta, q_ref, kv_ref, first_ref, second_ref, stream_ref, bias_ref, weights, layer,
    samples, rows, padded, mixed, out_ref,
):
    w_out, w_up, w_down = weights
    channels = q_ref.shape[-1]
    heads = bias_ref.shape[1] // QUERY_BLOCK
    head_size = channels // heads
    first, second = halves(meta[0], 0, RIM + rows)
    for s in range(samples):
        padded[s, RIM : RIM + rows] = kv_ref[s * rows : (s + 1) * rows]
        padded[s, pl.ds(first, RIM)] = first_ref[s * RIM : (s + 1) * RIM]
        padded[s, pl.ds(second, RIM)] = second_ref[s * RIM : (s + 1) * RIM]
    lane = lax.broadcasted_iota(jnp.int32, (QUERY_BLOCK, channels), 1)
    head_masks = [(lane // head_size == h).astype(F32) for h in range(heads)]
    head_bits = [m.astype(BF) for m in head_masks]
    head_masks = [jnp.concatenate([m, m], 1) for m in head_masks]
    scale = head_size ** (-0.5) * LOG2E
    ones = jnp.ones((KEY_WINDOW, channels), BF)

    units = unit_rows(samples, rows)

    def window(b):
        return slice(QUERY_BLOCK * b, QUERY_BLOCK * b + KEY_WINDOW)

    def score(unit, _):
        b, s, at = unit
        query = q_ref[at]
        spread = jnp.concatenate([query * bit for bit in head_bits], 0)
        return dot_nt(spread, padded[s, window(b), :channels]) * scale + bias_ref[b]

    def soften(_, scores):
        return jnp.exp2(scores - jnp.max(scores, -1, keepdims=True)).astype(BF)

    def mix(unit, expo):
        b, s, at = unit
        values = padded[s, window(b), channels:]
        out = dot(expo, jnp.concatenate([values, ones], 1))
        merged = out[:QUERY_BLOCK] * head_masks[0]
        for h in range(1, heads):
            merged += out[h * QUERY_BLOCK : (h + 1) * QUERY_BLOCK] * head_masks[h]
        mixed[at] = (merged[:, :channels] * (1.0 / merged[:, channels:])).astype(BF)

    in_stages([score, soften, mix], units)
    stream = stream_ref[...] + dot(mixed[...], w_out[layer])
    gated = dot(normed(stream).astype(BF), w_up[layer])
    half = gated.shape[-1] // 2
    gate = gated[:, :half]
    hidden = (gate * (1.0 / (1.0 + jnp.exp(-gate))) * gated[:, half:]).astype(BF)
    stream = stream + dot(hidden, w_down[layer])
    if out_ref is not None:
        out_ref[...] = stream
    return normed(stream).astype(BF)


def block_scratch(samples, rows, channels):
    return [
        pltpu.VMEM((samples, rows + 2 * RIM, 2 * channels), BF),
        pltpu.VMEM((samples * rows, channels), BF),
    ]


def embed_kernel(
    meta, level_hbm, x_true_hbm, noise_hbm, single_hbm, w_coord_hbm, w_qkv_hbm,
    stream_ref, q_ref, kv_ref, first_ref, second_ref,
    level, x_true, noise, single, w_coord, w_qkv, sems, *, samples, rows,
):
    copies = fetch(
        [
            (level_hbm, level),
            (x_true_hbm, x_true),
            (noise_hbm, noise),
            (single_hbm, single),
            (w_coord_hbm, w_coord),
            (w_qkv_hbm.at[0], w_qkv),
        ],
        sems,
    )
    channels = single.shape[-1]
    for copy in copies:
        copy.wait()
    sigma, total = sigma_of(level, samples)
    inverse = lax.rsqrt(total)
    base = single[...].astype(F32)
    scaled = [
        (x_true[c : c + 1] + sigma * noise[c]) * inverse for c in range(x_true.shape[0])
    ]

    def place(s, _):
        coords = jnp.concatenate([one[s : s + 1] for one in scaled], 0)
        return base + lax.dot_general(
            coords, w_coord[...], (((0,), (0,)), ((), ())),
            precision=lax.Precision.HIGHEST, preferred_element_type=F32,
        )

    def normalise(s, stream):
        stream_ref[s * rows : (s + 1) * rows] = stream
        return normed(stream).astype(BF)

    def project(s, normal):
        projected = dot(normal, w_qkv[...])
        q_ref[s * rows : (s + 1) * rows] = projected[:, :channels].astype(BF)
        kv_ref[s * rows : (s + 1) * rows] = projected[:, channels:].astype(BF)

    in_stages([place, normalise, project], range(samples))
    emit_rims(kv_ref, meta[0], samples, rows, first_ref, second_ref)


def prepare_kernel(meta, edges_hbm, bias_hbm, _, *rest):
    moved = (len(rest) - 4) // 2
    sources, out_ref, targets = rest[:moved], rest[moved], rest[moved + 1 : 2 * moved + 1]
    bias, edges, sems = rest[2 * moved + 1 :]
    blocks, heads, queries, window = bias.shape
    pieces = [(bias_hbm.at[b], bias.at[b]) for b in range(blocks)]
    copies = fetch(pieces + list(zip(sources, targets)) + [(edges_hbm, edges)], sems)
    copies.pop().wait()
    lane = lax.broadcasted_iota(jnp.int32, (heads * queries, window), 1)
    for b in range(blocks):
        position = meta[1] * (blocks * QUERY_BLOCK) - RIM + QUERY_BLOCK * b + lane
        allowed = (position >= edges[0, b]) & (position < edges[1, b])
        copies[b].wait()
        values = bias[b].reshape(heads * queries, window) * LOG2E
        out_ref[b] = jnp.where(allowed, values, -jnp.inf)
    for copy in copies[blocks:]:
        copy.wait()


def sigma_of(level, samples):
    row = lax.broadcasted_iota(jnp.int32, (samples, 1), 0)
    levels = jnp.zeros((samples, 1), jnp.int32)
    for s in range(samples):
        levels = jnp.where(row == s, level[s], levels)
    sigma = noise_scale(levels)
    return sigma, sigma * sigma + SIGMA_DATA * SIGMA_DATA


def block_kernel(
    meta, q, kv, first, second, stream, bias, w_out, w_up, w_down, w_qkv,
    stream_ref, q_ref, kv_ref, first_ref, second_ref, padded, mixed, *, layer, samples, rows,
):
    channels = q.shape[-1]
    normal = run_block(
        meta, q, kv, first, second, stream, bias, (w_out, w_up, w_down), layer,
        samples, rows, padded, mixed, stream_ref,
    )
    projected = dot(normal, w_qkv[layer + 1]).astype(BF)
    q_ref[...] = projected[:, :channels]
    kv_ref[...] = projected[:, channels:]
    emit_rims(kv_ref, meta[0], samples, rows, first_ref, second_ref)


def selector_of(meta, atom_token, tokens):
    rows = atom_token.shape[-1]
    relative = atom_token[...] - (meta[1] - 1) * tokens
    row = lax.broadcasted_iota(jnp.int32, (3 * tokens, rows), 0)
    return (row == relative).astype(F32)


def pool_kernel(
    meta, q, kv, first, second, stream, bias, w_out, w_up, w_down, pooling, owners, single,
    *rest, layer, samples, rows, tokens,
):
    (stream_ref, mid_ref, first_ref, second_ref, first_rim, second_rim,
     padded, mixed, sums) = rest[-9:]
    normal = run_block(
        meta, q, kv, first, second, stream, bias, (w_out, w_up, w_down), layer,
        samples, rows, padded, mixed, stream_ref,
    )
    selector = selector_of(meta, owners, tokens)
    counts = jnp.sum(selector, -1, keepdims=True)
    selector = selector.astype(BF)
    width = pooling.shape[-1]

    def pool(s, _):
        return jnp.maximum(dot(normal[s * rows : (s + 1) * rows], pooling[...]), 0.0)

    def gather(s, pooled):
        upper = pooled.astype(BF)
        lower = (pooled - upper.astype(F32)).astype(BF)
        sums[s, :, :width] = dot(selector, upper) + dot(selector, lower)
        sums[s, :, width:] = jnp.broadcast_to(counts, (3 * tokens, COUNT_LANES))

    in_stages([pool, gather], range(samples))
    ends = [owners[:, :RIM], owners[:, rows - RIM :]]
    for at, side in ((first_rim, 0), (second_rim, 1)):
        for s in range(samples):
            start = halves(meta[0], s * rows, (s + 1) * rows - RIM)[side]
            at[s * RIM : (s + 1) * RIM] = stream_ref[pl.ds(start, RIM)]
        named = jnp.where(meta[0] == side, ends[1], ends[0]).astype(F32)
        at[samples * RIM :] = jnp.zeros((8, at.shape[-1]), F32)
        at[samples * RIM : samples * RIM + 1, :RIM] = named
    mid_ref[samples * tokens :, :width] = single[...]
    mid_ref[samples * tokens :, width:] = jnp.zeros((tokens, COUNT_LANES), F32)
    for s in range(samples):
        at = slice(s * tokens, (s + 1) * tokens)
        mid_ref[at] = sums[s, tokens : 2 * tokens]
        first_at, second_at = halves(meta[0], 0, 2 * tokens)
        first_ref[at] = sums[s, pl.ds(first_at, tokens)].astype(BF)
        second_ref[at] = sums[s, pl.ds(second_at, tokens)].astype(BF)


def token_in_kernel(
    meta, mid, first, second, state_ref, *rest, samples, tokens
):
    send_refs, normal_all = rest[:samples], rest[samples]
    width = state_ref.shape[-1]
    held = samples * tokens
    single = mid[held:, :width]
    total = mid[:held] + first[...].astype(F32) + second[...].astype(F32)
    share = total[:, :width] / total[:, width : width + 1]
    for s in range(samples):
        at = slice(s * tokens, (s + 1) * tokens)
        state = share[at] + single
        state_ref[at] = state
        normal_all[s] = normed(state).astype(BF)
    mine = meta[2]
    for k in range(samples):
        send_refs[k][...] = normal_all[lax.bitwise_xor(mine, k)]


def plane_kernel(meta, *rest, samples, tokens):
    parts, out_ref = rest[:samples], rest[samples]
    mine = meta[2]
    for k in range(samples):
        at = pl.multiple_of(lax.bitwise_xor(mine, k) * tokens, tokens)
        out_ref[pl.ds(at, tokens)] = parts[k][...]


def token_own_kernel(meta, normal, *rest, samples, tokens):
    biases, (w_qkv, q_ref, kv_ref, bias_ref, sems) = rest[:samples], rest[samples:]
    mine = meta[2]
    starts = [
        pl.multiple_of(lax.bitwise_xor(mine, k) * tokens, tokens) for k in range(samples)
    ]
    copies = fetch(
        [(biases[k], bias_ref.at[:, pl.ds(starts[k], tokens)]) for k in range(samples)], sems
    )
    width = normal.shape[-1]
    projected = dot(normal[...], w_qkv[...]).astype(BF)
    q_ref[...] = projected[:, :width]
    kv_ref[...] = projected[:, width:]
    for copy in copies:
        copy.wait()


def token_kernel(meta, q_own, kv_own, bias_all, *rest, samples, tokens, planes, heads):
    gathered, w_qkv, rest = rest[: planes - 1], rest[planes - 1], rest[planes:]
    send_refs, (kv_all, mixed_all) = rest[:samples], rest[samples:]
    rows = samples * tokens
    width = q_own.shape[-1]
    head_size = width // heads
    mine = meta[2]
    plane = meta[3]
    kv_all[pl.ds(pl.multiple_of(plane * rows, rows), rows)] = kv_own[...]
    others = jnp.concatenate([one[...] for one in gathered], 0)
    others = dot(others, w_qkv[:, width:]).astype(BF)
    for k in range(1, planes):
        origin = plane - k + jnp.where(plane < k, planes, 0)
        at = pl.multiple_of(origin * rows, rows)
        kv_all[pl.ds(at, rows)] = others[(k - 1) * rows : k * rows]
    scale = head_size ** (-0.5) * LOG2E
    mixed_all[...] = jnp.zeros_like(mixed_all)

    def lanes_of(h):
        start = h * head_size // 128 * 128
        stop = -(-(h + 1) * head_size // 128) * 128
        lane = lax.broadcasted_iota(jnp.int32, (rows, stop - start), 1) + start
        mask = ((lane >= h * head_size) & (lane < (h + 1) * head_size)).astype(F32)
        return slice(start, stop), mask

    def score(h, _):
        at, mask = lanes_of(h)
        query = q_own[:, at] * mask.astype(BF)
        return dot_nt(query, kv_all[:, at]) * scale + bias_all[h] * LOG2E

    def soften(h, scores):
        expo = jnp.exp2(scores - jnp.max(scores, -1, keepdims=True))
        attend = expo * (1.0 / jnp.sum(expo, -1, keepdims=True))
        upper = attend.astype(BF)
        return upper, (attend - upper.astype(F32)).astype(BF)

    def mix(h, attends):
        at, mask = lanes_of(h)
        values = kv_all[:, width + at.start : width + at.stop]
        mixed_all[:, at] += (dot(attends[0], values) + dot(attends[1], values)) * mask

    in_stages([score, soften, mix], range(heads))
    for k in range(samples):
        at = pl.multiple_of(lax.bitwise_xor(mine, k) * tokens, tokens)
        send_refs[k][...] = mixed_all[pl.ds(at, tokens)].astype(BF)


def token_out_kernel(meta, state, *rest, samples, tokens):
    parts, (w_out, w_back, out_ref, back_ref, mixed) = rest[:samples], rest[samples:]
    mine = meta[2]
    for k in range(samples):
        at = pl.multiple_of(lax.bitwise_xor(mine, k) * tokens, tokens)
        mixed[pl.ds(at, tokens)] = parts[k][...]
    after = state[...] + dot(mixed[...], w_out[...])
    for s in range(samples):
        out_ref[s] = after[s * tokens : (s + 1) * tokens]
    back_ref[...] = dot(normed(after).astype(BF), w_back[...]).astype(BF)


def unpool_kernel(
    meta, stream, atom_token, back, first, second, first_rim, second_rim, w_qkv,
    stream_ref, q_ref, kv_ref, first_ref, second_ref, padded, *, samples, rows, tokens,
):
    channels = stream.shape[-1]
    weight = w_qkv.at[ENC_LAYERS]
    selector = selector_of(meta, atom_token, tokens).astype(BF)
    first_at, second_at = halves(meta[0], 0, 2 * tokens)
    row = lax.broadcasted_iota(jnp.int32, (3 * tokens, RIM), 0).astype(F32)
    base = ((meta[1] - 1) * tokens).astype(F32)
    rims = [
        (rim, (row == rim[samples * RIM : samples * RIM + 1, :RIM] - base).astype(BF), out)
        for rim, out in ((first_rim, first_ref), (second_rim, second_ref))
    ]

    def pick(chosen, s):
        return lax.dot_general(
            chosen, padded[s], (((0,), (0,)), ((), ())), preferred_element_type=F32
        )

    def place(s, _):
        at = slice(s * tokens, (s + 1) * tokens)
        padded[s, tokens : 2 * tokens] = back[at]
        padded[s, pl.ds(first_at, tokens)] = first[at]
        padded[s, pl.ds(second_at, tokens)] = second[at]
        own = stream[s * rows : (s + 1) * rows] + pick(selector, s)
        stream_ref[s * rows : (s + 1) * rows] = own
        parts = [own]
        for rim, chosen, _ in rims:
            parts.append(rim[s * RIM : (s + 1) * RIM] + pick(chosen, s))
        return jnp.concatenate(parts, 0)

    def normalise(s, after):
        return normed(after).astype(BF)

    def project(s, normal):
        projected = dot(normal, weight[...])
        q_ref[s * rows : (s + 1) * rows] = projected[:rows, :channels].astype(BF)
        key_values = projected[:, channels:].astype(BF)
        kv_ref[s * rows : (s + 1) * rows] = key_values[:rows]
        for side, (_, _, out) in enumerate(rims):
            start = rows + side * RIM
            out[s * RIM : (s + 1) * RIM] = key_values[start : start + RIM]

    in_stages([place, normalise, project], range(samples))


def final_kernel(
    meta, q, kv, first, second, stream, bias, w_out, w_up, w_down, w_final,
    level_hbm, x_true, noise, state, denoised_ref, state_ref, padded, mixed,
    level, late_sems, *, layer, samples, rows,
):
    late = fetch([(level_hbm, level), (state, state_ref)], late_sems)

    normal = run_block(
        meta, q, kv, first, second, stream, bias, (w_out, w_up, w_down), layer,
        samples, rows, padded, mixed, None,
    )
    late[0].wait()
    sigma, total = sigma_of(level, samples)
    keep = SIGMA_DATA * SIGMA_DATA / total
    move = sigma * SIGMA_DATA * lax.rsqrt(total)
    updates = [
        dot_nt(w_final[...], normal[s * rows : (s + 1) * rows]) for s in range(samples)
    ]
    for c in range(x_true.shape[0]):
        noisy = x_true[c : c + 1] + sigma * noise[c]
        update = jnp.concatenate([one[c : c + 1] for one in updates], 0)
        denoised_ref[c] = (keep * noisy + move * update) / SIGMA_DATA
    late[1].wait()


def swap(pair, count):
    first, second = pair
    groups = lax.axis_size("groups")
    lower = [(i, i ^ 1) for i in range(count)]
    upper = []
    for g in range(groups):
        inner = [(g * count + i, g * count + i + 1) for i in range(1, count - 1, 2)]
        upper += inner + [(j, i) for i, j in inner]
        for end in (0, count - 1):
            other = (g ^ 1) * count + end if groups % 2 == 0 else (g + 1) * count - 1 - end
            upper.append((g * count + end, other))
    second = lax.ppermute(second, ("groups",) + SEQ, upper)
    first = lax.ppermute(first, SEQ, lower)
    return first, second


def toward(array, k, count):
    return lax.ppermute(array, "p", [(i, i ^ k) for i in range(count)])


def across(arrays, count):
    return [toward(array, k, count) for k, array in enumerate(arrays, 1)]


def shards(
    x_true, noise, noise_level, atom_single, atom_token, window_edges, atom_pair_bias,
    token_single, pair_bias, w_coord, w_atom_qkv, w_atom_out, w_atom_up, w_atom_down,
    w_pool, w_token_qkv, w_token_out, w_back, w_final,
):
    samples = noise.shape[0]
    rows, channels = atom_single.shape
    tokens, width = token_single.shape
    heads = pair_bias.shape[0]
    planes = lax.axis_size("z")
    count = planes * samples
    atom_token = atom_token[None, :]
    edges = window_edges.T
    noise = noise.transpose(1, 0, 2)
    whole = samples * rows
    held = samples * tokens
    rim = struct((samples * RIM, 2 * channels), BF)
    atom_outs = (
        struct((whole, channels), F32),
        struct((whole, channels), BF),
        struct((whole, 2 * channels), BF),
        rim,
        rim,
    )
    stacks = (w_atom_out, w_atom_up, w_atom_down)
    scratch = block_scratch(samples, rows, channels)
    sizes = dict(samples=samples, rows=rows)

    stream, q, kv, *rims = call(
        functools.partial(embed_kernel, **sizes), atom_outs, [HB] * 6,
        (noise_level, x_true, noise, atom_single, w_coord, w_atom_qkv),
        [
            pltpu.SMEM(noise_level.shape, jnp.int32),
            pltpu.VMEM(x_true.shape, F32),
            pltpu.VMEM(noise.shape, F32),
            pltpu.VMEM(atom_single.shape, BF),
            pltpu.VMEM(w_coord.shape, F32),
            pltpu.VMEM(w_atom_qkv.shape[1:], BF),
            pltpu.SemaphoreType.DMA((6,)),
        ],
    )
    blocks, atom_heads, queries, window = atom_pair_bias.shape
    moved = (*stacks, w_atom_qkv, w_pool, atom_token, token_single)
    bias, *stacks, w_atom_qkv, w_pool, atom_token, token_single = call(
        prepare_kernel,
        (struct((blocks, atom_heads * queries, window), F32),)
        + tuple(struct(array.shape, array.dtype) for array in moved),
        [HB, HB, VM] + [HB] * len(moved), (edges, atom_pair_bias, stream, *moved),
        [
            pltpu.VMEM(atom_pair_bias.shape, F32),
            pltpu.SMEM(edges.shape, jnp.int32),
            pltpu.SemaphoreType.DMA((blocks + len(moved) + 1,)),
        ],
    )

    def block(layer, q, kv, rims, stream):
        return call(
            functools.partial(block_kernel, layer=layer, **sizes), atom_outs,
            [VM] * 10,
            (q, kv, *rims, stream, bias, *stacks, w_atom_qkv),
            scratch,
        )

    for layer in range(ENC_LAYERS - 1):
        rims = swap(rims, count)
        if layer == 0:
            held_bias, _ = lax.optimization_barrier((pair_bias, stream))
            biases = [pair_bias]
            for k in (1, 2):
                biases.append(toward(held_bias, k, samples))
        stream, q, kv, *rims = block(layer, q, kv, rims, stream)
    rims = swap(rims, count)
    lanes = width + COUNT_LANES
    edge = struct((held, lanes), BF)
    stream_rim = struct((samples * RIM + 8, channels), F32)
    encoded, mid, first, second, *stream_rims = call(
        functools.partial(pool_kernel, layer=ENC_LAYERS - 1, tokens=tokens, **sizes),
        (atom_outs[0], struct((held + tokens, lanes), F32), edge, edge, stream_rim, stream_rim),
        [VM] * 14,
        (
            q, kv, *rims, stream, bias, *stacks, w_pool, atom_token, token_single,
            *biases[1:3],
        ),
        scratch + [pltpu.VMEM((samples, 3 * tokens, lanes), F32)],
    )
    passed, _ = lax.optimization_barrier((biases[2], mid))
    biases.append(toward(passed, 1, samples))
    rims = swap((first, second), count)
    piece = struct((tokens, width), BF)
    state, *sends = call(
        functools.partial(token_in_kernel, samples=samples, tokens=tokens),
        (struct((held, width), F32),) + (piece,) * samples,
        [VM] * 3, (mid, *rims),
        [pltpu.VMEM((samples, tokens, width), BF)],
    )
    got = across(sends[1:], samples)
    normal = call(
        functools.partial(plane_kernel, samples=samples, tokens=tokens),
        struct((held, width), BF), [VM] * samples, (sends[0], *got),
    )
    gathered = []
    for k in range(1, planes):
        shift = [(i, (i + k) % planes) for i in range(planes)]
        gathered.append(lax.ppermute(normal, "z", shift))
    stream_rims = swap(stream_rims, count)
    every = planes * held
    q_own, kv_own, bias_all = call(
        functools.partial(token_own_kernel, samples=samples, tokens=tokens),
        (
            struct((held, width), BF),
            struct((held, 2 * width), BF),
            struct((heads, held, every), F32),
        ),
        [VM, HB] + [VM] * samples, (normal, *biases, w_token_qkv),
        [pltpu.SemaphoreType.DMA((samples,))],
    )
    sends = call(
        functools.partial(
            token_kernel, samples=samples, tokens=tokens, planes=planes, heads=heads
        ),
        (piece,) * samples, [VM] * (3 + planes),
        (q_own, kv_own, bias_all, *gathered, w_token_qkv),
        [pltpu.VMEM((every, 2 * width), BF), pltpu.VMEM((held, width), F32)],
    )
    got = across(sends[1:], samples)
    after, back = call(
        functools.partial(token_out_kernel, samples=samples, tokens=tokens),
        (struct((samples, tokens, width), F32), struct((held, channels), BF)),
        [VM] * (1 + samples + 2), (state, sends[0], *got, w_token_out, w_back),
        [pltpu.VMEM((held, width), BF)],
    )
    backs = swap((back, back), count)
    stream, q, kv, *rims = call(
        functools.partial(unpool_kernel, tokens=tokens, **sizes), atom_outs,
        [VM] * 8,
        (encoded, atom_token, back, *backs, *stream_rims, w_atom_qkv),
        [pltpu.VMEM((samples, 3 * tokens, channels), BF)],
    )
    for layer in range(ENC_LAYERS, LAYERS - 1):
        if layer > ENC_LAYERS:
            rims = swap(rims, count)
        stream, q, kv, *rims = block(layer, q, kv, rims, stream)
    rims = swap(rims, count)
    denoised, token_state = call(
        functools.partial(final_kernel, layer=LAYERS - 1, **sizes),
        (struct(noise.shape, F32), struct((samples, tokens, width), F32)),
        [VM] * 10 + [HB, VM, VM, VM],
        (
            q, kv, *rims, stream, bias, *stacks, w_final, noise_level, x_true, noise,
            after,
        ),
        scratch
        + [
            pltpu.SMEM(noise_level.shape, jnp.int32),
            pltpu.SemaphoreType.DMA((2,)),
        ],
        (VM, HB),
    )
    return denoised.transpose(1, 0, 2), token_state


def solution(mesh):
    def step(*args):
        groups, seq = mesh.devices.shape
        samples = args[1].shape[0] // groups
        split = Mesh(
            mesh.devices.reshape(groups, seq // samples, samples), ("groups",) + SEQ
        )
        both = ("groups",) + SEQ
        in_specs = (
            P(None, both),
            P("groups", None, SEQ),
            P("groups"),
            P(both, None),
            P(both),
            P(both, None),
            P(both, None, None, None),
            P(both, None),
            P("groups", SEQ, None),
        ) + (P(),) * 10
        out_specs = (P("groups", None, SEQ), P("groups", SEQ, None))
        return jax.shard_map(
            shards, mesh=split, in_specs=in_specs, out_specs=out_specs, check_vma=False
        )(*args)

    return step
```

```python
import functools

import jax
import jax.numpy as jnp
from jax import lax
from jax.experimental import pallas as pl
from jax.experimental.pallas import tpu as pltpu
from jax.sharding import Mesh
from jax.sharding import PartitionSpec as P


QUERY_BLOCK = 32
KEY_WINDOW = 128
ENC_LAYERS = 2
LEVELS = 200
RIM = 48
LAYERS = 4

EPS = 1e-05
SIGMA_DATA = 16.0
BF = jnp.bfloat16
F32 = jnp.float32
SEQ = ("z", "p")
VM = pl.BlockSpec(memory_space=pltpu.VMEM)
HB = pl.BlockSpec(memory_space=pltpu.HBM)
COUNT_LANES = 128
LOG2E = 1.4426950408889634


def normed(values):
    centre = jnp.mean(values, -1, keepdims=True)
    centred = values - centre
    spread = jnp.mean(centred * centred, -1, keepdims=True)
    return centred * lax.rsqrt(spread + EPS)


def dot(a, b):
    return jnp.dot(a, b, preferred_element_type=F32)


def dot_nt(a, b):
    return lax.dot_general(a, b, (((1,), (1,)), ((), ())), preferred_element_type=F32)


def noise_scale(noise_level):
    upper_root = 160.0 ** (1.0 / 7.0)
    lower_root = 0.0004 ** (1.0 / 7.0)
    fraction = noise_level.astype(F32) / (LEVELS - 1)
    root = upper_root + fraction * (lower_root - upper_root)
    square = root * root
    return SIGMA_DATA * (square * square * square * root)


def struct(shape, dtype):
    return jax.ShapeDtypeStruct(shape, dtype)


def places():
    mine = lax.axis_index("p")
    plane = lax.axis_index("z")
    device = plane * lax.axis_size("p") + mine
    return lax.rem(device, 2), device, mine, plane


def call(kernel, out_shape, specs, args, scratch=(), out_specs=None):
    def body(*refs):
        kernel(places(), *refs)

    return pl.pallas_call(
        body,
        out_shape=out_shape,
        in_specs=specs,
        out_specs=out_specs or jax.tree.map(lambda _: VM, out_shape),
        scratch_shapes=scratch,
        compiler_params=pltpu.CompilerParams(vmem_limit_bytes=48 * 1024 * 1024),
    )(
        *[
            pltpu.with_memory_space_constraint(arg, pltpu.HBM) if spec is HB else arg
            for spec, arg in zip(specs, args)
        ]
    )


def halves(odd, lower, upper):
    first = jnp.where(odd == 0, upper, lower)
    second = jnp.where(odd == 0, lower, upper)
    return pl.multiple_of(first, 16), pl.multiple_of(second, 16)


def emit_rims(kv_ref, odd, samples, rows, first_ref, second_ref):
    for s in range(samples):
        first, second = halves(odd, s * rows, (s + 1) * rows - RIM)
        first_ref[s * RIM : (s + 1) * RIM] = kv_ref[pl.ds(first, RIM)]
        second_ref[s * RIM : (s + 1) * RIM] = kv_ref[pl.ds(second, RIM)]


def unit_rows(samples, rows):
    starts = [(b, s, s * rows + b * QUERY_BLOCK) for b in range(rows // QUERY_BLOCK) for s in range(samples)]
    return [(b, s, slice(at, at + QUERY_BLOCK)) for b, s, at in starts]


def in_stages(stages, units):
    held = [None] * len(units)
    for stage in stages:
        held = [stage(unit, before) for unit, before in zip(units, held)]


def fetch(pairs, sems):
    copies = [
        pltpu.make_async_copy(source, target, sems.at[i])
        for i, (source, target) in enumerate(pairs)
    ]
    for copy in copies:
        copy.start()
    return copies


def run_block(
    meta, q_ref, kv_ref, first_ref, second_ref, stream_ref, bias_ref, weights, layer,
    samples, rows, padded, mixed, out_ref,
):
    w_out, w_up, w_down = weights
    channels = q_ref.shape[-1]
    heads = bias_ref.shape[1] // QUERY_BLOCK
    head_size = channels // heads
    first, second = halves(meta[0], 0, RIM + rows)
    for s in range(samples):
        padded[s, RIM : RIM + rows] = kv_ref[s * rows : (s + 1) * rows]
        padded[s, pl.ds(first, RIM)] = first_ref[s * RIM : (s + 1) * RIM]
        padded[s, pl.ds(second, RIM)] = second_ref[s * RIM : (s + 1) * RIM]
    lane = lax.broadcasted_iota(jnp.int32, (QUERY_BLOCK, channels), 1)
    head_masks = [(lane // head_size == h).astype(F32) for h in range(heads)]
    head_bits = [m.astype(BF) for m in head_masks]
    head_masks = [jnp.concatenate([m, m], 1) for m in head_masks]
    scale = head_size ** (-0.5) * LOG2E
    ones = jnp.ones((KEY_WINDOW, channels), BF)

    units = unit_rows(samples, rows)

    def window(b):
        return slice(QUERY_BLOCK * b, QUERY_BLOCK * b + KEY_WINDOW)

    def score(unit, _):
        b, s, at = unit
        query = q_ref[at]
        spread = jnp.concatenate([query * bit for bit in head_bits], 0)
        return dot_nt(spread, padded[s, window(b), :channels]) * scale + bias_ref[b]

    def soften(_, scores):
        return jnp.exp2(scores - jnp.max(scores, -1, keepdims=True)).astype(BF)

    def mix(unit, expo):
        b, s, at = unit
        values = padded[s, window(b), channels:]
        out = dot(expo, jnp.concatenate([values, ones], 1))
        merged = out[:QUERY_BLOCK] * head_masks[0]
        for h in range(1, heads):
            merged += out[h * QUERY_BLOCK : (h + 1) * QUERY_BLOCK] * head_masks[h]
        mixed[at] = (merged[:, :channels] * (1.0 / merged[:, channels:])).astype(BF)

    in_stages([score, soften, mix], units)
    stream = stream_ref[...] + dot(mixed[...], w_out[layer])
    gated = dot(normed(stream).astype(BF), w_up[layer])
    half = gated.shape[-1] // 2
    gate = gated[:, :half]
    hidden = (gate * (1.0 / (1.0 + jnp.exp(-gate))) * gated[:, half:]).astype(BF)
    stream = stream + dot(hidden, w_down[layer])
    if out_ref is not None:
        out_ref[...] = stream
    return normed(stream).astype(BF)


def block_scratch(samples, rows, channels):
    return [
        pltpu.VMEM((samples, rows + 2 * RIM, 2 * channels), BF),
        pltpu.VMEM((samples * rows, channels), BF),
    ]


def embed_kernel(
    meta, level_hbm, x_true_hbm, noise_hbm, single_hbm, w_coord_hbm, w_qkv_hbm,
    stream_ref, q_ref, kv_ref, first_ref, second_ref,
    level, x_true, noise, single, w_coord, w_qkv, sems, *, samples, rows,
):
    copies = fetch(
        [
            (level_hbm, level),
            (x_true_hbm, x_true),
            (noise_hbm, noise),
            (single_hbm, single),
            (w_coord_hbm, w_coord),
            (w_qkv_hbm.at[0], w_qkv),
        ],
        sems,
    )
    channels = single.shape[-1]
    for copy in copies:
        copy.wait()
    sigma, total = sigma_of(level, samples)
    inverse = lax.rsqrt(total)
    base = single[...].astype(F32)
    scaled = [
        (x_true[c : c + 1] + sigma * noise[c]) * inverse for c in range(x_true.shape[0])
    ]

    def place(s, _):
        coords = jnp.concatenate([one[s : s + 1] for one in scaled], 0)
        return base + lax.dot_general(
            coords, w_coord[...], (((0,), (0,)), ((), ())),
            precision=lax.Precision.HIGHEST, preferred_element_type=F32,
        )

    def normalise(s, stream):
        stream_ref[s * rows : (s + 1) * rows] = stream
        return normed(stream).astype(BF)

    def project(s, normal):
        projected = dot(normal, w_qkv[...])
        q_ref[s * rows : (s + 1) * rows] = projected[:, :channels].astype(BF)
        kv_ref[s * rows : (s + 1) * rows] = projected[:, channels:].astype(BF)

    in_stages([place, normalise, project], range(samples))
    emit_rims(kv_ref, meta[0], samples, rows, first_ref, second_ref)


def prepare_kernel(meta, edges_hbm, bias_hbm, _, *rest):
    moved = (len(rest) - 4) // 2
    sources, out_ref, targets = rest[:moved], rest[moved], rest[moved + 1 : 2 * moved + 1]
    bias, edges, sems = rest[2 * moved + 1 :]
    blocks, heads, queries, window = bias.shape
    pieces = [(bias_hbm.at[b], bias.at[b]) for b in range(blocks)]
    copies = fetch(pieces + list(zip(sources, targets)) + [(edges_hbm, edges)], sems)
    copies.pop().wait()
    lane = lax.broadcasted_iota(jnp.int32, (heads * queries, window), 1)
    for b in range(blocks):
        position = meta[1] * (blocks * QUERY_BLOCK) - RIM + QUERY_BLOCK * b + lane
        allowed = (position >= edges[0, b]) & (position < edges[1, b])
        copies[b].wait()
        values = bias[b].reshape(heads * queries, window) * LOG2E
        out_ref[b] = jnp.where(allowed, values, -jnp.inf)
    for copy in copies[blocks:]:
        copy.wait()


def sigma_of(level, samples):
    row = lax.broadcasted_iota(jnp.int32, (samples, 1), 0)
    levels = jnp.zeros((samples, 1), jnp.int32)
    for s in range(samples):
        levels = jnp.where(row == s, level[s], levels)
    sigma = noise_scale(levels)
    return sigma, sigma * sigma + SIGMA_DATA * SIGMA_DATA


def block_kernel(
    meta, q, kv, first, second, stream, bias, w_out, w_up, w_down, w_qkv,
    stream_ref, q_ref, kv_ref, first_ref, second_ref, padded, mixed, *, layer, samples, rows,
):
    channels = q.shape[-1]
    normal = run_block(
        meta, q, kv, first, second, stream, bias, (w_out, w_up, w_down), layer,
        samples, rows, padded, mixed, stream_ref,
    )
    projected = dot(normal, w_qkv[layer + 1]).astype(BF)
    q_ref[...] = projected[:, :channels]
    kv_ref[...] = projected[:, channels:]
    emit_rims(kv_ref, meta[0], samples, rows, first_ref, second_ref)


def selector_of(meta, atom_token, tokens):
    rows = atom_token.shape[-1]
    relative = atom_token[...] - (meta[1] - 1) * tokens
    row = lax.broadcasted_iota(jnp.int32, (3 * tokens, rows), 0)
    return (row == relative).astype(F32)


def pool_kernel(
    meta, q, kv, first, second, stream, bias, w_out, w_up, w_down, pooling, owners, single,
    *rest, layer, samples, rows, tokens,
):
    (stream_ref, mid_ref, first_ref, second_ref, first_rim, second_rim,
     padded, mixed, sums) = rest[-9:]
    normal = run_block(
        meta, q, kv, first, second, stream, bias, (w_out, w_up, w_down), layer,
        samples, rows, padded, mixed, stream_ref,
    )
    selector = selector_of(meta, owners, tokens)
    counts = jnp.sum(selector, -1, keepdims=True)
    selector = selector.astype(BF)
    width = pooling.shape[-1]

    def pool(s, _):
        return jnp.maximum(dot(normal[s * rows : (s + 1) * rows], pooling[...]), 0.0)

    def gather(s, pooled):
        upper = pooled.astype(BF)
        lower = (pooled - upper.astype(F32)).astype(BF)
        sums[s, :, :width] = dot(selector, upper) + dot(selector, lower)
        sums[s, :, width:] = jnp.broadcast_to(counts, (3 * tokens, COUNT_LANES))

    in_stages([pool, gather], range(samples))
    ends = [owners[:, :RIM], owners[:, rows - RIM :]]
    for at, side in ((first_rim, 0), (second_rim, 1)):
        for s in range(samples):
            start = halves(meta[0], s * rows, (s + 1) * rows - RIM)[side]
            at[s * RIM : (s + 1) * RIM] = stream_ref[pl.ds(start, RIM)]
        named = jnp.where(meta[0] == side, ends[1], ends[0]).astype(F32)
        at[samples * RIM :] = jnp.zeros((8, at.shape[-1]), F32)
        at[samples * RIM : samples * RIM + 1, :RIM] = named
    mid_ref[samples * tokens :, :width] = single[...]
    mid_ref[samples * tokens :, width:] = jnp.zeros((tokens, COUNT_LANES), F32)
    for s in range(samples):
        at = slice(s * tokens, (s + 1) * tokens)
        mid_ref[at] = sums[s, tokens : 2 * tokens]
        first_at, second_at = halves(meta[0], 0, 2 * tokens)
        first_ref[at] = sums[s, pl.ds(first_at, tokens)].astype(BF)
        second_ref[at] = sums[s, pl.ds(second_at, tokens)].astype(BF)


def token_in_kernel(
    meta, mid, first, second, state_ref, *rest, samples, tokens
):
    send_refs, normal_all = rest[:samples], rest[samples]
    width = state_ref.shape[-1]
    held = samples * tokens
    single = mid[held:, :width]
    total = mid[:held] + first[...].astype(F32) + second[...].astype(F32)
    share = total[:, :width] / total[:, width : width + 1]
    for s in range(samples):
        at = slice(s * tokens, (s + 1) * tokens)
        state = share[at] + single
        state_ref[at] = state
        normal_all[s] = normed(state).astype(BF)
    mine = meta[2]
    for k in range(samples):
        send_refs[k][...] = normal_all[lax.bitwise_xor(mine, k)]


def plane_kernel(meta, *rest, samples, tokens):
    parts, out_ref = rest[:samples], rest[samples]
    mine = meta[2]
    for k in range(samples):
        at = pl.multiple_of(lax.bitwise_xor(mine, k) * tokens, tokens)
        out_ref[pl.ds(at, tokens)] = parts[k][...]


def token_own_kernel(meta, normal, *rest, samples, tokens):
    biases, (w_qkv, q_ref, kv_ref, bias_ref, sems) = rest[:samples], rest[samples:]
    mine = meta[2]
    starts = [
        pl.multiple_of(lax.bitwise_xor(mine, k) * tokens, tokens) for k in range(samples)
    ]
    copies = fetch(
        [(biases[k], bias_ref.at[:, pl.ds(starts[k], tokens)]) for k in range(samples)], sems
    )
    width = normal.shape[-1]
    projected = dot(normal[...], w_qkv[...]).astype(BF)
    q_ref[...] = projected[:, :width]
    kv_ref[...] = projected[:, width:]
    for copy in copies:
        copy.wait()


def token_kernel(meta, q_own, kv_own, bias_all, *rest, samples, tokens, planes, heads):
    gathered, w_qkv, rest = rest[: planes - 1], rest[planes - 1], rest[planes:]
    send_refs, (kv_all, mixed_all) = rest[:samples], rest[samples:]
    rows = samples * tokens
    width = q_own.shape[-1]
    head_size = width // heads
    mine = meta[2]
    plane = meta[3]
    kv_all[pl.ds(pl.multiple_of(plane * rows, rows), rows)] = kv_own[...]
    others = jnp.concatenate([one[...] for one in gathered], 0)
    others = dot(others, w_qkv[:, width:]).astype(BF)
    for k in range(1, planes):
        origin = plane - k + jnp.where(plane < k, planes, 0)
        at = pl.multiple_of(origin * rows, rows)
        kv_all[pl.ds(at, rows)] = others[(k - 1) * rows : k * rows]
    scale = head_size ** (-0.5) * LOG2E
    mixed_all[...] = jnp.zeros_like(mixed_all)

    def lanes_of(h):
        start = h * head_size // 128 * 128
        stop = -(-(h + 1) * head_size // 128) * 128
        lane = lax.broadcasted_iota(jnp.int32, (rows, stop - start), 1) + start
        mask = ((lane >= h * head_size) & (lane < (h + 1) * head_size)).astype(F32)
        return slice(start, stop), mask

    def score(h, _):
        at, mask = lanes_of(h)
        query = q_own[:, at] * mask.astype(BF)
        return dot_nt(query, kv_all[:, at]) * scale + bias_all[h] * LOG2E

    def soften(h, scores):
        expo = jnp.exp2(scores - jnp.max(scores, -1, keepdims=True))
        attend = expo * (1.0 / jnp.sum(expo, -1, keepdims=True))
        upper = attend.astype(BF)
        return upper, (attend - upper.astype(F32)).astype(BF)

    def mix(h, attends):
        at, mask = lanes_of(h)
        values = kv_all[:, width + at.start : width + at.stop]
        mixed_all[:, at] += (dot(attends[0], values) + dot(attends[1], values)) * mask

    in_stages([score, soften, mix], range(heads))
    for k in range(samples):
        at = pl.multiple_of(lax.bitwise_xor(mine, k) * tokens, tokens)
        send_refs[k][...] = mixed_all[pl.ds(at, tokens)].astype(BF)


def token_out_kernel(meta, state, *rest, samples, tokens):
    parts, (w_out, w_back, out_ref, back_ref, mixed) = rest[:samples], rest[samples:]
    mine = meta[2]
    for k in range(samples):
        at = pl.multiple_of(lax.bitwise_xor(mine, k) * tokens, tokens)
        mixed[pl.ds(at, tokens)] = parts[k][...]
    after = state[...] + dot(mixed[...], w_out[...])
    for s in range(samples):
        out_ref[s] = after[s * tokens : (s + 1) * tokens]
    back_ref[...] = dot(normed(after).astype(BF), w_back[...]).astype(BF)


def unpool_kernel(
    meta, stream, atom_token, back, first, second, first_rim, second_rim, w_qkv,
    stream_ref, q_ref, kv_ref, first_ref, second_ref, padded, *, samples, rows, tokens,
):
    channels = stream.shape[-1]
    weight = w_qkv.at[ENC_LAYERS]
    selector = selector_of(meta, atom_token, tokens).astype(BF)
    first_at, second_at = halves(meta[0], 0, 2 * tokens)
    row = lax.broadcasted_iota(jnp.int32, (3 * tokens, RIM), 0).astype(F32)
    base = ((meta[1] - 1) * tokens).astype(F32)
    rims = [
        (rim, (row == rim[samples * RIM : samples * RIM + 1, :RIM] - base).astype(BF), out)
        for rim, out in ((first_rim, first_ref), (second_rim, second_ref))
    ]

    def pick(chosen, s):
        return lax.dot_general(
            chosen, padded[s], (((0,), (0,)), ((), ())), preferred_element_type=F32
        )

    def place(s, _):
        at = slice(s * tokens, (s + 1) * tokens)
        padded[s, tokens : 2 * tokens] = back[at]
        padded[s, pl.ds(first_at, tokens)] = first[at]
        padded[s, pl.ds(second_at, tokens)] = second[at]
        own = stream[s * rows : (s + 1) * rows] + pick(selector, s)
        stream_ref[s * rows : (s + 1) * rows] = own
        parts = [own]
        for rim, chosen, _ in rims:
            parts.append(rim[s * RIM : (s + 1) * RIM] + pick(chosen, s))
        return jnp.concatenate(parts, 0)

    def normalise(s, after):
        return normed(after).astype(BF)

    def project(s, normal):
        projected = dot(normal, weight[...])
        q_ref[s * rows : (s + 1) * rows] = projected[:rows, :channels].astype(BF)
        key_values = projected[:, channels:].astype(BF)
        kv_ref[s * rows : (s + 1) * rows] = key_values[:rows]
        for side, (_, _, out) in enumerate(rims):
            start = rows + side * RIM
            out[s * RIM : (s + 1) * RIM] = key_values[start : start + RIM]

    in_stages([place, normalise, project], range(samples))


def final_kernel(
    meta, q, kv, first, second, stream, bias, w_out, w_up, w_down, w_final,
    level_hbm, x_true, noise, state, denoised_ref, state_ref, padded, mixed,
    level, late_sems, *, layer, samples, rows,
):
    late = fetch([(level_hbm, level), (state, state_ref)], late_sems)

    normal = run_block(
        meta, q, kv, first, second, stream, bias, (w_out, w_up, w_down), layer,
        samples, rows, padded, mixed, None,
    )
    late[0].wait()
    sigma, total = sigma_of(level, samples)
    keep = SIGMA_DATA * SIGMA_DATA / total
    move = sigma * SIGMA_DATA * lax.rsqrt(total)
    updates = [
        dot_nt(w_final[...], normal[s * rows : (s + 1) * rows]) for s in range(samples)
    ]
    for c in range(x_true.shape[0]):
        noisy = x_true[c : c + 1] + sigma * noise[c]
        update = jnp.concatenate([one[c : c + 1] for one in updates], 0)
        denoised_ref[c] = (keep * noisy + move * update) / SIGMA_DATA
    late[1].wait()


def swap(pair, count):
    first, second = pair
    groups = lax.axis_size("groups")
    lower = [(i, i ^ 1) for i in range(count)]
    upper = []
    for g in range(groups):
        inner = [(g * count + i, g * count + i + 1) for i in range(1, count - 1, 2)]
        upper += inner + [(j, i) for i, j in inner]
        for end in (0, count - 1):
            other = (g ^ 1) * count + end if groups % 2 == 0 else (g + 1) * count - 1 - end
            upper.append((g * count + end, other))
    second = lax.ppermute(second, ("groups",) + SEQ, upper)
    first = lax.ppermute(first, SEQ, lower)
    return first, second


def toward(array, k, count):
    return lax.ppermute(array, "p", [(i, i ^ k) for i in range(count)])


def across(arrays, count):
    return [toward(array, k, count) for k, array in enumerate(arrays, 1)]


def shards(
    x_true, noise, noise_level, atom_single, atom_token, window_edges, atom_pair_bias,
    token_single, pair_bias, w_coord, w_atom_qkv, w_atom_out, w_atom_up, w_atom_down,
    w_pool, w_token_qkv, w_token_out, w_back, w_final,
):
    samples = noise.shape[0]
    rows, channels = atom_single.shape
    tokens, width = token_single.shape
    heads = pair_bias.shape[0]
    planes = lax.axis_size("z")
    count = planes * samples
    atom_token = atom_token[None, :]
    edges = window_edges.T
    noise = noise.transpose(1, 0, 2)
    whole = samples * rows
    held = samples * tokens
    rim = struct((samples * RIM, 2 * channels), BF)
    atom_outs = (
        struct((whole, channels), F32),
        struct((whole, channels), BF),
        struct((whole, 2 * channels), BF),
        rim,
        rim,
    )
    stacks = (w_atom_out, w_atom_up, w_atom_down)
    scratch = block_scratch(samples, rows, channels)
    sizes = dict(samples=samples, rows=rows)

    stream, q, kv, *rims = call(
        functools.partial(embed_kernel, **sizes), atom_outs, [HB] * 6,
        (noise_level, x_true, noise, atom_single, w_coord, w_atom_qkv),
        [
            pltpu.SMEM(noise_level.shape, jnp.int32),
            pltpu.VMEM(x_true.shape, F32),
            pltpu.VMEM(noise.shape, F32),
            pltpu.VMEM(atom_single.shape, BF),
            pltpu.VMEM(w_coord.shape, F32),
            pltpu.VMEM(w_atom_qkv.shape[1:], BF),
            pltpu.SemaphoreType.DMA((6,)),
        ],
    )
    blocks, atom_heads, queries, window = atom_pair_bias.shape
    moved = (*stacks, w_atom_qkv, w_pool, atom_token, token_single)
    bias, *stacks, w_atom_qkv, w_pool, atom_token, token_single = call(
        prepare_kernel,
        (struct((blocks, atom_heads * queries, window), F32),)
        + tuple(struct(array.shape, array.dtype) for array in moved),
        [HB, HB, VM] + [HB] * len(moved), (edges, atom_pair_bias, stream, *moved),
        [
            pltpu.VMEM(atom_pair_bias.shape, F32),
            pltpu.SMEM(edges.shape, jnp.int32),
            pltpu.SemaphoreType.DMA((blocks + len(moved) + 1,)),
        ],
    )

    def block(layer, q, kv, rims, stream):
        return call(
            functools.partial(block_kernel, layer=layer, **sizes), atom_outs,
            [VM] * 10,
            (q, kv, *rims, stream, bias, *stacks, w_atom_qkv),
            scratch,
        )

    for layer in range(ENC_LAYERS - 1):
        rims = swap(rims, count)
        stream, q, kv, *rims = block(layer, q, kv, rims, stream)
    rims = swap(rims, count)
    lanes = width + COUNT_LANES
    edge = struct((held, lanes), BF)
    stream_rim = struct((samples * RIM + 8, channels), F32)
    encoded, mid, first, second, *stream_rims = call(
        functools.partial(pool_kernel, layer=ENC_LAYERS - 1, tokens=tokens, **sizes),
        (atom_outs[0], struct((held + tokens, lanes), F32), edge, edge, stream_rim, stream_rim),
        [VM] * 12,
        (q, kv, *rims, stream, bias, *stacks, w_pool, atom_token, token_single),
        scratch + [pltpu.VMEM((samples, 3 * tokens, lanes), F32)],
    )
    rims = swap((first, second), count)
    piece = struct((tokens, width), BF)
    state, *sends = call(
        functools.partial(token_in_kernel, samples=samples, tokens=tokens),
        (struct((held, width), F32),) + (piece,) * samples,
        [VM] * 3, (mid, *rims),
        [pltpu.VMEM((samples, tokens, width), BF)],
    )
    got = across(sends[1:], samples)
    held_bias, _ = lax.optimization_barrier((pair_bias, state))
    biases = [pair_bias]
    for k in (1, 2):
        biases.append(toward(held_bias, k, samples))
    normal = call(
        functools.partial(plane_kernel, samples=samples, tokens=tokens),
        struct((held, width), BF), [VM] * samples, (sends[0], *got),
    )
    gathered = []
    for k in range(1, planes):
        shift = [(i, (i + k) % planes) for i in range(planes)]
        gathered.append(lax.ppermute(normal, "z", shift))
    stream_rims = swap(stream_rims, count)
    passed, _ = lax.optimization_barrier((biases[2], normal))
    biases.append(toward(passed, 1, samples))
    every = planes * held
    q_own, kv_own, bias_all = call(
        functools.partial(token_own_kernel, samples=samples, tokens=tokens),
        (
            struct((held, width), BF),
            struct((held, 2 * width), BF),
            struct((heads, held, every), F32),
        ),
        [VM, HB] + [VM] * samples, (normal, *biases, w_token_qkv),
        [pltpu.SemaphoreType.DMA((samples,))],
    )
    sends = call(
        functools.partial(
            token_kernel, samples=samples, tokens=tokens, planes=planes, heads=heads
        ),
        (piece,) * samples, [VM] * (3 + planes),
        (q_own, kv_own, bias_all, *gathered, w_token_qkv),
        [pltpu.VMEM((every, 2 * width), BF), pltpu.VMEM((held, width), F32)],
    )
    got = across(sends[1:], samples)
    after, back = call(
        functools.partial(token_out_kernel, samples=samples, tokens=tokens),
        (struct((samples, tokens, width), F32), struct((held, channels), BF)),
        [VM] * (1 + samples + 2), (state, sends[0], *got, w_token_out, w_back),
        [pltpu.VMEM((held, width), BF)],
    )
    backs = swap((back, back), count)
    stream, q, kv, *rims = call(
        functools.partial(unpool_kernel, tokens=tokens, **sizes), atom_outs,
        [VM] * 8,
        (encoded, atom_token, back, *backs, *stream_rims, w_atom_qkv),
        [pltpu.VMEM((samples, 3 * tokens, channels), BF)],
    )
    for layer in range(ENC_LAYERS, LAYERS - 1):
        if layer > ENC_LAYERS:
            rims = swap(rims, count)
        stream, q, kv, *rims = block(layer, q, kv, rims, stream)
    rims = swap(rims, count)
    denoised, token_state = call(
        functools.partial(final_kernel, layer=LAYERS - 1, **sizes),
        (struct(noise.shape, F32), struct((samples, tokens, width), F32)),
        [VM] * 10 + [HB, VM, VM, VM],
        (
            q, kv, *rims, stream, bias, *stacks, w_final, noise_level, x_true, noise,
            after,
        ),
        scratch
        + [
            pltpu.SMEM(noise_level.shape, jnp.int32),
            pltpu.SemaphoreType.DMA((2,)),
        ],
        (VM, HB),
    )
    return denoised.transpose(1, 0, 2), token_state


def solution(mesh):
    def step(*args):
        groups, seq = mesh.devices.shape
        samples = args[1].shape[0] // groups
        split = Mesh(
            mesh.devices.reshape(groups, seq // samples, samples), ("groups",) + SEQ
        )
        both = ("groups",) + SEQ
        in_specs = (
            P(None, both),
            P("groups", None, SEQ),
            P("groups"),
            P(both, None),
            P(both),
            P(both, None),
            P(both, None, None, None),
            P(both, None),
            P("groups", SEQ, None),
        ) + (P(),) * 10
        out_specs = (P("groups", None, SEQ), P("groups", SEQ, None))
        return jax.shard_map(
            shards, mesh=split, in_specs=in_specs, out_specs=out_specs, check_vma=False
        )(*args)

    return step
```

```python
import functools

import jax
import jax.numpy as jnp
from jax import lax
from jax.experimental import pallas as pl
from jax.experimental.pallas import tpu as pltpu
from jax.sharding import Mesh
from jax.sharding import PartitionSpec as P


QUERY_BLOCK = 32
KEY_WINDOW = 128
ENC_LAYERS = 2
LEVELS = 200
RIM = 48
LAYERS = 4

EPS = 1e-05
SIGMA_DATA = 16.0
BF = jnp.bfloat16
F32 = jnp.float32
SEQ = ("z", "p")
VM = pl.BlockSpec(memory_space=pltpu.VMEM)
HB = pl.BlockSpec(memory_space=pltpu.HBM)
COUNT_LANES = 128
LOG2E = 1.4426950408889634


def normed(values):
    centre = jnp.mean(values, -1, keepdims=True)
    centred = values - centre
    spread = jnp.mean(centred * centred, -1, keepdims=True)
    return centred * lax.rsqrt(spread + EPS)


def dot(a, b):
    return jnp.dot(a, b, preferred_element_type=F32)


def dot_nt(a, b):
    return lax.dot_general(a, b, (((1,), (1,)), ((), ())), preferred_element_type=F32)


def noise_scale(noise_level):
    upper_root = 160.0 ** (1.0 / 7.0)
    lower_root = 0.0004 ** (1.0 / 7.0)
    fraction = noise_level.astype(F32) / (LEVELS - 1)
    root = upper_root + fraction * (lower_root - upper_root)
    square = root * root
    return SIGMA_DATA * (square * square * square * root)


def struct(shape, dtype):
    return jax.ShapeDtypeStruct(shape, dtype)


def places():
    mine = lax.axis_index("p")
    plane = lax.axis_index("z")
    device = plane * lax.axis_size("p") + mine
    return lax.rem(device, 2), device, mine, plane


def call(kernel, out_shape, specs, args, scratch=(), out_specs=None):
    def body(*refs):
        kernel(places(), *refs)

    return pl.pallas_call(
        body,
        out_shape=out_shape,
        in_specs=specs,
        out_specs=out_specs or jax.tree.map(lambda _: VM, out_shape),
        scratch_shapes=scratch,
        compiler_params=pltpu.CompilerParams(vmem_limit_bytes=48 * 1024 * 1024),
    )(
        *[
            pltpu.with_memory_space_constraint(arg, pltpu.HBM) if spec is HB else arg
            for spec, arg in zip(specs, args)
        ]
    )


def halves(odd, lower, upper):
    first = jnp.where(odd == 0, upper, lower)
    second = jnp.where(odd == 0, lower, upper)
    return pl.multiple_of(first, 16), pl.multiple_of(second, 16)


def emit_rims(kv_ref, odd, samples, rows, first_ref, second_ref):
    for s in range(samples):
        first, second = halves(odd, s * rows, (s + 1) * rows - RIM)
        first_ref[s * RIM : (s + 1) * RIM] = kv_ref[pl.ds(first, RIM)]
        second_ref[s * RIM : (s + 1) * RIM] = kv_ref[pl.ds(second, RIM)]


def unit_rows(samples, rows):
    starts = [(b, s, s * rows + b * QUERY_BLOCK) for b in range(rows // QUERY_BLOCK) for s in range(samples)]
    return [(b, s, slice(at, at + QUERY_BLOCK)) for b, s, at in starts]


def in_stages(stages, units):
    held = [None] * len(units)
    for stage in stages:
        held = [stage(unit, before) for unit, before in zip(units, held)]


def fetch(pairs, sems):
    copies = [
        pltpu.make_async_copy(source, target, sems.at[i])
        for i, (source, target) in enumerate(pairs)
    ]
    for copy in copies:
        copy.start()
    return copies


def run_block(
    meta, q_ref, kv_ref, first_ref, second_ref, stream_ref, bias_ref, weights, layer,
    samples, rows, padded, mixed, out_ref,
):
    w_out, w_up, w_down = weights
    channels = q_ref.shape[-1]
    heads = bias_ref.shape[1] // QUERY_BLOCK
    head_size = channels // heads
    first, second = halves(meta[0], 0, RIM + rows)
    for s in range(samples):
        padded[s, RIM : RIM + rows] = kv_ref[s * rows : (s + 1) * rows]
        padded[s, pl.ds(first, RIM)] = first_ref[s * RIM : (s + 1) * RIM]
        padded[s, pl.ds(second, RIM)] = second_ref[s * RIM : (s + 1) * RIM]
    lane = lax.broadcasted_iota(jnp.int32, (QUERY_BLOCK, channels), 1)
    head_masks = [(lane // head_size == h).astype(F32) for h in range(heads)]
    head_bits = [m.astype(BF) for m in head_masks]
    head_masks = [jnp.concatenate([m, m], 1) for m in head_masks]
    scale = head_size ** (-0.5) * LOG2E
    ones = jnp.ones((KEY_WINDOW, channels), BF)

    units = unit_rows(samples, rows)

    def window(b):
        return slice(QUERY_BLOCK * b, QUERY_BLOCK * b + KEY_WINDOW)

    def score(unit, _):
        b, s, at = unit
        query = q_ref[at]
        spread = jnp.concatenate([query * bit for bit in head_bits], 0)
        return dot_nt(spread, padded[s, window(b), :channels]) * scale + bias_ref[b]

    def soften(_, scores):
        return jnp.exp2(scores - jnp.max(scores, -1, keepdims=True)).astype(BF)

    def mix(unit, expo):
        b, s, at = unit
        values = padded[s, window(b), channels:]
        out = dot(expo, jnp.concatenate([values, ones], 1))
        merged = out[:QUERY_BLOCK] * head_masks[0]
        for h in range(1, heads):
            merged += out[h * QUERY_BLOCK : (h + 1) * QUERY_BLOCK] * head_masks[h]
        mixed[at] = (merged[:, :channels] * (1.0 / merged[:, channels:])).astype(BF)

    in_stages([score, soften, mix], units)
    stream = stream_ref[...] + dot(mixed[...], w_out[layer])
    gated = dot(normed(stream).astype(BF), w_up[layer])
    half = gated.shape[-1] // 2
    gate = gated[:, :half]
    hidden = (gate * (1.0 / (1.0 + jnp.exp(-gate))) * gated[:, half:]).astype(BF)
    stream = stream + dot(hidden, w_down[layer])
    if out_ref is not None:
        out_ref[...] = stream
    return normed(stream).astype(BF)


def block_scratch(samples, rows, channels):
    return [
        pltpu.VMEM((samples, rows + 2 * RIM, 2 * channels), BF),
        pltpu.VMEM((samples * rows, channels), BF),
    ]


def embed_kernel(
    meta, level_hbm, x_true_hbm, noise_hbm, single_hbm, w_coord_hbm, w_qkv_hbm,
    stream_ref, q_ref, kv_ref, first_ref, second_ref,
    level, x_true, noise, single, w_coord, w_qkv, sems, *, samples, rows,
):
    copies = fetch(
        [
            (level_hbm, level),
            (x_true_hbm, x_true),
            (noise_hbm, noise),
            (single_hbm, single),
            (w_coord_hbm, w_coord),
            (w_qkv_hbm.at[0], w_qkv),
        ],
        sems,
    )
    channels = single.shape[-1]
    for copy in copies[:-1]:
        copy.wait()
    sigma, total = sigma_of(level, samples)
    inverse = lax.rsqrt(total)
    base = single[...].astype(F32)
    scaled = [
        (x_true[c : c + 1] + sigma * noise[c]) * inverse for c in range(x_true.shape[0])
    ]

    def place(s):
        coords = jnp.concatenate([one[s : s + 1] for one in scaled], 0)
        return base + lax.dot_general(
            coords, w_coord[...], (((0,), (0,)), ((), ())),
            precision=lax.Precision.HIGHEST, preferred_element_type=F32,
        )

    def normalise(s, stream):
        stream_ref[s * rows : (s + 1) * rows] = stream
        return normed(stream).astype(BF)

    def project(s, normal):
        projected = dot(normal, w_qkv[...])
        q_ref[s * rows : (s + 1) * rows] = projected[:, :channels].astype(BF)
        kv_ref[s * rows : (s + 1) * rows] = projected[:, channels:].astype(BF)

    units = range(samples)
    normals = [normalise(s, place(s)) for s in units]
    copies[-1].wait()
    for s in units:
        project(s, normals[s])
    emit_rims(kv_ref, meta[0], samples, rows, first_ref, second_ref)


def prepare_kernel(meta, edges_hbm, bias_hbm, _, *rest):
    moved = (len(rest) - 4) // 2
    sources, out_ref, targets = rest[:moved], rest[moved], rest[moved + 1 : 2 * moved + 1]
    bias, edges, sems = rest[2 * moved + 1 :]
    blocks, heads, queries, window = bias.shape
    pieces = [(bias_hbm.at[b], bias.at[b]) for b in range(blocks)]
    copies = fetch(pieces + list(zip(sources, targets)) + [(edges_hbm, edges)], sems)
    copies.pop().wait()
    lane = lax.broadcasted_iota(jnp.int32, (heads * queries, window), 1)
    for b in range(blocks):
        position = meta[1] * (blocks * QUERY_BLOCK) - RIM + QUERY_BLOCK * b + lane
        allowed = (position >= edges[0, b]) & (position < edges[1, b])
        copies[b].wait()
        values = bias[b].reshape(heads * queries, window) * LOG2E
        out_ref[b] = jnp.where(allowed, values, -jnp.inf)
    for copy in copies[blocks:]:
        copy.wait()


def sigma_of(level, samples):
    row = lax.broadcasted_iota(jnp.int32, (samples, 1), 0)
    levels = jnp.zeros((samples, 1), jnp.int32)
    for s in range(samples):
        levels = jnp.where(row == s, level[s], levels)
    sigma = noise_scale(levels)
    return sigma, sigma * sigma + SIGMA_DATA * SIGMA_DATA


def block_kernel(
    meta, q, kv, first, second, stream, bias, w_out, w_up, w_down, w_qkv,
    stream_ref, q_ref, kv_ref, first_ref, second_ref, padded, mixed, *, layer, samples, rows,
):
    channels = q.shape[-1]
    normal = run_block(
        meta, q, kv, first, second, stream, bias, (w_out, w_up, w_down), layer,
        samples, rows, padded, mixed, stream_ref,
    )
    projected = dot(normal, w_qkv[layer + 1]).astype(BF)
    q_ref[...] = projected[:, :channels]
    kv_ref[...] = projected[:, channels:]
    emit_rims(kv_ref, meta[0], samples, rows, first_ref, second_ref)


def selector_of(meta, atom_token, tokens):
    rows = atom_token.shape[-1]
    relative = atom_token[...] - (meta[1] - 1) * tokens
    row = lax.broadcasted_iota(jnp.int32, (3 * tokens, rows), 0)
    return (row == relative).astype(F32)


def pool_kernel(
    meta, q, kv, first, second, stream, bias, w_out, w_up, w_down, pooling, owners, single,
    *rest, layer, samples, rows, tokens,
):
    (stream_ref, mid_ref, first_ref, second_ref, first_rim, second_rim,
     padded, mixed, sums) = rest[-9:]
    normal = run_block(
        meta, q, kv, first, second, stream, bias, (w_out, w_up, w_down), layer,
        samples, rows, padded, mixed, stream_ref,
    )
    selector = selector_of(meta, owners, tokens)
    counts = jnp.sum(selector, -1, keepdims=True)
    selector = selector.astype(BF)
    width = pooling.shape[-1]

    def pool(s, _):
        return jnp.maximum(dot(normal[s * rows : (s + 1) * rows], pooling[...]), 0.0)

    def gather(s, pooled):
        upper = pooled.astype(BF)
        lower = (pooled - upper.astype(F32)).astype(BF)
        sums[s, :, :width] = dot(selector, upper) + dot(selector, lower)
        sums[s, :, width:] = jnp.broadcast_to(counts, (3 * tokens, COUNT_LANES))

    in_stages([pool, gather], range(samples))
    ends = [owners[:, :RIM], owners[:, rows - RIM :]]
    for at, side in ((first_rim, 0), (second_rim, 1)):
        for s in range(samples):
            start = halves(meta[0], s * rows, (s + 1) * rows - RIM)[side]
            at[s * RIM : (s + 1) * RIM] = stream_ref[pl.ds(start, RIM)]
        named = jnp.where(meta[0] == side, ends[1], ends[0]).astype(F32)
        at[samples * RIM :] = jnp.zeros((8, at.shape[-1]), F32)
        at[samples * RIM : samples * RIM + 1, :RIM] = named
    mid_ref[samples * tokens :, :width] = single[...]
    mid_ref[samples * tokens :, width:] = jnp.zeros((tokens, COUNT_LANES), F32)
    for s in range(samples):
        at = slice(s * tokens, (s + 1) * tokens)
        mid_ref[at] = sums[s, tokens : 2 * tokens]
        first_at, second_at = halves(meta[0], 0, 2 * tokens)
        first_ref[at] = sums[s, pl.ds(first_at, tokens)].astype(BF)
        second_ref[at] = sums[s, pl.ds(second_at, tokens)].astype(BF)


def token_in_kernel(
    meta, mid, first, second, state_ref, *rest, samples, tokens
):
    send_refs, normal_all = rest[:samples], rest[samples]
    width = state_ref.shape[-1]
    held = samples * tokens
    single = mid[held:, :width]
    total = mid[:held] + first[...].astype(F32) + second[...].astype(F32)
    share = total[:, :width] / total[:, width : width + 1]
    for s in range(samples):
        at = slice(s * tokens, (s + 1) * tokens)
        state = share[at] + single
        state_ref[at] = state
        normal_all[s] = normed(state).astype(BF)
    mine = meta[2]
    for k in range(samples):
        send_refs[k][...] = normal_all[lax.bitwise_xor(mine, k)]


def plane_kernel(meta, *rest, samples, tokens):
    parts, out_ref = rest[:samples], rest[samples]
    mine = meta[2]
    for k in range(samples):
        at = pl.multiple_of(lax.bitwise_xor(mine, k) * tokens, tokens)
        out_ref[pl.ds(at, tokens)] = parts[k][...]


def token_own_kernel(meta, normal, *rest, samples, tokens):
    biases, (w_qkv, q_ref, kv_ref, bias_ref, sems) = rest[:samples], rest[samples:]
    mine = meta[2]
    starts = [
        pl.multiple_of(lax.bitwise_xor(mine, k) * tokens, tokens) for k in range(samples)
    ]
    copies = fetch(
        [(biases[k], bias_ref.at[:, pl.ds(starts[k], tokens)]) for k in range(samples)], sems
    )
    width = normal.shape[-1]
    projected = dot(normal[...], w_qkv[...]).astype(BF)
    q_ref[...] = projected[:, :width]
    kv_ref[...] = projected[:, width:]
    for copy in copies:
        copy.wait()


def token_kernel(meta, q_own, kv_own, bias_all, *rest, samples, tokens, planes, heads):
    gathered, w_qkv, rest = rest[: planes - 1], rest[planes - 1], rest[planes:]
    send_refs, (kv_all, mixed_all) = rest[:samples], rest[samples:]
    rows = samples * tokens
    width = q_own.shape[-1]
    head_size = width // heads
    mine = meta[2]
    plane = meta[3]
    kv_all[pl.ds(pl.multiple_of(plane * rows, rows), rows)] = kv_own[...]
    others = jnp.concatenate([one[...] for one in gathered], 0)
    others = dot(others, w_qkv[:, width:]).astype(BF)
    for k in range(1, planes):
        origin = plane - k + jnp.where(plane < k, planes, 0)
        at = pl.multiple_of(origin * rows, rows)
        kv_all[pl.ds(at, rows)] = others[(k - 1) * rows : k * rows]
    scale = head_size ** (-0.5) * LOG2E
    mixed_all[...] = jnp.zeros_like(mixed_all)

    def lanes_of(h):
        start = h * head_size // 128 * 128
        stop = -(-(h + 1) * head_size // 128) * 128
        lane = lax.broadcasted_iota(jnp.int32, (rows, stop - start), 1) + start
        mask = ((lane >= h * head_size) & (lane < (h + 1) * head_size)).astype(F32)
        return slice(start, stop), mask

    def score(h, _):
        at, mask = lanes_of(h)
        query = q_own[:, at] * mask.astype(BF)
        return dot_nt(query, kv_all[:, at]) * scale + bias_all[h] * LOG2E

    def soften(h, scores):
        expo = jnp.exp2(scores - jnp.max(scores, -1, keepdims=True))
        upper = expo.astype(BF)
        lower = (expo - upper.astype(F32)).astype(BF)
        return upper, lower, 1.0 / jnp.sum(expo, -1, keepdims=True)

    def mix(h, attends):
        at, mask = lanes_of(h)
        values = kv_all[:, width + at.start : width + at.stop]
        upper, lower, inverse = attends
        mixed_all[:, at] += (dot(upper, values) + dot(lower, values)) * (mask * inverse)

    in_stages([score, soften, mix], range(heads))
    for k in range(samples):
        at = pl.multiple_of(lax.bitwise_xor(mine, k) * tokens, tokens)
        send_refs[k][...] = mixed_all[pl.ds(at, tokens)].astype(BF)


def token_out_kernel(meta, state, *rest, samples, tokens):
    parts, (w_out, w_back, out_ref, back_ref, mixed) = rest[:samples], rest[samples:]
    mine = meta[2]
    for k in range(samples):
        at = pl.multiple_of(lax.bitwise_xor(mine, k) * tokens, tokens)
        mixed[pl.ds(at, tokens)] = parts[k][...]
    after = state[...] + dot(mixed[...], w_out[...])
    for s in range(samples):
        out_ref[s] = after[s * tokens : (s + 1) * tokens]
    back_ref[...] = dot(normed(after).astype(BF), w_back[...]).astype(BF)


def unpool_kernel(
    meta, stream, atom_token, back, first, second, first_rim, second_rim, w_qkv,
    stream_ref, q_ref, kv_ref, first_ref, second_ref, padded, *, samples, rows, tokens,
):
    channels = stream.shape[-1]
    weight = w_qkv.at[ENC_LAYERS]
    selector = selector_of(meta, atom_token, tokens).astype(BF)
    first_at, second_at = halves(meta[0], 0, 2 * tokens)
    row = lax.broadcasted_iota(jnp.int32, (3 * tokens, RIM), 0).astype(F32)
    base = ((meta[1] - 1) * tokens).astype(F32)
    rims = [
        (rim, (row == rim[samples * RIM : samples * RIM + 1, :RIM] - base).astype(BF), out)
        for rim, out in ((first_rim, first_ref), (second_rim, second_ref))
    ]

    def pick(chosen, s):
        return lax.dot_general(
            chosen, padded[s], (((0,), (0,)), ((), ())), preferred_element_type=F32
        )

    def place(s, _):
        at = slice(s * tokens, (s + 1) * tokens)
        padded[s, tokens : 2 * tokens] = back[at]
        padded[s, pl.ds(first_at, tokens)] = first[at]
        padded[s, pl.ds(second_at, tokens)] = second[at]
        own = stream[s * rows : (s + 1) * rows] + pick(selector, s)
        stream_ref[s * rows : (s + 1) * rows] = own
        parts = [own]
        for rim, chosen, _ in rims:
            parts.append(rim[s * RIM : (s + 1) * RIM] + pick(chosen, s))
        return jnp.concatenate(parts, 0)

    def normalise(s, after):
        return normed(after).astype(BF)

    def project(s, normal):
        projected = dot(normal, weight[...])
        q_ref[s * rows : (s + 1) * rows] = projected[:rows, :channels].astype(BF)
        key_values = projected[:, channels:].astype(BF)
        kv_ref[s * rows : (s + 1) * rows] = key_values[:rows]
        for side, (_, _, out) in enumerate(rims):
            start = rows + side * RIM
            out[s * RIM : (s + 1) * RIM] = key_values[start : start + RIM]

    in_stages([place, normalise, project], range(samples))


def final_kernel(
    meta, q, kv, first, second, stream, bias, w_out, w_up, w_down, w_final,
    level_hbm, x_true, noise, state, denoised_ref, state_ref, padded, mixed,
    level, late_sems, *, layer, samples, rows,
):
    late = fetch([(level_hbm, level), (state, state_ref)], late_sems)

    normal = run_block(
        meta, q, kv, first, second, stream, bias, (w_out, w_up, w_down), layer,
        samples, rows, padded, mixed, None,
    )
    late[0].wait()
    sigma, total = sigma_of(level, samples)
    keep = SIGMA_DATA * SIGMA_DATA / total
    move = sigma * SIGMA_DATA * lax.rsqrt(total)
    updates = [
        dot_nt(w_final[...], normal[s * rows : (s + 1) * rows]) for s in range(samples)
    ]
    for c in range(x_true.shape[0]):
        noisy = x_true[c : c + 1] + sigma * noise[c]
        update = jnp.concatenate([one[c : c + 1] for one in updates], 0)
        denoised_ref[c] = (keep * noisy + move * update) / SIGMA_DATA
    late[1].wait()


def swap(pair, count):
    first, second = pair
    groups = lax.axis_size("groups")
    lower = [(i, i ^ 1) for i in range(count)]
    upper = []
    for g in range(groups):
        inner = [(g * count + i, g * count + i + 1) for i in range(1, count - 1, 2)]
        upper += inner + [(j, i) for i, j in inner]
        for end in (0, count - 1):
            other = (g ^ 1) * count + end if groups % 2 == 0 else (g + 1) * count - 1 - end
            upper.append((g * count + end, other))
    second = lax.ppermute(second, ("groups",) + SEQ, upper)
    first = lax.ppermute(first, SEQ, lower)
    return first, second


def toward(array, k, count):
    return lax.ppermute(array, "p", [(i, i ^ k) for i in range(count)])


def across(arrays, count):
    return [toward(array, k, count) for k, array in enumerate(arrays, 1)]


def shards(
    x_true, noise, noise_level, atom_single, atom_token, window_edges, atom_pair_bias,
    token_single, pair_bias, w_coord, w_atom_qkv, w_atom_out, w_atom_up, w_atom_down,
    w_pool, w_token_qkv, w_token_out, w_back, w_final,
):
    samples = noise.shape[0]
    rows, channels = atom_single.shape
    tokens, width = token_single.shape
    heads = pair_bias.shape[0]
    planes = lax.axis_size("z")
    count = planes * samples
    atom_token = atom_token[None, :]
    edges = window_edges.T
    noise = noise.transpose(1, 0, 2)
    whole = samples * rows
    held = samples * tokens
    rim = struct((samples * RIM, 2 * channels), BF)
    atom_outs = (
        struct((whole, channels), F32),
        struct((whole, channels), BF),
        struct((whole, 2 * channels), BF),
        rim,
        rim,
    )
    stacks = (w_atom_out, w_atom_up, w_atom_down)
    scratch = block_scratch(samples, rows, channels)
    sizes = dict(samples=samples, rows=rows)

    stream, q, kv, *rims = call(
        functools.partial(embed_kernel, **sizes), atom_outs, [HB] * 6,
        (noise_level, x_true, noise, atom_single, w_coord, w_atom_qkv),
        [
            pltpu.SMEM(noise_level.shape, jnp.int32),
            pltpu.VMEM(x_true.shape, F32),
            pltpu.VMEM(noise.shape, F32),
            pltpu.VMEM(atom_single.shape, BF),
            pltpu.VMEM(w_coord.shape, F32),
            pltpu.VMEM(w_atom_qkv.shape[1:], BF),
            pltpu.SemaphoreType.DMA((6,)),
        ],
    )
    blocks, atom_heads, queries, window = atom_pair_bias.shape
    moved = (*stacks, w_atom_qkv, w_pool, atom_token, token_single)
    bias, *stacks, w_atom_qkv, w_pool, atom_token, token_single = call(
        prepare_kernel,
        (struct((blocks, atom_heads * queries, window), F32),)
        + tuple(struct(array.shape, array.dtype) for array in moved),
        [HB, HB, VM] + [HB] * len(moved), (edges, atom_pair_bias, stream, *moved),
        [
            pltpu.VMEM(atom_pair_bias.shape, F32),
            pltpu.SMEM(edges.shape, jnp.int32),
            pltpu.SemaphoreType.DMA((blocks + len(moved) + 1,)),
        ],
    )

    def block(layer, q, kv, rims, stream):
        return call(
            functools.partial(block_kernel, layer=layer, **sizes), atom_outs,
            [VM] * 10,
            (q, kv, *rims, stream, bias, *stacks, w_atom_qkv),
            scratch,
        )

    for layer in range(ENC_LAYERS - 1):
        rims = swap(rims, count)
        stream, q, kv, *rims = block(layer, q, kv, rims, stream)
    rims = swap(rims, count)
    lanes = width + COUNT_LANES
    edge = struct((held, lanes), BF)
    stream_rim = struct((samples * RIM + 8, channels), F32)
    encoded, mid, first, second, *stream_rims = call(
        functools.partial(pool_kernel, layer=ENC_LAYERS - 1, tokens=tokens, **sizes),
        (atom_outs[0], struct((held + tokens, lanes), F32), edge, edge, stream_rim, stream_rim),
        [VM] * 12,
        (q, kv, *rims, stream, bias, *stacks, w_pool, atom_token, token_single),
        scratch + [pltpu.VMEM((samples, 3 * tokens, lanes), F32)],
    )
    rims = swap((first, second), count)
    piece = struct((tokens, width), BF)
    state, *sends = call(
        functools.partial(token_in_kernel, samples=samples, tokens=tokens),
        (struct((held, width), F32),) + (piece,) * samples,
        [VM] * 3, (mid, *rims),
        [pltpu.VMEM((samples, tokens, width), BF)],
    )
    got = across(sends[1:], samples)
    held_bias, _ = lax.optimization_barrier((pair_bias, state))
    biases = [pair_bias]
    for k in (1, 2):
        biases.append(toward(held_bias, k, samples))
    normal = call(
        functools.partial(plane_kernel, samples=samples, tokens=tokens),
        struct((held, width), BF), [VM] * samples, (sends[0], *got),
    )
    gathered = []
    for k in range(1, planes):
        shift = [(i, (i + k) % planes) for i in range(planes)]
        gathered.append(lax.ppermute(normal, "z", shift))
    stream_rims = swap(stream_rims, count)
    passed, _ = lax.optimization_barrier((biases[2], normal))
    biases.append(toward(passed, 1, samples))
    every = planes * held
    q_own, kv_own, bias_all = call(
        functools.partial(token_own_kernel, samples=samples, tokens=tokens),
        (
            struct((held, width), BF),
            struct((held, 2 * width), BF),
            struct((heads, held, every), F32),
        ),
        [VM, HB] + [VM] * samples, (normal, *biases, w_token_qkv),
        [pltpu.SemaphoreType.DMA((samples,))],
    )
    sends = call(
        functools.partial(
            token_kernel, samples=samples, tokens=tokens, planes=planes, heads=heads
        ),
        (piece,) * samples, [VM] * (3 + planes),
        (q_own, kv_own, bias_all, *gathered, w_token_qkv),
        [pltpu.VMEM((every, 2 * width), BF), pltpu.VMEM((held, width), F32)],
    )
    got = across(sends[1:], samples)
    after, back = call(
        functools.partial(token_out_kernel, samples=samples, tokens=tokens),
        (struct((samples, tokens, width), F32), struct((held, channels), BF)),
        [VM] * (1 + samples + 2), (state, sends[0], *got, w_token_out, w_back),
        [pltpu.VMEM((held, width), BF)],
    )
    backs = swap((back, back), count)
    stream, q, kv, *rims = call(
        functools.partial(unpool_kernel, tokens=tokens, **sizes), atom_outs,
        [VM] * 8,
        (encoded, atom_token, back, *backs, *stream_rims, w_atom_qkv),
        [pltpu.VMEM((samples, 3 * tokens, channels), BF)],
    )
    for layer in range(ENC_LAYERS, LAYERS - 1):
        if layer > ENC_LAYERS:
            rims = swap(rims, count)
        stream, q, kv, *rims = block(layer, q, kv, rims, stream)
    rims = swap(rims, count)
    denoised, token_state = call(
        functools.partial(final_kernel, layer=LAYERS - 1, **sizes),
        (struct(noise.shape, F32), struct((samples, tokens, width), F32)),
        [VM] * 10 + [HB, VM, VM, VM],
        (
            q, kv, *rims, stream, bias, *stacks, w_final, noise_level, x_true, noise,
            after,
        ),
        scratch
        + [
            pltpu.SMEM(noise_level.shape, jnp.int32),
            pltpu.SemaphoreType.DMA((2,)),
        ],
        (VM, HB),
    )
    return denoised.transpose(1, 0, 2), token_state


def solution(mesh):
    def step(*args):
        groups, seq = mesh.devices.shape
        samples = args[1].shape[0] // groups
        split = Mesh(
            mesh.devices.reshape(groups, seq // samples, samples), ("groups",) + SEQ
        )
        both = ("groups",) + SEQ
        in_specs = (
            P(None, both),
            P("groups", None, SEQ),
            P("groups"),
            P(both, None),
            P(both),
            P(both, None),
            P(both, None, None, None),
            P(both, None),
            P("groups", SEQ, None),
        ) + (P(),) * 10
        out_specs = (P("groups", None, SEQ), P("groups", SEQ, None))
        return jax.shard_map(
            shards, mesh=split, in_specs=in_specs, out_specs=out_specs, check_vma=False
        )(*args)

    return step
```
